128 devices in a mesh: dp: 4 (over x), expert: 32 (over z, y, core).
Axes of the slice: x: 4, y: 4, z: 4, core: 2. Of those that a mesh axis runs over, the one named last changes fastest.
Arguments:
- tokens: bfloat16 [16384, 2048], P(('dp', 'expert')), may hold values from -6 to 6
- out_grad: bfloat16 [16384, 2048], P(('dp', 'expert')), may hold values from -6 to 6
- expert_ids: int32 [16384, 8], P(('dp', 'expert')), may hold values from 0 to 63, all different within a row
- route_probs: bfloat16 [16384, 8], P(('dp', 'expert')), may hold values from 0.019897461 to 0.5
- w_gate: bfloat16 [64, 2048, 768], P('expert'), may hold values from -0.125 to 0.125
- w_up: bfloat16 [64, 2048, 768], P('expert'), may hold values from -0.125 to 0.125
- w_down: bfloat16 [64, 2048, 768], P('expert'), may hold values from -0.21875 to 0.21875
- decay_mask: int32 [64, 3], P('expert'), may hold values from 0 to 1
Outputs:
- grad_tokens: bfloat16 [16384, 2048], P(('dp', 'expert'))
- grad_probs: bfloat16 [16384, 8], P(('dp', 'expert'))
- new_gate: bfloat16 [64, 2048, 768], P('expert', 'dp')
- new_up: bfloat16 [64, 2048, 768], P('expert', 'dp')
- new_down: bfloat16 [64, 2048, 768], P('expert', 'dp')
The draws below stay inside these ranges and needn't reach their ends.
All inputs are finite; a program needn't handle non-finite values.
Results may differ from the reference program's by a relative error of at most 0.015.
Values may be sent and summed in bfloat16 or wider, within the bound.
No kernel may reach another device: no remote copies, remote signals or barrier semaphores. Data moves between devices by JAX's collectives and lax.ppermute only.
A program may use at most 192 MiB of HBM per device.

```python
import math
import jax
import jax.numpy as jnp
from jax import lax

D = 2048
H = 768
TOP = 8
TOK_DEV = 128
EXPERTS = 64
CAP = 16
TOKENS = 16384
N_DP = 4
N_EXPERT = 32


def with_ends(result, own_key, low, largest):
    longest = result.shape.index(max(result.shape))
    spots = []
    for shift in (0, 1):
        where = [jax.random.randint(jax.random.fold_in(own_key, axis), (), 0, length) for axis, length in enumerate(result.shape)]
        where[longest] = (where[longest] + shift) % result.shape[longest]
        spots.append(tuple(where))
    return result.at[spots[0]].set(low).at[spots[1]].set(largest)


def block_levels(own_key, shape, split, least, high):
    def one(dim, shards_of):
        steps = jax.random.uniform(jax.random.fold_in(jax.random.fold_in(own_key, 6), dim), (shards_of,), jnp.float32, least / len(split), high / len(split))
        return jnp.repeat(jnp.exp(steps), shape[dim] // shards_of).reshape((-1,) + (1,) * (len(shape) - dim - 1))

    gain = one(*split[0])
    for cut in split[1:]:
        gain = gain * one(*cut)
    return gain


def picks_of(rng, rows, number_of, top, lift):
    ranking = jax.random.permutation(jax.random.fold_in(rng, 1), number_of)
    pull = ranking
    for power in range(3):
        pull = pull * pull // number_of
    pull = pull * lift // number_of
    lots = jax.random.randint(jax.random.fold_in(rng, 2), (rows, number_of), 0, 4096) + pull
    holders = jax.random.permutation(jax.random.fold_in(rng, 3), rows)[jnp.arange(number_of) % rows]
    lots = jnp.where(jnp.arange(rows)[:, None] == holders[None, :], 1 << 14, lots)
    score = lots * number_of + jnp.arange(number_of)
    return lax.top_k(score.astype(jnp.int32), top)[1].astype(jnp.int32)


def bell_draw(rng, extent, scale, limit, cuts=(), kind=jnp.bfloat16):
    gain = block_levels(rng, extent, cuts, -0.22, 0.18) if cuts else 1.0
    values = jax.random.normal(rng, extent, jnp.float32) * scale * gain
    return jnp.minimum(jnp.maximum(values, -limit), limit).astype(kind)


def setup_inputs(seed: int = 0) -> dict:
    key_list = jax.random.split(jax.random.key(seed), 9)
    return {
        "tokens": bell_draw(key_list[0], (TOKENS, D), 1.0, 6.0, ((0, 128),)),
        "out_grad": bell_draw(key_list[1], (TOKENS, D), 1.0, 6.0, ((0, 128),)),
        "expert_ids": picks_of(key_list[2], TOKENS, EXPERTS, TOP, 1024),
        "route_probs": jnp.clip(jnp.exp(math.log(0.5) - 3.224016 * jax.random.uniform(key_list[3], (TOKENS, TOP), jnp.float32) ** block_levels(key_list[3], (TOKENS, TOP), ((0, 128),), -0.2, 0.2)), 0.019897461, 0.5).astype(jnp.bfloat16),
        "w_gate": bell_draw(key_list[4], (EXPERTS, D, H), D ** -0.5, 0.125, ((0, 32),)),
        "w_up": bell_draw(key_list[5], (EXPERTS, D, H), D ** -0.5, 0.125, ((0, 32),)),
        "w_down": bell_draw(key_list[6], (EXPERTS, D, H), H ** -0.5, 0.21875, ((0, 32),)),
        "decay_mask": with_ends(jax.random.randint(key_list[7], (EXPERTS, 3), 0, 2), jax.random.fold_in(key_list[7], 1), 0, 1).astype(jnp.int32),
    }


step_size = 0.004
shrink_rate = 0.1

def fill_table(slot_row, values, empty):
    table = jnp.full((EXPERTS * CAP + 1,), empty, jnp.int32)
    return table.at[slot_row].set(values)[:-1]

def take_rows(padded, index):
    return padded[index]

def reference(tokens, out_grad, expert_ids, route_probs, w_gate, w_up, w_down, decay_mask):
    devices = N_DP * N_EXPERT
    assigns = TOK_DEV * TOP
    ids = expert_ids.reshape(devices, assigns)
    onehot = (ids[:, :, None] == jnp.arange(EXPERTS, dtype=jnp.int32)[None, None, :]).astype(jnp.int32)
    before = jnp.cumsum(onehot, axis=1) - onehot
    position = lax.optimization_barrier(jnp.sum(before * onehot, axis=2)).astype(jnp.int32)
    slots = jnp.where(position < CAP, ids * CAP + position, EXPERTS * CAP).astype(jnp.int32)
    order = jnp.arange(assigns, dtype=jnp.int32)
    slot_token = jax.vmap(lambda s: fill_table(s, order // TOP, TOK_DEV))(slots)
    slot_assign = jax.vmap(lambda s: fill_table(s, order, assigns))(slots)
    slot_token = slot_token.reshape(devices, EXPERTS, CAP).transpose(1, 0, 2)
    slot_assign = slot_assign.reshape(devices, EXPERTS, CAP).transpose(1, 0, 2)
    zero_rows = jnp.zeros((devices, 1, D), jnp.bfloat16)
    tok_pad = jnp.concatenate([tokens.reshape(devices, TOK_DEV, D), zero_rows], axis=1)
    grad_pad = jnp.concatenate([out_grad.reshape(devices, TOK_DEV, D), zero_rows], axis=1)
    prob_pad = jnp.concatenate([route_probs.reshape(devices, assigns), jnp.zeros((devices, 1), jnp.bfloat16)], axis=1)

    def group_grad(left, right):
        left_g = left.reshape(N_DP, N_EXPERT * CAP, -1).astype(jnp.float32)
        right_g = right.reshape(N_DP, N_EXPERT * CAP, -1).astype(jnp.float32)
        partial_g = jnp.einsum('prd,prh->pdh', left_g, right_g).astype(jnp.bfloat16)
        partial_g = lax.optimization_barrier(partial_g)
        return lax.optimization_barrier(jnp.sum(partial_g.astype(jnp.float32), axis=0))

    def expert_step(carry, inputs):
        dx_acc, dp_acc = carry
        tok_e, asg_e, weight_g, weight_u, weight_d, mask_e = inputs
        x_rows = jax.vmap(take_rows)(tok_pad, tok_e).reshape(devices * CAP, D)
        dy_rows = jax.vmap(take_rows)(grad_pad, tok_e).reshape(devices * CAP, D)
        p_rows = jax.vmap(take_rows)(prob_pad, asg_e).reshape(devices * CAP)
        gate = jnp.dot(x_rows, weight_g, preferred_element_type=jnp.float32)
        upper = jnp.dot(x_rows, weight_u, preferred_element_type=jnp.float32)
        sig = jax.nn.sigmoid(gate)
        act = gate * sig
        hid = (act * upper).astype(jnp.bfloat16)
        outs = jnp.dot(hid, weight_d.T, preferred_element_type=jnp.float32).astype(jnp.bfloat16)
        dp_rows = lax.optimization_barrier(jnp.sum(dy_rows.astype(jnp.float32) * outs.astype(jnp.float32), axis=1)).astype(jnp.bfloat16)
        dout = (p_rows.astype(jnp.float32)[:, None] * dy_rows.astype(jnp.float32)).astype(jnp.bfloat16)
        dhid = jnp.dot(dout, weight_d, preferred_element_type=jnp.float32)
        dgate = (dhid * upper * sig * (1.0 + gate * (1.0 - sig))).astype(jnp.bfloat16)
        dup = (dhid * act).astype(jnp.bfloat16)
        dx_rows = (jnp.dot(dgate, weight_g.T, preferred_element_type=jnp.float32) + jnp.dot(dup, weight_u.T, preferred_element_type=jnp.float32)).astype(jnp.bfloat16)
        grad_g = group_grad(x_rows, dgate)
        grad_u = group_grad(x_rows, dup)
        grad_d = group_grad(dout, hid)
        mask_f = mask_e.astype(jnp.float32)

        def update(weight, grad_w, rate):
            weight_f = weight.astype(jnp.float32)
            return (weight_f - step_size * grad_w - shrink_rate * rate * weight_f).astype(jnp.bfloat16)
        new_g = update(weight_g, grad_g, mask_f[0])
        new_u = update(weight_u, grad_u, mask_f[1])
        new_d = update(weight_d, grad_d, mask_f[2])
        dx_acc = jax.vmap(lambda acc, idx, val: acc.at[idx].add(val))(dx_acc, tok_e, dx_rows.reshape(devices, CAP, D).astype(jnp.float32))
        dp_acc = jax.vmap(lambda acc, idx, val: acc.at[idx].set(val))(dp_acc, asg_e, dp_rows.reshape(devices, CAP))
        return ((dx_acc, dp_acc), (new_g, new_u, new_d))
    dx_init = jnp.zeros((devices, TOK_DEV + 1, D), jnp.float32)
    dp_init = jnp.zeros((devices, assigns + 1), jnp.bfloat16)
    carry, updated = lax.scan(expert_step, (dx_init, dp_init), (slot_token, slot_assign, w_gate, w_up, w_down, decay_mask))
    dx_acc, dp_acc = carry
    grad_tokens = dx_acc[:, :TOK_DEV, :].reshape(TOKENS, D).astype(jnp.bfloat16)
    grad_probs = dp_acc[:, :assigns].reshape(TOKENS, TOP)
    return (grad_tokens, grad_probs, updated[0], updated[1], updated[2])
```

```python
import functools

import jax
import jax.numpy as jnp
from jax import lax
from jax.experimental import pallas as pl
from jax.experimental.pallas import tpu as pltpu
from jax.sharding import PartitionSpec as P

step_size = 0.004
shrink_rate = 0.1
LANES = 128
F32 = jnp.float32
BF16 = jnp.bfloat16
VMEM_LIMIT = 60 * 1024 * 1024


def dot(a, b, dims):
    return lax.dot_general(a, b, (dims, ((), ())), preferred_element_type=F32)


def cost(flops, moved):
    return pl.CostEstimate(flops=flops, transcendentals=0, bytes_accessed=moved)


NN = ((1,), (0,))
NT = ((1,), (1,))
TN = ((0,), (0,))


def slot_values(ids_t, n_experts, capacity):
    topk, tok = ids_t.shape
    rows = lax.broadcasted_iota(jnp.int32, (n_experts, tok), 0)
    hit = ids_t[0:1, :] == rows
    for k in range(1, topk):
        hit = jnp.logical_or(hit, ids_t[k : k + 1, :] == rows)
    hit_f = jnp.where(hit, 1.0, 0.0)
    earlier = lax.broadcasted_iota(jnp.int32, (tok, tok), 0) < lax.broadcasted_iota(
        jnp.int32, (tok, tok), 1
    )
    count = dot(hit_f.astype(BF16), jnp.where(earlier, 1.0, 0.0).astype(BF16), NN)
    return jnp.where(jnp.logical_and(hit, count < capacity), count, -1.0)


def slot_rows(values, chunk, local_exp, capacity):
    n_experts, tok = values.shape
    n_rows = n_experts // local_exp * capacity
    expert_of = lax.broadcasted_iota(jnp.int32, (n_rows, n_experts), 0) // capacity * local_exp + chunk
    spread = jnp.where(expert_of == lax.broadcasted_iota(jnp.int32, (n_rows, n_experts), 1), 1.0, 0.0)
    spread = spread.astype(BF16)
    at = dot(spread, values.astype(BF16), NN)
    place = (lax.broadcasted_iota(jnp.int32, (n_rows, tok), 0) % capacity).astype(F32)
    return at == place, spread


def dispatch_kernel(local_exp, capacity, ids_ref, probs_ref, tok_ref, grad_ref, *out_refs):
    ids_t = ids_ref[...]
    topk, tok = ids_t.shape
    n_experts = out_refs[0].shape[0] // capacity * local_exp
    width = tok_ref.shape[1]
    values = slot_values(ids_t, n_experts, capacity)
    rows = lax.broadcasted_iota(jnp.int32, (n_experts, tok), 0)
    prob = jnp.zeros((n_experts, tok), F32)
    for k in range(topk):
        prob = prob + jnp.where(ids_t[k : k + 1, :] == rows, probs_ref[k : k + 1, :].astype(F32), 0.0)
    for chunk, out_ref in enumerate(out_refs):
        onehot, spread = slot_rows(values, chunk, local_exp, capacity)
        prob_rows = dot(spread, prob.astype(BF16), NN)
        pick = jnp.where(onehot, 1.0, 0.0).astype(BF16)
        weighted = jnp.where(onehot, prob_rows, 0.0).astype(BF16)
        out_ref[:, :width] = dot(pick, tok_ref[...], NN).astype(BF16)
        out_ref[:, width:] = dot(weighted, grad_ref[...], NN).astype(BF16)


def dispatch(local_exp, capacity, n_experts, ids_t, probs_t, tokens, out_grad):
    tok, width = tokens.shape
    n_rows = n_experts // local_exp * capacity
    return pl.pallas_call(
        functools.partial(dispatch_kernel, local_exp, capacity),
        out_shape=[jax.ShapeDtypeStruct((n_rows, 2 * width), BF16)] * local_exp,
        compiler_params=pltpu.CompilerParams(vmem_limit_bytes=VMEM_LIMIT),
        cost_estimate=cost(4 * local_exp * n_rows * tok * width, 4 * width * (tok + local_exp * n_rows)),
        name="dispatch",
    )(ids_t, probs_t, tokens, out_grad)


def grads_kernel(x_ref, do_ref, wg_ref, wu_ref, wd_ref, g_ref, da_ref, db_ref, s_ref):
    x = x_ref[...]
    do = do_ref[...]
    gate = dot(x, wg_ref[0], NN)
    upper = dot(x, wu_ref[0], NN)
    sig = jax.nn.sigmoid(gate)
    act = gate * sig
    hid = (act * upper).astype(BF16)
    dhid = dot(do, wd_ref[0], NN)
    total = jnp.sum(hid.astype(F32) * dhid, axis=1, keepdims=True)
    high = total.astype(BF16).astype(F32)
    lane = lax.broadcasted_iota(jnp.int32, s_ref.shape, 1)
    s_ref[...] = jnp.where(lane == 0, high, jnp.where(lane == 1, total - high, 0.0)).astype(BF16)
    hidden = hid.shape[1]
    g_ref[:, 2 * hidden :] = dot(do, hid, TN).astype(BF16)
    dgate = (dhid * upper * sig * (1.0 + gate * (1.0 - sig))).astype(BF16)
    da_ref[...] = dgate
    g_ref[:, :hidden] = dot(x, dgate, TN).astype(BF16)
    dup = (dhid * act).astype(BF16)
    db_ref[...] = dup
    g_ref[:, hidden : 2 * hidden] = dot(x, dup, TN).astype(BF16)


def expert_grads(chunk, rows, wg, wu, wd):
    n_rows, width = rows.shape[0], rows.shape[1] // 2
    hidden = wg.shape[2]
    weight = pl.BlockSpec((1, width, hidden), lambda i: (chunk, 0, 0), pipeline_mode=pl.Buffered(1))

    def whole(shape):
        return pl.BlockSpec(shape, lambda i: (0, 0), pipeline_mode=pl.Buffered(1))

    return pl.pallas_call(
        grads_kernel,
        grid=(1,),
        in_specs=[
            pl.BlockSpec((n_rows, width), lambda i: (0, 0), pipeline_mode=pl.Buffered(1)),
            pl.BlockSpec((n_rows, width), lambda i: (0, 1), pipeline_mode=pl.Buffered(1)),
            weight,
            weight,
            weight,
        ],
        out_specs=[
            whole((width, 3 * hidden)),
            whole((n_rows, hidden)),
            whole((n_rows, hidden)),
            whole((n_rows, LANES)),
        ],
        out_shape=[
            jax.ShapeDtypeStruct((width, 3 * hidden), BF16),
            jax.ShapeDtypeStruct((n_rows, hidden), BF16),
            jax.ShapeDtypeStruct((n_rows, hidden), BF16),
            jax.ShapeDtypeStruct((n_rows, LANES), BF16),
        ],
        compiler_params=pltpu.CompilerParams(vmem_limit_bytes=VMEM_LIMIT),
        cost_estimate=cost(12000 * n_rows * width * hidden, 12 * width * hidden + 4 * n_rows * (width + hidden)),
        name=f"grads{chunk}",
    )(rows, rows, wg, wu, wd)


def dx_kernel(da_ref, db_ref, s_ref, wg_ref, wu_ref, out_ref):
    width = wg_ref.shape[1]
    out_ref[:, :width] = (dot(da_ref[...], wg_ref[0], NT) + dot(db_ref[...], wu_ref[0], NT)).astype(BF16)
    out_ref[:, width:] = s_ref[...]


def input_grads(chunk, da, db, s, wg, wu):
    n_rows, hidden = da.shape
    width = wg.shape[1]
    weight = pl.BlockSpec((1, width, hidden), lambda i: (chunk, 0, 0), pipeline_mode=pl.Buffered(1))

    def whole(shape):
        return pl.BlockSpec(shape, lambda i: (0, 0), pipeline_mode=pl.Buffered(1))

    return pl.pallas_call(
        dx_kernel,
        grid=(1,),
        in_specs=[whole((n_rows, hidden)), whole((n_rows, hidden)), whole((n_rows, LANES)), weight, weight],
        out_specs=whole((n_rows, width + LANES)),
        out_shape=jax.ShapeDtypeStruct((n_rows, width + LANES), BF16),
        compiler_params=pltpu.CompilerParams(vmem_limit_bytes=VMEM_LIMIT),
        cost_estimate=cost(4 * n_rows * width * hidden, 4 * width * hidden + 2 * n_rows * (width + 2 * hidden)),
        name=f"dx{chunk}",
    )(da, db, s, wg, wu)


def combine_kernel(local_exp, capacity, ids_ref, *refs):
    ids_t = ids_ref[...]
    back = refs[:local_exp]
    tok_ref, prob_ref = refs[local_exp:]
    topk, tok = ids_t.shape
    n_experts = back[0].shape[0] // capacity * local_exp
    width = tok_ref.shape[1]
    values = slot_values(ids_t, n_experts, capacity)
    total = jnp.zeros((tok, width), F32)
    by_expert = jnp.zeros((n_experts, tok), F32)
    for chunk in range(local_exp):
        onehot, spread = slot_rows(values, chunk, local_exp, capacity)
        pick = jnp.where(onehot, 1.0, 0.0)
        total = total + dot(pick.astype(BF16), back[chunk][:, :width], TN)
        s = back[chunk][:, width:].astype(F32)
        s = s[:, 0:1] + s[:, 1:2]
        placed = pick * s
        high = placed.astype(BF16)
        low = (placed - high.astype(F32)).astype(BF16)
        by_expert = by_expert + dot(spread, high, TN) + dot(spread, low, TN)
    tok_ref[...] = total.astype(BF16)
    rows = lax.broadcasted_iota(jnp.int32, (n_experts, tok), 0)
    for k in range(topk):
        mine = jnp.where(ids_t[k : k + 1, :] == rows, by_expert, 0.0)
        prob_ref[k : k + 1, :] = jnp.sum(mine, axis=0, keepdims=True)


def combine(local_exp, capacity, ids_t, backs, width):
    topk, tok = ids_t.shape
    n_rows = local_exp * backs[0].shape[0]
    return pl.pallas_call(
        functools.partial(combine_kernel, local_exp, capacity),
        out_shape=[
            jax.ShapeDtypeStruct((tok, width), BF16),
            jax.ShapeDtypeStruct((topk, tok), F32),
        ],
        compiler_params=pltpu.CompilerParams(vmem_limit_bytes=VMEM_LIMIT),
        cost_estimate=cost(2000 * n_rows * tok * width, 2 * width * (n_rows + tok)),
        name="combine",
    )(ids_t, *backs)


def body(tokens, out_grad, expert_ids, route_probs, w_gate, w_up, w_down, decay_mask):
    n_owner = lax.axis_size("expert")
    n_group = lax.axis_size("dp")
    local_exp = w_gate.shape[0]
    width = tokens.shape[1]
    hidden = w_gate.shape[2]
    tok_rows, topk = expert_ids.shape
    n_experts = n_owner * local_exp
    capacity = tok_rows * topk // n_experts
    ids_t = expert_ids.T
    probs_t = route_probs.T
    shard_rows = width // n_group
    first_row = lax.axis_index("dp") * shard_rows

    sends = dispatch(local_exp, capacity, n_experts, ids_t, probs_t, tokens, out_grad)
    got = []
    for rows in sends:
        if got:
            rows, got[-1] = lax.optimization_barrier((rows, got[-1]))
        rows = rows.reshape(n_owner, capacity, 2 * width)
        got.append(lax.all_to_all(rows, "expert", split_axis=0, concat_axis=0, tiled=True))
    summed, backs = [], []
    for chunk in range(local_exp):
        rows = got[chunk].reshape(n_owner * capacity, 2 * width)
        g, da, db, s = expert_grads(chunk, rows, w_gate, w_up, w_down)
        summed.append(lax.psum_scatter(g, "dp", scatter_dimension=0, tiled=True))
        if chunk + 1 < local_exp:
            da, got[chunk + 1] = lax.optimization_barrier((da, got[chunk + 1]))
        dx = input_grads(chunk, da, db, s, w_gate, w_up).reshape(n_owner, capacity, width + LANES)
        back = lax.all_to_all(dx, "expert", split_axis=0, concat_axis=0, tiled=True)
        backs.append(back.reshape(n_owner * capacity, width + LANES))
    grad_tokens, scores = combine(local_exp, capacity, ids_t, backs, width)
    grad_probs = (scores / probs_t.astype(F32)).astype(BF16).T

    rates = decay_mask.astype(F32)

    def update(weight, column):
        weight_f = lax.dynamic_slice_in_dim(weight, first_row, shard_rows, 1).astype(F32)
        grad_w = jnp.stack([s[:, column * hidden : (column + 1) * hidden] for s in summed]).astype(F32)
        factor = rates[:, column][:, None, None]
        return (weight_f - step_size * grad_w - shrink_rate * factor * weight_f).astype(BF16)

    return (grad_tokens, grad_probs, update(w_gate, 0), update(w_up, 1), update(w_down, 2))


def solution(mesh):
    placed = (
        P(("dp", "expert"), None),
        P(("dp", "expert"), None),
        P(("dp", "expert"), None),
        P(("dp", "expert"), None),
        P("expert", None, None),
        P("expert", None, None),
        P("expert", None, None),
        P("expert", None),
    )
    return jax.shard_map(
        body,
        mesh=mesh,
        in_specs=placed,
        out_specs=(
            P(("dp", "expert"), None),
            P(("dp", "expert"), None),
            P("expert", "dp", None),
            P("expert", "dp", None),
            P("expert", "dp", None),
        ),
        check_vma=False,
    )
```

```python
import functools

import jax
import jax.numpy as jnp
from jax import lax
from jax.experimental import pallas as pl
from jax.experimental.pallas import tpu as pltpu
from jax.sharding import PartitionSpec as P

step_size = 0.004
shrink_rate = 0.1
LANES = 128
CORES = 2
F32 = jnp.float32
BF16 = jnp.bfloat16
NN = ((1,), (0,))
NT = ((1,), (1,))
TN = ((0,), (0,))
ANY = pl.BlockSpec(memory_space=pl.ANY)
SMEM = pl.BlockSpec(memory_space=pltpu.SMEM)


def dot(a, b, dims):
    return lax.dot_general(a, b, (dims, ((), ())), preferred_element_type=F32)


def iota(shape, dim):
    return lax.broadcasted_iota(jnp.int32, shape, dim)


def params(mib):
    return pltpu.CompilerParams(vmem_limit_bytes=60 * 1024 * 1024)


def cost(flops, moved):
    return pl.CostEstimate(flops=flops, transcendentals=0, bytes_accessed=moved)


def whole(shape):
    return pl.BlockSpec(shape, lambda *_: (0,) * len(shape), pipeline_mode=pl.Buffered(1))


def routing(meta, topk, n_chip, capacity, stride, plane):
    tok = meta.shape[0]
    eye = jnp.where(iota((tok, tok), 0) == iota((tok, tok), 1), 1.0, 0.0).astype(BF16)
    meta_t = dot(meta, eye, TN)
    expert = (iota((n_chip, tok), 0) * stride + plane).astype(F32)
    hit = jnp.zeros((n_chip, tok), F32)
    prob = jnp.zeros((n_chip, tok), F32)
    for k in range(topk):
        same = meta_t[k : k + 1, :] == expert
        hit = hit + jnp.where(same, 1.0, 0.0)
        prob = prob + jnp.where(same, meta_t[topk + k : topk + k + 1, :], 0.0)
    earlier = jnp.where(iota((tok, tok), 0) < iota((tok, tok), 1), 1.0, 0.0).astype(BF16)
    count = dot(hit.astype(BF16), earlier, NN)
    values = jnp.where(jnp.logical_and(hit > 0.5, count < capacity), count, -1.0)
    rows = n_chip * capacity
    spread = jnp.where(iota((rows, n_chip), 0) // capacity == iota((rows, n_chip), 1), 1.0, 0.0).astype(BF16)
    place = (iota((rows, tok), 0) % capacity).astype(F32)
    onehot = dot(spread, values.astype(BF16), NN) == place
    return onehot, dot(spread, prob.astype(BF16), NN)


def dispatch_kernel(topk, capacity, stride, plane_ref, *refs):
    packed, out_ref = refs[:-1], refs[-1]
    n_chip = out_ref.shape[0]
    width = out_ref.shape[2] // 2
    for g, ref in enumerate(packed):
        onehot, prob_rows = routing(ref[:, 2 * width :], topk, n_chip, capacity, stride, plane_ref[0])
        pick = jnp.where(onehot, 1.0, 0.0).astype(BF16)
        weighted = jnp.where(onehot, prob_rows, 0.0).astype(BF16)
        x = dot(pick, ref[:, :width], NN).astype(BF16)
        do = dot(weighted, ref[:, width : 2 * width], NN).astype(BF16)
        rows = slice(g * capacity, (g + 1) * capacity)
        out_ref[:, rows, :width] = x.reshape(n_chip, capacity, width)
        out_ref[:, rows, width:] = do.reshape(n_chip, capacity, width)


def dispatch(name, plane, packed, n_chip, topk, capacity, stride, width):
    n_rows = len(packed) * capacity
    return pl.pallas_call(
        functools.partial(dispatch_kernel, topk, capacity, stride),
        in_specs=[SMEM] + [pl.BlockSpec(memory_space=pltpu.VMEM)] * len(packed),
        out_shape=jax.ShapeDtypeStruct((n_chip, n_rows, 2 * width), BF16),
        compiler_params=params(32),
        cost_estimate=cost(4 * n_chip * n_rows * LANES * width, 8 * n_chip * n_rows * width),
        name=name,
    )(plane, *packed)


def hidden_kernel(x_ref, do_ref, wg_ref, wu_ref, wd_ref, hid_ref, da_ref, db_ref, s_ref):
    gate = dot(x_ref[...], wg_ref[...], NN)
    upper = dot(x_ref[...], wu_ref[...], NN)
    sig = jax.nn.sigmoid(gate)
    act = gate * sig
    hid = (act * upper).astype(BF16)
    hid_ref[...] = hid
    dhid = dot(do_ref[...], wd_ref[...], NN)
    total = jnp.sum(hid.astype(F32) * dhid, axis=1, keepdims=True)
    high = total.astype(BF16).astype(F32)
    lane = iota(s_ref.shape, 1)
    s_ref[...] = jnp.where(lane == 0, high, jnp.where(lane == 1, total - high, 0.0)).astype(BF16)
    da_ref[...] = (dhid * upper * sig * (1.0 + gate * (1.0 - sig))).astype(BF16)
    db_ref[...] = (dhid * act).astype(BF16)


def hidden_grads(name, rows, wg, wu, wd):
    n_rows, width = rows.shape[0], rows.shape[1] // 2
    hidden = wg.shape[1]
    return pl.pallas_call(
        hidden_kernel,
        grid=(1,),
        in_specs=[
            pl.BlockSpec((n_rows, width), lambda i: (0, 0), pipeline_mode=pl.Buffered(1)),
            pl.BlockSpec((n_rows, width), lambda i: (0, 1), pipeline_mode=pl.Buffered(1)),
            whole((width, hidden)),
            whole((width, hidden)),
            whole((width, hidden)),
        ],
        out_specs=[whole((n_rows, hidden))] * 3 + [whole((n_rows, LANES))],
        out_shape=[jax.ShapeDtypeStruct((n_rows, hidden), BF16)] * 3
        + [jax.ShapeDtypeStruct((n_rows, LANES), BF16)],
        compiler_params=params(32),
        cost_estimate=cost(6 * n_rows * width * hidden, 6 * width * hidden + n_rows * (4 * width + 6 * hidden)),
        name=name,
    )(rows, rows, wg, wu, wd)


def dx_kernel(da_ref, db_ref, s_ref, wg_ref, wu_ref, *refs):
    out_ref = refs[-1]
    n_chip, capacity, hidden = da_ref.shape
    width = wg_ref.shape[0]
    da = da_ref[...].reshape(n_chip * capacity, hidden)
    db = db_ref[...].reshape(n_chip * capacity, hidden)
    dx = (dot(da, wg_ref[...], NT) + dot(db, wu_ref[...], NT)).astype(BF16)
    out_ref[:, :, :width] = dx.reshape(n_chip, capacity, width)
    out_ref[:, :, width:] = s_ref[...]


def input_grads(name, da, db, s, wg, wu, n_chip, capacity, n_group, first, into):
    width, hidden = wg.shape
    count = da.shape[0] // (n_chip * capacity)

    def split(a):
        return a.reshape(n_chip, count * capacity, a.shape[1])

    def group(lanes, shift):
        return pl.BlockSpec((n_chip, capacity, lanes), lambda i: (0, i + shift, 0))

    extra = [] if into is None else [into]
    return pl.pallas_call(
        dx_kernel,
        grid=(count,),
        in_specs=[
            group(hidden, 0),
            group(hidden, 0),
            group(LANES, 0),
            whole((width, hidden)),
            whole((width, hidden)),
        ]
        + [ANY] * len(extra),
        out_specs=group(width + LANES, first),
        out_shape=jax.ShapeDtypeStruct((n_chip, n_group * capacity, width + LANES), BF16),
        input_output_aliases={5: 0} if extra else {},
        compiler_params=params(32),
        cost_estimate=cost(4 * da.shape[0] * width * hidden, 4 * width * hidden + 2 * da.shape[0] * width),
        name=name,
    )(split(da), split(db), split(s), wg, wu, *extra)


def weight_kernel(n_chunk, with_sum, where_ref, *refs):
    xs, dos = refs[:n_chunk], refs[n_chunk : 2 * n_chunk]
    hids, das, dbs = (refs[(2 + i) * n_chunk : (3 + i) * n_chunk] for i in range(3))
    rest = refs[5 * n_chunk :]
    out_ref = rest[-1]
    hidden = hids[0].shape[1]

    def total(lefts, rights):
        out = dot(lefts[0][...], rights[0][...], TN)
        for left, right in zip(lefts[1:], rights[1:]):
            out = out + dot(left[...], right[...], TN)
        return out

    for m, (lefts, rights) in enumerate(((xs, das), (xs, dbs), (dos, hids))):
        part = total(lefts, rights)
        lanes = slice(m * hidden, (m + 1) * hidden)
        if with_sum:
            part = part + rest[0][0, :, lanes].astype(F32)
        out_ref[0, :, lanes] = part.astype(BF16)


def weight_grads(name, where, steps, rows, hids, das, dbs, add=None, add_at=0):
    n_chunk = len(rows)
    width, hidden = rows[0].shape[1] // 2, hids[0].shape[1]
    half = width // 8
    lefts = width // half

    def columns(r, shift):
        return pl.BlockSpec((r.shape[0], half), lambda i, at: (0, at[i] + shift))

    in_specs = [columns(r, 0) for r in rows] + [columns(r, lefts) for r in rows]
    in_specs += [whole(a.shape) for a in hids + das + dbs]
    args = rows + rows + hids + das + dbs
    if add is not None:
        in_specs.append(pl.BlockSpec((1, half, 3 * hidden), lambda i, at: (i + add_at, 0, 0)))
        args.append(add)
    total = sum(r.shape[0] for r in rows)
    return pl.pallas_call(
        functools.partial(weight_kernel, n_chunk, add is not None),
        grid_spec=pltpu.PrefetchScalarGridSpec(
            num_scalar_prefetch=1,
            grid=(steps,),
            in_specs=in_specs,
            out_specs=pl.BlockSpec((1, half, 3 * hidden), lambda i, at: (i, 0, 0)),
        ),
        out_shape=jax.ShapeDtypeStruct((steps, half, 3 * hidden), BF16),
        compiler_params=params(32),
        cost_estimate=cost(6 * steps * total * half * hidden, 6 * total * hidden + 6 * steps * half * hidden),
        name=name,
    )(where, *args)


def pick_kernel(n_out, index_ref, *refs):
    sources, out_refs, sems = refs[: -n_out - 1], refs[-n_out - 1 : -1], refs[-1]
    per = out_refs[0].shape[0]
    for o in range(n_out * per):
        for s, source in enumerate(sources):

            @pl.when(index_ref[o] == s)
            def _():
                pltpu.make_async_copy(source.at[0], out_refs[o // per].at[o % per], sems.at[o]).start()

    for o in range(n_out * per):
        pltpu.make_async_copy(sources[0].at[0], out_refs[o // per].at[o % per], sems.at[o]).wait()


def pick(index, sources, n_out, per):
    shape = (per,) + sources[0].shape[1:]
    return pl.pallas_call(
        functools.partial(pick_kernel, n_out),
        in_specs=[SMEM] + [ANY] * len(sources),
        out_specs=[ANY] * n_out,
        out_shape=[jax.ShapeDtypeStruct(shape, BF16)] * n_out,
        scratch_shapes=[pltpu.SemaphoreType.DMA((n_out * per,))],
        compiler_params=params(16),
        name="pick",
    )(index, *sources)


def update_kernel(where_ref, mask_ref, own_ref, other_ref, *refs):
    weights, outs = refs[:3], refs[3:]
    hidden = weights[0].shape[2]
    j = pl.program_id(1)

    def write(grad_ref):
        for m in range(3):
            rate = mask_ref[j, m].astype(F32)
            weight = weights[m][0].astype(F32)
            grad = grad_ref[0, :, m * hidden : (m + 1) * hidden].astype(F32)
            outs[m][0] = (weight - step_size * grad - shrink_rate * rate * weight).astype(BF16)

    @pl.when(pl.program_id(0) == 0)
    def _():
        write(own_ref)

    @pl.when(pl.program_id(0) == 1)
    def _():
        write(other_ref)


def update(where, mask, own, other, weights, shard_rows):
    local, half, _ = own.shape
    hidden = weights[0].shape[2]
    last = local - 1

    def at(h, w):
        return w[0] * (1 - h) + (1 - w[0]) * h

    weight = pl.BlockSpec((1, half, hidden), lambda h, j, w: (j, CORES * w[1] + at(h, w), 0))
    result = pl.BlockSpec((1, half, hidden), lambda h, j, w: (j, at(h, w), 0))
    return pl.pallas_call(
        update_kernel,
        grid_spec=pltpu.PrefetchScalarGridSpec(
            num_scalar_prefetch=1,
            grid=(CORES, local),
            in_specs=[
                SMEM,
                pl.BlockSpec((1, half, 3 * hidden), lambda h, j, w: (j * (1 - h) + last * h, 0, 0)),
                pl.BlockSpec((1, half, 3 * hidden), lambda h, j, w: (j * h, 0, 0)),
            ]
            + [weight] * 3,
            out_specs=[result] * 3,
        ),
        out_shape=[jax.ShapeDtypeStruct((local, shard_rows, hidden), BF16)] * 3,
        compiler_params=params(32),
        name="update",
    )(where, mask, own, other, *weights)


def combine_kernel(topk, capacity, stride, plane_ref, back_ref, *refs):
    count = len(refs) // 2
    n_chip = back_ref.shape[0]
    width = back_ref.shape[2] - LANES
    for g in range(count):
        meta = refs[g][:, 2 * width :]
        out_ref = refs[count + g]
        tok = meta.shape[0]
        onehot, _ = routing(meta, topk, n_chip, capacity, stride, plane_ref[0])
        pick_f = jnp.where(onehot, 1.0, 0.0)
        n_rows = n_chip * capacity
        rows = slice(g * capacity, (g + 1) * capacity)
        dx = back_ref[:, rows, :width].reshape(n_rows, width)
        out_ref[:, :width] = dot(pick_f.astype(BF16), dx, TN).astype(BF16)
        s = back_ref[:, rows, width:].reshape(n_rows, LANES).astype(F32)
        placed = pick_f * (s[:, 0:1] + s[:, 1:2])
        high = placed.astype(BF16)
        low = (placed - high.astype(F32)).astype(BF16)
        spread = jnp.where(iota((n_rows, LANES), 0) // capacity == iota((n_rows, LANES), 1), 1.0, 0.0)
        spread = spread.astype(BF16)
        by_expert = dot(high, spread, TN) + dot(low, spread, TN)
        lane = iota((tok, LANES), 1)
        expert = (lane * stride + plane_ref[0]).astype(F32)
        ids = meta.astype(F32)
        scores = jnp.zeros((tok, LANES), F32)
        for k in range(topk):
            mine = jnp.where(ids[:, k : k + 1] == expert, by_expert, 0.0)
            mine = jnp.sum(mine, axis=1, keepdims=True)
            top = mine.astype(BF16).astype(F32)
            scores = scores + jnp.where(lane == k, top, 0.0) + jnp.where(lane == topk + k, mine - top, 0.0)
        out_ref[:, width:] = scores.astype(BF16)


def combine(plane, back, packed, topk, capacity, stride):
    tok = packed[0].shape[0]
    lanes = back.shape[2]
    return pl.pallas_call(
        functools.partial(combine_kernel, topk, capacity, stride),
        in_specs=[SMEM] + [pl.BlockSpec(memory_space=pltpu.VMEM)] * (1 + len(packed)),
        out_shape=[jax.ShapeDtypeStruct((tok, lanes), BF16)] * len(packed),
        compiler_params=params(32),
        cost_estimate=cost(2 * back.shape[0] * back.shape[1] * tok * lanes, 4 * back.size),
        name="combine",
    )(plane, back, *packed)


def finish_kernel(topk, probs_ref, *refs):
    parts, (tok_ref, prob_ref) = refs[:-2], refs[-2:]
    width = tok_ref.shape[1]
    total = parts[0][...].astype(F32)
    for part in parts[1:]:
        total = total + part[...].astype(F32)
    tok_ref[...] = total[:, :width].astype(BF16)
    scores = total[:, width : width + topk] + total[:, width + topk : width + 2 * topk]
    prob_ref[...] = (scores / probs_ref[...].astype(F32)).astype(BF16)


def finish(probs, parts, width):
    tok, topk = probs.shape
    return pl.pallas_call(
        functools.partial(finish_kernel, topk),
        out_shape=[jax.ShapeDtypeStruct((tok, width), BF16), jax.ShapeDtypeStruct((tok, topk), BF16)],
        compiler_params=params(32),
        name="finish",
    )(probs, *parts)


def body(tokens, out_grad, expert_ids, route_probs, w_gate, w_up, w_down, decay_mask):
    n_owner = lax.axis_size("expert")
    n_group = lax.axis_size("dp")
    local_exp = w_gate.shape[0]
    width = tokens.shape[1]
    tok_rows, topk = expert_ids.shape
    n_experts = n_owner * local_exp
    capacity = tok_rows * topk // n_experts
    n_chip = n_owner // CORES
    stride = CORES * local_exp
    shard_rows = width // n_group
    p = lax.axis_index("dp").astype(jnp.int32)
    core = lax.axis_index("expert").astype(jnp.int32) % CORES
    plane = p.reshape(1)
    same_core = [[CORES * c + k for c in range(n_chip)] for k in range(CORES)]
    other_core = [(q, q ^ 1) for q in range(n_owner)]

    def across(a, r):
        return lax.ppermute(a, "dp", [(i, (i + r) % n_group) for i in range(n_group)])

    def exchange(a):
        return lax.all_to_all(a, "expert", 0, 0, axis_index_groups=same_core, tiled=True)

    meta = jnp.concatenate(
        [expert_ids.astype(BF16), route_probs, jnp.zeros((tok_rows, LANES - 2 * topk), BF16)], axis=1
    )
    packed = jnp.concatenate([tokens, out_grad, meta], axis=1)
    near, far = (1, n_group - 1), (2,)
    from_near = [across(packed, r) for r in near]
    from_far = [across(packed, r) for r in far]

    mine = core == p // local_exp
    weights = []
    for w in (w_gate, w_up, w_down):
        other = lax.ppermute(w, "expert", other_core)
        pick_of = functools.partial(lax.dynamic_index_in_dim, index=p % local_exp, axis=0, keepdims=False)
        weights.append(jnp.where(mine, pick_of(w), pick_of(other)))
    wg, wu, wd = weights

    got = []
    for name, chunk in (("own", [packed]), ("near", from_near), ("far", from_far)):
        if got:
            chunk = list(chunk)
            chunk[0], got[-1] = lax.optimization_barrier((chunk[0], got[-1])) if False else (chunk[0], got[-1])
        rows = dispatch("send_" + name, plane, chunk, n_chip, topk, capacity, stride, width)
        if got:
            rows, got[-1] = lax.optimization_barrier((rows, got[-1]))
        got.append(exchange(rows))

    rows, hids, das, dbs, sums = [], [], [], [], []
    for name, part in zip(("own", "near", "far"), got):
        part = part.reshape(-1, 2 * width)
        hid, da, db, s = hidden_grads("hidden_" + name, part, wg, wu, wd)
        rows.append(part)
        hids.append(hid)
        das.append(da)
        dbs.append(db)
        sums.append(s)

    order = (2, 1, n_group - 1, 0)
    blocks = jnp.stack([CORES * ((p + r) % n_group) for r in order]).astype(jnp.int32)
    theirs = weight_grads("theirs", blocks + (1 - core), n_group, rows, hids, das, dbs)
    added = lax.ppermute(theirs, "expert", other_core)

    dx, first = None, 0
    for i, name in enumerate(("own", "near", "far")):
        dx = input_grads("dx_" + name, das[i], dbs[i], sums[i], wg, wu, n_chip, capacity, n_group, first, dx)
        first += rows[i].shape[0] // (n_chip * capacity)
    back = exchange(dx)

    landed = [None] * n_group
    for i, r in enumerate(order):
        block = weight_grads(
            f"mine_{r}", blocks[i : i + 1] + core, 1, rows, hids, das, dbs, added, i
        )
        landed[r] = across(block, r) if r else block

    parts = combine(plane, back, [packed] + from_near + from_far, topk, capacity, stride)
    home = [parts[0]] + [across(a, n_group - r) for a, r in zip(parts[1:], near + far)]
    grad_tokens, grad_probs = finish(route_probs, home, width)

    def source(owner, j):
        return (p - (local_exp * owner + j)) % n_group

    index = jnp.stack(
        [source(1 - core, j) for j in range(local_exp)] + [source(core, j) for j in range(local_exp)]
    ).astype(jnp.int32)
    outgoing, own = pick(index, landed, 2, local_exp)
    other = lax.ppermute(outgoing, "expert", other_core)
    where = jnp.stack([core, p]).astype(jnp.int32)
    new = update(where, decay_mask, own, other, (w_gate, w_up, w_down), shard_rows)
    return (grad_tokens, grad_probs, *new)


def solution(mesh):
    placed = (
        P(("dp", "expert"), None),
        P(("dp", "expert"), None),
        P(("dp", "expert"), None),
        P(("dp", "expert"), None),
        P("expert", None, None),
        P("expert", None, None),
        P("expert", None, None),
        P("expert", None),
    )
    return jax.shard_map(
        body,
        mesh=mesh,
        in_specs=placed,
        out_specs=(
            P(("dp", "expert"), None),
            P(("dp", "expert"), None),
            P("expert", "dp", None),
            P("expert", "dp", None),
            P("expert", "dp", None),
        ),
        check_vma=False,
    )
```

```python
import functools

import jax
import jax.numpy as jnp
from jax import lax
from jax.experimental import pallas as pl
from jax.experimental.pallas import tpu as pltpu
from jax.sharding import PartitionSpec as P

step_size = 0.004
shrink_rate = 0.1
LANES = 128
CORES = 2
F32 = jnp.float32
BF16 = jnp.bfloat16
NN = ((1,), (0,))
NT = ((1,), (1,))
TN = ((0,), (0,))
ANY = pl.BlockSpec(memory_space=pl.ANY)
SMEM = pl.BlockSpec(memory_space=pltpu.SMEM)


def dot(a, b, dims):
    return lax.dot_general(a, b, (dims, ((), ())), preferred_element_type=F32)


def iota(shape, dim):
    return lax.broadcasted_iota(jnp.int32, shape, dim)


def params(mib):
    return pltpu.CompilerParams(vmem_limit_bytes=60 * 1024 * 1024)


def cost(flops, moved):
    return pl.CostEstimate(flops=flops, transcendentals=0, bytes_accessed=moved)


def whole(shape):
    return pl.BlockSpec(shape, lambda *_: (0,) * len(shape), pipeline_mode=pl.Buffered(1))


def routing(meta, topk, n_chip, capacity, stride, plane):
    tok = meta.shape[0]
    eye = jnp.where(iota((tok, tok), 0) == iota((tok, tok), 1), 1.0, 0.0).astype(BF16)
    meta_t = dot(meta, eye, TN)
    expert = (iota((n_chip, tok), 0) * stride + plane).astype(F32)
    hit = jnp.zeros((n_chip, tok), F32)
    prob = jnp.zeros((n_chip, tok), F32)
    for k in range(topk):
        same = meta_t[k : k + 1, :] == expert
        hit = hit + jnp.where(same, 1.0, 0.0)
        prob = prob + jnp.where(same, meta_t[topk + k : topk + k + 1, :], 0.0)
    earlier = jnp.where(iota((tok, tok), 0) < iota((tok, tok), 1), 1.0, 0.0).astype(BF16)
    count = dot(hit.astype(BF16), earlier, NN)
    values = jnp.where(jnp.logical_and(hit > 0.5, count < capacity), count, -1.0)
    rows = n_chip * capacity
    spread = jnp.where(iota((rows, n_chip), 0) // capacity == iota((rows, n_chip), 1), 1.0, 0.0).astype(BF16)
    place = (iota((rows, tok), 0) % capacity).astype(F32)
    onehot = dot(spread, values.astype(BF16), NN) == place
    return onehot, dot(spread, prob.astype(BF16), NN)


def dispatch_kernel(topk, capacity, stride, plane_ref, *refs):
    packed, out_ref = refs[:-1], refs[-1]
    n_chip = out_ref.shape[0]
    width = out_ref.shape[2] // 2
    for g, ref in enumerate(packed):
        onehot, prob_rows = routing(ref[:, 2 * width :], topk, n_chip, capacity, stride, plane_ref[0])
        pick = jnp.where(onehot, 1.0, 0.0).astype(BF16)
        weighted = jnp.where(onehot, prob_rows, 0.0).astype(BF16)
        x = dot(pick, ref[:, :width], NN).astype(BF16)
        do = dot(weighted, ref[:, width : 2 * width], NN).astype(BF16)
        rows = slice(g * capacity, (g + 1) * capacity)
        out_ref[:, rows, :width] = x.reshape(n_chip, capacity, width)
        out_ref[:, rows, width:] = do.reshape(n_chip, capacity, width)


def dispatch(name, plane, packed, n_chip, topk, capacity, stride, width):
    n_rows = len(packed) * capacity
    return pl.pallas_call(
        functools.partial(dispatch_kernel, topk, capacity, stride),
        in_specs=[SMEM] + [pl.BlockSpec(memory_space=pltpu.VMEM)] * len(packed),
        out_shape=jax.ShapeDtypeStruct((n_chip, n_rows, 2 * width), BF16),
        compiler_params=params(32),
        cost_estimate=cost(4 * n_chip * n_rows * LANES * width, 8 * n_chip * n_rows * width),
        name=name,
    )(plane, *packed)


def hidden_kernel(x_ref, do_ref, wg_ref, wu_ref, wd_ref, hid_ref, da_ref, db_ref, s_ref, sum_ref):
    step = pl.program_id(0)
    gate = dot(x_ref[...], wg_ref[...], NN)
    upper = dot(x_ref[...], wu_ref[...], NN)
    sig = jax.nn.sigmoid(gate)
    act = gate * sig
    hid = (act * upper).astype(BF16)
    hid_ref[...] = hid
    dhid = dot(do_ref[...], wd_ref[...], NN)
    part = jnp.sum(hid.astype(F32) * dhid, axis=1, keepdims=True)
    da_ref[...] = (dhid * upper * sig * (1.0 + gate * (1.0 - sig))).astype(BF16)
    db_ref[...] = (dhid * act).astype(BF16)

    @pl.when(step == 0)
    def _():
        sum_ref[...] = jnp.broadcast_to(part, sum_ref.shape)

    @pl.when(step > 0)
    def _():
        sum_ref[...] = sum_ref[...] + part

    @pl.when(step == pl.num_programs(0) - 1)
    def _():
        total = sum_ref[...]
        high = total.astype(BF16).astype(F32)
        lane = iota(s_ref.shape, 1)
        s_ref[...] = jnp.where(lane == 0, high, jnp.where(lane == 1, total - high, 0.0)).astype(BF16)


def hidden_grads(name, rows, wg, wu, wd):
    n_rows, width = rows.shape[0], rows.shape[1] // 2
    hidden = wg.shape[1]
    block = 2 * LANES
    weight = pl.BlockSpec((width, block), lambda i: (0, i))
    result = pl.BlockSpec((n_rows, block), lambda i: (0, i))
    return pl.pallas_call(
        hidden_kernel,
        grid=(hidden // block,),
        in_specs=[
            pl.BlockSpec((n_rows, width), lambda i: (0, 0), pipeline_mode=pl.Buffered(1)),
            pl.BlockSpec((n_rows, width), lambda i: (0, 1), pipeline_mode=pl.Buffered(1)),
            weight,
            weight,
            weight,
        ],
        out_specs=[result] * 3 + [whole((n_rows, LANES))],
        out_shape=[jax.ShapeDtypeStruct((n_rows, hidden), BF16)] * 3
        + [jax.ShapeDtypeStruct((n_rows, LANES), BF16)],
        scratch_shapes=[pltpu.VMEM((n_rows, LANES), F32)],
        compiler_params=params(32),
        cost_estimate=cost(6 * n_rows * width * hidden, 6 * width * hidden + n_rows * (4 * width + 6 * hidden)),
        name=name,
    )(rows, rows, wg, wu, wd)


def dx_kernel(da_ref, db_ref, s_ref, wg_ref, wu_ref, *refs):
    out_ref = refs[-1]
    n_chip, capacity, hidden = da_ref.shape
    width = wg_ref.shape[0]
    da = da_ref[...].reshape(n_chip * capacity, hidden)
    db = db_ref[...].reshape(n_chip * capacity, hidden)
    dx = (dot(da, wg_ref[...], NT) + dot(db, wu_ref[...], NT)).astype(BF16)
    out_ref[:, :, :width] = dx.reshape(n_chip, capacity, width)
    out_ref[:, :, width:] = s_ref[...]


def input_grads(name, da, db, s, wg, wu, n_chip, capacity, n_group, first, into):
    width, hidden = wg.shape
    count = da.shape[0] // (n_chip * capacity)

    def split(a):
        return a.reshape(n_chip, count * capacity, a.shape[1])

    def group(lanes, shift):
        return pl.BlockSpec((n_chip, capacity, lanes), lambda i: (0, i + shift, 0))

    extra = [] if into is None else [into]
    return pl.pallas_call(
        dx_kernel,
        grid=(count,),
        in_specs=[
            group(hidden, 0),
            group(hidden, 0),
            group(LANES, 0),
            whole((width, hidden)),
            whole((width, hidden)),
        ]
        + [ANY] * len(extra),
        out_specs=group(width + LANES, first),
        out_shape=jax.ShapeDtypeStruct((n_chip, n_group * capacity, width + LANES), BF16),
        input_output_aliases={5: 0} if extra else {},
        compiler_params=params(32),
        cost_estimate=cost(4 * da.shape[0] * width * hidden, 4 * width * hidden + 2 * da.shape[0] * width),
        name=name,
    )(split(da), split(db), split(s), wg, wu, *extra)


def weight_kernel(n_chunk, where_ref, *refs):
    xs, dos = refs[:n_chunk], refs[n_chunk : 2 * n_chunk]
    hids, das, dbs = (refs[(2 + i) * n_chunk : (3 + i) * n_chunk] for i in range(3))
    rest = refs[5 * n_chunk :]
    out_ref = rest[-1]
    hidden = hids[0].shape[1]

    def total(lefts, rights):
        out = dot(lefts[0][...], rights[0][...], TN)
        for left, right in zip(lefts[1:], rights[1:]):
            out = out + dot(left[...], right[...], TN)
        return out

    for m, (lefts, rights) in enumerate(((xs, das), (xs, dbs), (dos, hids))):
        part = total(lefts, rights)
        lanes = slice(m * hidden, (m + 1) * hidden)
        for addend in rest[:-1]:
            part = part + addend[0, :, lanes].astype(F32)
        out_ref[0, :, lanes] = part.astype(BF16)


def weight_grads(name, where, steps, rows, hids, das, dbs, add=()):
    n_chunk = len(rows)
    width, hidden = rows[0].shape[1] // 2, hids[0].shape[1]
    half = width // 8
    lefts = width // half

    def columns(r, shift):
        return pl.BlockSpec((r.shape[0], half), lambda i, at: (0, at[i] + shift))

    in_specs = [columns(r, 0) for r in rows] + [columns(r, lefts) for r in rows]
    in_specs += [whole(a.shape) for a in hids + das + dbs]
    args = rows + rows + hids + das + dbs
    for addend, first in add:
        in_specs.append(pl.BlockSpec((1, half, 3 * hidden), lambda i, at, first=first: (i + first, 0, 0)))
        args.append(addend)
    total = sum(r.shape[0] for r in rows)
    return pl.pallas_call(
        functools.partial(weight_kernel, n_chunk),
        grid_spec=pltpu.PrefetchScalarGridSpec(
            num_scalar_prefetch=1,
            grid=(steps,),
            in_specs=in_specs,
            out_specs=pl.BlockSpec((1, half, 3 * hidden), lambda i, at: (i, 0, 0)),
        ),
        out_shape=jax.ShapeDtypeStruct((steps, half, 3 * hidden), BF16),
        compiler_params=params(32),
        cost_estimate=cost(6 * steps * total * half * hidden, 6 * total * hidden + 6 * steps * half * hidden),
        name=name,
    )(where, *args)


def fetch(index, sources, target, sem):
    for i, source in enumerate(sources):

        @pl.when(index == i)
        def _():
            pltpu.make_async_copy(source.at[0], target, sem).start()

    pltpu.make_async_copy(sources[0].at[0], target, sem).wait()


def pick_kernel(index_ref, *refs):
    fetch(index_ref[pl.program_id(0)], refs[:-2], refs[-2].at[0], refs[-1])


def pick(index, sources, count):
    _, half, lanes = sources[0].shape
    return pl.pallas_call(
        pick_kernel,
        grid_spec=pltpu.PrefetchScalarGridSpec(
            num_scalar_prefetch=1,
            grid=(count,),
            in_specs=[ANY] * len(sources),
            out_specs=pl.BlockSpec((1, half, lanes), lambda j, w: (j, 0, 0)),
            scratch_shapes=[pltpu.SemaphoreType.DMA],
        ),
        out_shape=jax.ShapeDtypeStruct((count, half, lanes), BF16),
        compiler_params=params(16),
        name="pick",
    )(index, *sources)


def update_kernel(n_source, where_ref, mask_ref, *refs):
    sources, other_ref = refs[:n_source], refs[n_source]
    weights, outs = refs[n_source + 1 : n_source + 4], refs[n_source + 4 : n_source + 7]
    own_ref, sem = refs[-2:]
    hidden = weights[0].shape[2]
    j = pl.program_id(1)

    def write(grad_ref, *lead):
        for m in range(3):
            rate = mask_ref[j, m].astype(F32)
            weight = weights[m][0].astype(F32)
            grad = grad_ref[(*lead, slice(None), slice(m * hidden, (m + 1) * hidden))].astype(F32)
            outs[m][0] = (weight - step_size * grad - shrink_rate * rate * weight).astype(BF16)

    @pl.when(pl.program_id(0) == 0)
    def _():
        fetch(where_ref[2 + j], sources, own_ref, sem)
        write(own_ref)

    @pl.when(pl.program_id(0) == 1)
    def _():
        write(other_ref, 0)


def update(where, mask, sources, other, weights, shard_rows):
    local, half, _ = other.shape
    hidden = weights[0].shape[2]

    def at(h, w):
        return w[0] * (1 - h) + (1 - w[0]) * h

    weight = pl.BlockSpec((1, half, hidden), lambda h, j, w: (j, CORES * w[1] + at(h, w), 0))
    result = pl.BlockSpec((1, half, hidden), lambda h, j, w: (j, at(h, w), 0))
    return pl.pallas_call(
        functools.partial(update_kernel, len(sources)),
        grid_spec=pltpu.PrefetchScalarGridSpec(
            num_scalar_prefetch=1,
            grid=(CORES, local),
            in_specs=[SMEM]
            + [ANY] * len(sources)
            + [pl.BlockSpec((1, half, 3 * hidden), lambda h, j, w: (j * h, 0, 0))]
            + [weight] * 3,
            out_specs=[result] * 3,
            scratch_shapes=[pltpu.VMEM((half, 3 * hidden), BF16), pltpu.SemaphoreType.DMA],
        ),
        out_shape=[jax.ShapeDtypeStruct((local, shard_rows, hidden), BF16)] * 3,
        compiler_params=params(32),
        name="update",
    )(where, mask, *sources, other, *weights)


def combine_kernel(topk, capacity, stride, plane_ref, back_ref, *refs):
    count = len(refs) // 2
    n_chip = back_ref.shape[0]
    width = back_ref.shape[2] - LANES
    for g in range(count):
        meta = refs[g][:, 2 * width :]
        out_ref = refs[count + g]
        tok = meta.shape[0]
        onehot, _ = routing(meta, topk, n_chip, capacity, stride, plane_ref[0])
        pick_f = jnp.where(onehot, 1.0, 0.0)
        n_rows = n_chip * capacity
        rows = slice(g * capacity, (g + 1) * capacity)
        dx = back_ref[:, rows, :width].reshape(n_rows, width)
        out_ref[:, :width] = dot(pick_f.astype(BF16), dx, TN).astype(BF16)
        s = back_ref[:, rows, width:].reshape(n_rows, LANES).astype(F32)
        placed = pick_f * (s[:, 0:1] + s[:, 1:2])
        high = placed.astype(BF16)
        low = (placed - high.astype(F32)).astype(BF16)
        spread = jnp.where(iota((n_rows, LANES), 0) // capacity == iota((n_rows, LANES), 1), 1.0, 0.0)
        spread = spread.astype(BF16)
        by_expert = dot(high, spread, TN) + dot(low, spread, TN)
        lane = iota((tok, LANES), 1)
        expert = (lane * stride + plane_ref[0]).astype(F32)
        ids = meta.astype(F32)
        scores = jnp.zeros((tok, LANES), F32)
        for k in range(topk):
            mine = jnp.where(ids[:, k : k + 1] == expert, by_expert, 0.0)
            mine = jnp.sum(mine, axis=1, keepdims=True)
            top = mine.astype(BF16).astype(F32)
            scores = scores + jnp.where(lane == k, top, 0.0) + jnp.where(lane == topk + k, mine - top, 0.0)
        out_ref[:, width:] = scores.astype(BF16)


def combine(plane, back, packed, topk, capacity, stride):
    tok = packed[0].shape[0]
    lanes = back.shape[2]
    return pl.pallas_call(
        functools.partial(combine_kernel, topk, capacity, stride),
        in_specs=[SMEM] + [pl.BlockSpec(memory_space=pltpu.VMEM)] * (1 + len(packed)),
        out_shape=[jax.ShapeDtypeStruct((tok, lanes), BF16)] * len(packed),
        compiler_params=params(32),
        cost_estimate=cost(2 * back.shape[0] * back.shape[1] * tok * lanes, 4 * back.size),
        name="combine",
    )(plane, back, *packed)


def finish_kernel(topk, probs_ref, *refs):
    parts, (tok_ref, prob_ref) = refs[:-2], refs[-2:]
    width = tok_ref.shape[1]
    total = parts[0][...].astype(F32)
    for part in parts[1:]:
        total = total + part[...].astype(F32)
    tok_ref[...] = total[:, :width].astype(BF16)
    scores = total[:, width : width + topk] + total[:, width + topk : width + 2 * topk]
    prob_ref[...] = (scores / probs_ref[...].astype(F32)).astype(BF16)


def finish(probs, parts, width):
    tok, topk = probs.shape
    return pl.pallas_call(
        functools.partial(finish_kernel, topk),
        out_shape=[jax.ShapeDtypeStruct((tok, width), BF16), jax.ShapeDtypeStruct((tok, topk), BF16)],
        compiler_params=params(32),
        name="finish",
    )(probs, *parts)


def body(tokens, out_grad, expert_ids, route_probs, w_gate, w_up, w_down, decay_mask):
    n_owner = lax.axis_size("expert")
    n_group = lax.axis_size("dp")
    local_exp = w_gate.shape[0]
    width = tokens.shape[1]
    tok_rows, topk = expert_ids.shape
    n_experts = n_owner * local_exp
    capacity = tok_rows * topk // n_experts
    n_chip = n_owner // CORES
    stride = CORES * local_exp
    shard_rows = width // n_group
    p = lax.axis_index("dp").astype(jnp.int32)
    core = lax.axis_index("expert").astype(jnp.int32) % CORES
    plane = p.reshape(1)
    same_core = [[CORES * c + k for c in range(n_chip)] for k in range(CORES)]
    other_core = [(q, q ^ 1) for q in range(n_owner)]

    def across(a, r):
        return lax.ppermute(a, "dp", [(i, (i + r) % n_group) for i in range(n_group)])

    def exchange(a):
        return lax.all_to_all(a, "expert", 0, 0, axis_index_groups=same_core, tiled=True)

    meta = jnp.concatenate(
        [expert_ids.astype(BF16), route_probs, jnp.zeros((tok_rows, LANES - 2 * topk), BF16)], axis=1
    )
    packed = jnp.concatenate([tokens, out_grad, meta], axis=1)
    shifts = (1, n_group - 1, 2)
    moved = [across(packed, r) for r in shifts]
    from_near, from_far = moved[:2], moved[2:]

    mine = core == p // local_exp
    weights = []
    for w in (w_gate, w_up, w_down):
        other = lax.ppermute(w, "expert", other_core)
        pick_of = functools.partial(lax.dynamic_index_in_dim, index=p % local_exp, axis=0, keepdims=False)
        weights.append(jnp.where(mine, pick_of(w), pick_of(other)))

    def send(name, chunk):
        return dispatch("send_" + name, plane, chunk, n_chip, topk, capacity, stride, width)

    def flat(part):
        return part.reshape(-1, 2 * width)

    def hidden_of(name, part):
        return hidden_grads("hidden_" + name, part, *weights)

    def dx_of(name, grads, first, into):
        _, da, db, s = grads
        return input_grads("dx_" + name, da, db, s, weights[0], weights[1], n_chip, capacity, n_group, first, into)

    got_own = exchange(send("own", [packed]))
    to_near, got_own = lax.optimization_barrier((send("near", from_near), got_own))
    got_near = exchange(to_near)
    own = flat(got_own)
    own_grads = hidden_of("own", own)
    dx = dx_of("own", own_grads, 0, None)
    to_far, got_near, dx, *own_grads = lax.optimization_barrier((send("far", from_far), got_near, dx, *own_grads))
    got_far = exchange(to_far)
    near = flat(got_near)
    near_grads = hidden_of("near", near)
    dx = dx_of("near", near_grads, 1, dx)
    order = (2, 1, n_group - 1, 0)
    blocks = jnp.stack([CORES * ((p + r) % n_group) for r in order]).astype(jnp.int32)
    both = jnp.concatenate([blocks + (1 - core), blocks + core])
    hids, das, dbs = ([own_grads[i], near_grads[i]] for i in range(3))
    partial = weight_grads("partial", both, CORES * n_group, [own, near], hids, das, dbs)
    got_far, partial, dx = lax.optimization_barrier((got_far, partial, dx))
    last = flat(got_far)
    far_grads = hidden_of("far", last)
    hids, das, dbs = ([a] for a in far_grads[:3])
    theirs = weight_grads("theirs", blocks + (1 - core), n_group, [last], hids, das, dbs, [(partial, 0)])
    added = lax.ppermute(theirs, "expert", other_core)
    back = exchange(dx_of("far", far_grads, 3, dx))

    landed = [None] * n_group
    for i, r in enumerate(order):
        add = [(partial, n_group + i), (added, i)]
        block = weight_grads(f"mine_{r}", blocks[i : i + 1] + core, 1, [last], hids, das, dbs, add)
        landed[r] = across(block, r) if r else block

    parts = combine(plane, back, [packed] + from_near + from_far, topk, capacity, stride)
    home = [parts[0]] + [across(a, n_group - r) for a, r in zip(parts[1:], shifts)]
    grad_tokens, grad_probs = finish(route_probs, home, width)

    def source(owner, j):
        return (p - (local_exp * owner + j)) % n_group

    index = jnp.stack([source(1 - core, j) for j in range(local_exp)]).astype(jnp.int32)
    other = lax.ppermute(pick(index, landed, local_exp), "expert", other_core)
    where = jnp.stack([core, p] + [source(core, j) for j in range(local_exp)]).astype(jnp.int32)
    new = update(where, decay_mask, landed, other, (w_gate, w_up, w_down), shard_rows)
    return (grad_tokens, grad_probs, *new)


def solution(mesh):
    placed = (
        P(("dp", "expert"), None),
        P(("dp", "expert"), None),
        P(("dp", "expert"), None),
        P(("dp", "expert"), None),
        P("expert", None, None),
        P("expert", None, None),
        P("expert", None, None),
        P("expert", None),
    )
    return jax.shard_map(
        body,
        mesh=mesh,
        in_specs=placed,
        out_specs=(
            P(("dp", "expert"), None),
            P(("dp", "expert"), None),
            P("expert", "dp", None),
            P("expert", "dp", None),
            P("expert", "dp", None),
        ),
        check_vma=False,
    )
```

```python
import functools

import jax
import jax.numpy as jnp
from jax import lax
from jax.experimental import pallas as pl
from jax.experimental.pallas import tpu as pltpu
from jax.sharding import PartitionSpec as P

step_size = 0.004
shrink_rate = 0.1
LANES = 128
F32 = jnp.float32
BF16 = jnp.bfloat16
VMEM_LIMIT = 60 * 1024 * 1024


def dot(a, b, dims):
    return lax.dot_general(a, b, (dims, ((), ())), preferred_element_type=F32)


def cost(flops, moved):
    return pl.CostEstimate(flops=flops, transcendentals=0, bytes_accessed=moved)


NN = ((1,), (0,))
NT = ((1,), (1,))
TN = ((0,), (0,))


def slot_values(ids_t, n_experts, capacity):
    topk, tok = ids_t.shape
    rows = lax.broadcasted_iota(jnp.int32, (n_experts, tok), 0)
    hit = ids_t[0:1, :] == rows
    for k in range(1, topk):
        hit = jnp.logical_or(hit, ids_t[k : k + 1, :] == rows)
    hit_f = jnp.where(hit, 1.0, 0.0)
    earlier = lax.broadcasted_iota(jnp.int32, (tok, tok), 0) < lax.broadcasted_iota(
        jnp.int32, (tok, tok), 1
    )
    count = dot(hit_f.astype(BF16), jnp.where(earlier, 1.0, 0.0).astype(BF16), NN)
    return jnp.where(jnp.logical_and(hit, count < capacity), count, -1.0)


def slot_rows(values, chunk, local_exp, capacity):
    n_experts, tok = values.shape
    n_rows = n_experts // local_exp * capacity
    expert_of = lax.broadcasted_iota(jnp.int32, (n_rows, n_experts), 0) // capacity * local_exp + chunk
    spread = jnp.where(expert_of == lax.broadcasted_iota(jnp.int32, (n_rows, n_experts), 1), 1.0, 0.0)
    spread = spread.astype(BF16)
    at = dot(spread, values.astype(BF16), NN)
    place = (lax.broadcasted_iota(jnp.int32, (n_rows, tok), 0) % capacity).astype(F32)
    return at == place, spread


def dispatch_kernel(chunk, local_exp, capacity, ids_ref, probs_ref, tok_ref, grad_ref, out_ref):
    ids_t = ids_ref[...]
    topk, tok = ids_t.shape
    n_experts = out_ref.shape[0] // capacity * local_exp
    width = tok_ref.shape[1]
    values = slot_values(ids_t, n_experts, capacity)
    rows = lax.broadcasted_iota(jnp.int32, (n_experts, tok), 0)
    prob = jnp.zeros((n_experts, tok), F32)
    for k in range(topk):
        prob = prob + jnp.where(ids_t[k : k + 1, :] == rows, probs_ref[k : k + 1, :].astype(F32), 0.0)
    onehot, spread = slot_rows(values, chunk, local_exp, capacity)
    prob_rows = dot(spread, prob.astype(BF16), NN)
    pick = jnp.where(onehot, 1.0, 0.0).astype(BF16)
    weighted = jnp.where(onehot, prob_rows, 0.0).astype(BF16)
    out_ref[:, :width] = dot(pick, tok_ref[...], NN).astype(BF16)
    out_ref[:, width:] = dot(weighted, grad_ref[...], NN).astype(BF16)


def dispatch(chunk, local_exp, capacity, n_experts, ids_t, probs_t, tokens, out_grad):
    tok, width = tokens.shape
    n_rows = n_experts // local_exp * capacity
    return pl.pallas_call(
        functools.partial(dispatch_kernel, chunk, local_exp, capacity),
        out_shape=jax.ShapeDtypeStruct((n_rows, 2 * width), BF16),
        compiler_params=pltpu.CompilerParams(vmem_limit_bytes=VMEM_LIMIT),
        cost_estimate=cost(4 * n_rows * tok * width, 4 * width * (tok + n_rows)),
        name=f"dispatch{chunk}",
    )(ids_t, probs_t, tokens, out_grad)


def hidden_kernel(x_ref, do_ref, wg_ref, wu_ref, wd_ref, hid_ref, da_ref, db_ref, s_ref, sum_ref):
    step = pl.program_id(0)
    gate = dot(x_ref[...], wg_ref[0], NN)
    upper = dot(x_ref[...], wu_ref[0], NN)
    sig = jax.nn.sigmoid(gate)
    act = gate * sig
    hid = (act * upper).astype(BF16)
    hid_ref[...] = hid
    dhid = dot(do_ref[...], wd_ref[0], NN)
    part = jnp.sum(hid.astype(F32) * dhid, axis=1, keepdims=True)
    da_ref[...] = (dhid * upper * sig * (1.0 + gate * (1.0 - sig))).astype(BF16)
    db_ref[...] = (dhid * act).astype(BF16)

    @pl.when(step == 0)
    def _():
        sum_ref[...] = jnp.broadcast_to(part, sum_ref.shape)

    @pl.when(step > 0)
    def _():
        sum_ref[...] = sum_ref[...] + part

    @pl.when(step == pl.num_programs(0) - 1)
    def _():
        total = sum_ref[...]
        high = total.astype(BF16).astype(F32)
        lane = lax.broadcasted_iota(jnp.int32, s_ref.shape, 1)
        s_ref[...] = jnp.where(lane == 0, high, jnp.where(lane == 1, total - high, 0.0)).astype(BF16)


def whole(shape):
    return pl.BlockSpec(shape, lambda *_: (0,) * len(shape), pipeline_mode=pl.Buffered(1))


def hidden_grads(chunk, rows, wg, wu, wd):
    n_rows, width = rows.shape[0], rows.shape[1] // 2
    hidden = wg.shape[2]
    block = 2 * LANES
    weight = pl.BlockSpec((1, width, block), lambda i: (chunk, 0, i))
    result = pl.BlockSpec((n_rows, block), lambda i: (0, i))
    return pl.pallas_call(
        hidden_kernel,
        grid=(hidden // block,),
        in_specs=[
            pl.BlockSpec((n_rows, width), lambda i: (0, 0), pipeline_mode=pl.Buffered(1)),
            pl.BlockSpec((n_rows, width), lambda i: (0, 1), pipeline_mode=pl.Buffered(1)),
            weight,
            weight,
            weight,
        ],
        out_specs=[result] * 3 + [whole((n_rows, LANES))],
        out_shape=[jax.ShapeDtypeStruct((n_rows, hidden), BF16)] * 3
        + [jax.ShapeDtypeStruct((n_rows, LANES), BF16)],
        scratch_shapes=[pltpu.VMEM((n_rows, LANES), F32)],
        compiler_params=pltpu.CompilerParams(vmem_limit_bytes=VMEM_LIMIT),
        cost_estimate=cost(6 * n_rows * width * hidden, 6 * width * hidden + n_rows * (4 * width + 6 * hidden)),
        name=f"hidden{chunk}",
    )(rows, rows, wg, wu, wd)


def weight_kernel(n_add, where_ref, x_ref, do_ref, hid_ref, da_ref, db_ref, *refs):
    adds, outs = refs[:n_add], refs[n_add:]
    hidden = hid_ref.shape[1]
    for m, (left, right) in enumerate(((x_ref, da_ref), (x_ref, db_ref), (do_ref, hid_ref))):
        part = dot(left[...], right[...], TN)
        lanes = slice(m * hidden, (m + 1) * hidden)
        for addend in adds:
            part = part + addend[:, lanes].astype(F32)
        for i, out_ref in enumerate(outs):

            @pl.when(pl.program_id(0) == i)
            def _():
                out_ref[:, lanes] = part.astype(BF16)


def weight_grads(name, where, count, half, rows, hid, da, db, *adds):
    n_rows, width = rows.shape[0], rows.shape[1] // 2
    hidden = hid.shape[1]
    lefts = width // half
    shape = (half, 3 * hidden)
    return pl.pallas_call(
        functools.partial(weight_kernel, len(adds)),
        grid_spec=pltpu.PrefetchScalarGridSpec(
            num_scalar_prefetch=1,
            grid=(count,),
            in_specs=[
                pl.BlockSpec((n_rows, half), lambda i, at: (0, at[i])),
                pl.BlockSpec((n_rows, half), lambda i, at: (0, at[i] + lefts)),
            ]
            + [whole(a.shape) for a in (hid, da, db, *adds)],
            out_specs=[whole(shape)] * count,
        ),
        out_shape=[jax.ShapeDtypeStruct(shape, BF16)] * count,
        compiler_params=pltpu.CompilerParams(vmem_limit_bytes=VMEM_LIMIT),
        cost_estimate=cost(6 * count * n_rows * half * hidden, 6 * n_rows * hidden + 6 * count * half * hidden),
        name=name,
    )(where, rows, rows, hid, da, db, *adds)


def update_kernel(chunk, where_ref, mask_ref, *refs):
    grads, weights = refs[:6], refs[6:9]
    outs = refs[-3:]
    hidden = weights[0].shape[2]
    for half in range(2):

        @pl.when(pl.program_id(0) == half)
        def _():
            for m in range(3):
                lanes = slice(m * hidden, (m + 1) * hidden)
                grad = sum(g[:, lanes].astype(F32) for g in grads[3 * half : 3 * half + 3])
                weight = weights[m][0].astype(F32)
                rate = mask_ref[chunk, m].astype(F32)
                outs[m][0] = (weight - step_size * grad - shrink_rate * rate * weight).astype(BF16)


def update(chunk, where, mask, grads, weights, into):
    half, lanes = grads[0].shape
    local, _, hidden = weights[0].shape
    grad = pl.BlockSpec((half, lanes), lambda h, w: (0, 0), pipeline_mode=pl.Buffered(1))
    weight = pl.BlockSpec((1, half, hidden), lambda h, w: (chunk, 2 * w[0] + h, 0))
    result = pl.BlockSpec((1, half, hidden), lambda h, w: (chunk, h, 0))
    extra = list(into or [])
    return pl.pallas_call(
        functools.partial(update_kernel, chunk),
        grid_spec=pltpu.PrefetchScalarGridSpec(
            num_scalar_prefetch=1,
            grid=(2,),
            in_specs=[pl.BlockSpec(memory_space=pltpu.SMEM)]
            + [grad] * 6
            + [weight] * 3
            + [pl.BlockSpec(memory_space=pl.ANY)] * len(extra),
            out_specs=[result] * 3,
        ),
        out_shape=[jax.ShapeDtypeStruct((local, 2 * half, hidden), BF16)] * 3,
        input_output_aliases={11 + i: i for i in range(len(extra))},
        compiler_params=pltpu.CompilerParams(vmem_limit_bytes=VMEM_LIMIT),
        cost_estimate=cost(10 * half * lanes, 20 * half * lanes),
        name=f"update{chunk}",
    )(where, mask, *grads, *weights, *extra)


def dx_kernel(da_ref, db_ref, s_ref, wg_ref, wu_ref, out_ref):
    width = wg_ref.shape[1]
    out_ref[:, :width] = (dot(da_ref[...], wg_ref[0], NT) + dot(db_ref[...], wu_ref[0], NT)).astype(BF16)
    out_ref[:, width:] = s_ref[...]


def input_grads(chunk, da, db, s, wg, wu):
    n_rows, hidden = da.shape
    width = wg.shape[1]
    weight = pl.BlockSpec((1, width, hidden), lambda i: (chunk, 0, 0), pipeline_mode=pl.Buffered(1))

    def whole(shape):
        return pl.BlockSpec(shape, lambda i: (0, 0), pipeline_mode=pl.Buffered(1))

    return pl.pallas_call(
        dx_kernel,
        grid=(1,),
        in_specs=[whole((n_rows, hidden)), whole((n_rows, hidden)), whole((n_rows, LANES)), weight, weight],
        out_specs=whole((n_rows, width + LANES)),
        out_shape=jax.ShapeDtypeStruct((n_rows, width + LANES), BF16),
        compiler_params=pltpu.CompilerParams(vmem_limit_bytes=VMEM_LIMIT),
        cost_estimate=cost(4 * n_rows * width * hidden, 4 * width * hidden + 2 * n_rows * (width + 2 * hidden)),
        name=f"dx{chunk}",
    )(da, db, s, wg, wu)


def combine_kernel(local_exp, capacity, ids_ref, *refs):
    ids_t = ids_ref[...]
    back = refs[:local_exp]
    tok_ref, prob_ref = refs[local_exp:]
    topk, tok = ids_t.shape
    n_experts = back[0].shape[0] // capacity * local_exp
    width = tok_ref.shape[1]
    values = slot_values(ids_t, n_experts, capacity)
    total = jnp.zeros((tok, width), F32)
    by_expert = jnp.zeros((n_experts, tok), F32)
    for chunk in range(local_exp):
        onehot, spread = slot_rows(values, chunk, local_exp, capacity)
        pick = jnp.where(onehot, 1.0, 0.0)
        total = total + dot(pick.astype(BF16), back[chunk][:, :width], TN)
        s = back[chunk][:, width:].astype(F32)
        s = s[:, 0:1] + s[:, 1:2]
        placed = pick * s
        high = placed.astype(BF16)
        low = (placed - high.astype(F32)).astype(BF16)
        by_expert = by_expert + dot(spread, high, TN) + dot(spread, low, TN)
    tok_ref[...] = total.astype(BF16)
    rows = lax.broadcasted_iota(jnp.int32, (n_experts, tok), 0)
    for k in range(topk):
        mine = jnp.where(ids_t[k : k + 1, :] == rows, by_expert, 0.0)
        prob_ref[k : k + 1, :] = jnp.sum(mine, axis=0, keepdims=True)


def combine(local_exp, capacity, ids_t, backs, width):
    topk, tok = ids_t.shape
    n_rows = local_exp * backs[0].shape[0]
    return pl.pallas_call(
        functools.partial(combine_kernel, local_exp, capacity),
        out_shape=[
            jax.ShapeDtypeStruct((tok, width), BF16),
            jax.ShapeDtypeStruct((topk, tok), F32),
        ],
        compiler_params=pltpu.CompilerParams(vmem_limit_bytes=VMEM_LIMIT),
        cost_estimate=cost(2 * n_rows * tok * width, 2 * width * (n_rows + tok)),
        name="combine",
    )(ids_t, *backs)


def body(tokens, out_grad, expert_ids, route_probs, w_gate, w_up, w_down, decay_mask):
    n_owner = lax.axis_size("expert")
    n_group = lax.axis_size("dp")
    local_exp = w_gate.shape[0]
    width = tokens.shape[1]
    tok_rows, topk = expert_ids.shape
    n_experts = n_owner * local_exp
    capacity = tok_rows * topk // n_experts
    ids_t = expert_ids.T
    probs_t = route_probs.T
    half = width // n_group // 2
    plane = lax.axis_index("dp").astype(jnp.int32)
    where = plane.reshape(1)

    def half_shard(ahead, second):
        return 2 * ((plane + ahead) % n_group) + second

    def blocks(*pairs):
        return jnp.stack([half_shard(*pair) for pair in pairs]).astype(jnp.int32)

    def up(a):
        return lax.ppermute(a, "dp", [(i, (i + 1) % n_group) for i in range(n_group)])

    def down(a):
        return lax.ppermute(a, "dp", [(i, (i - 1) % n_group) for i in range(n_group)])

    got = []
    for chunk in range(local_exp):
        rows = dispatch(chunk, local_exp, capacity, n_experts, ids_t, probs_t, tokens, out_grad)
        if got:
            rows, got[-1] = lax.optimization_barrier((rows, got[-1]))
        rows = rows.reshape(n_owner, capacity, 2 * width)
        got.append(lax.all_to_all(rows, "expert", split_axis=0, concat_axis=0, tiled=True))
    def swap(a):
        a = a.reshape(n_owner, capacity, width + LANES)
        back = lax.all_to_all(a, "expert", split_axis=0, concat_axis=0, tiled=True)
        return back.reshape(n_owner * capacity, width + LANES)

    weights = (w_gate, w_up, w_down)
    near_pairs = ((1, 1), (n_group - 1, 0), (0, 0), (0, 1))
    new, backs, sent = None, [], None
    for chunk in range(local_exp):
        rows = got[chunk].reshape(n_owner * capacity, 2 * width)
        if sent:
            rows, near_up, near_down, dx = lax.optimization_barrier((rows, near_up, near_down, dx))
            backs.append(swap(dx))
        hid, da, db, s = hidden_grads(chunk, rows, *weights)
        first = weight_grads(f"first{chunk}", blocks((2, 0), (2, 1)), 2, half, rows, hid, da, db)
        far_up, far_down = up(first[0]), down(first[1])
        if sent:
            dx = input_grads(chunk, da, db, s, w_gate, w_up)
            rows, _, dx, *sent = lax.optimization_barrier((rows, first[0], dx, *sent))
            grads = (second[2], sent[0], near_down, second[3], near_up, sent[1])
            new = update(chunk - 1, where, decay_mask, grads, weights, new)
        second = weight_grads(f"second{chunk}", blocks(*near_pairs), 4, half, rows, hid, da, db)
        near_up, near_down = up(second[0]), down(second[1])
        far_up, far_down, _ = lax.optimization_barrier((far_up, far_down, second[0]))
        sum_up = weight_grads(f"up{chunk}", blocks((1, 0)), 1, half, rows, hid, da, db, far_up)[0]
        sum_down = weight_grads(f"down{chunk}", blocks((n_group - 1, 1)), 1, half, rows, hid, da, db, far_down)[0]
        sent = [up(sum_up), down(sum_down)]
        if chunk == 0:
            da, got[1], _, _ = lax.optimization_barrier((da, got[1], sum_up, sum_down))
            dx = input_grads(chunk, da, db, s, w_gate, w_up)
    backs.append(swap(dx))
    *backs, near_up, near_down = lax.optimization_barrier((*backs, near_up, near_down))
    grads = (second[2], sent[0], near_down, second[3], near_up, sent[1])
    new = update(local_exp - 1, where, decay_mask, grads, weights, new)
    grad_tokens, scores = combine(local_exp, capacity, ids_t, backs, width)
    grad_probs = (scores / probs_t.astype(F32)).astype(BF16).T

    return (grad_tokens, grad_probs, *new)


def solution(mesh):
    placed = (
        P(("dp", "expert"), None),
        P(("dp", "expert"), None),
        P(("dp", "expert"), None),
        P(("dp", "expert"), None),
        P("expert", None, None),
        P("expert", None, None),
        P("expert", None, None),
        P("expert", None),
    )
    return jax.shard_map(
        body,
        mesh=mesh,
        in_specs=placed,
        out_specs=(
            P(("dp", "expert"), None),
            P(("dp", "expert"), None),
            P("expert", "dp", None),
            P("expert", "dp", None),
            P("expert", "dp", None),
        ),
        check_vma=False,
    )
```

```python
import functools

import jax
import jax.numpy as jnp
from jax import lax
from jax.experimental import pallas as pl
from jax.experimental.pallas import tpu as pltpu
from jax.sharding import PartitionSpec as P

step_size = 0.004
shrink_rate = 0.1
LANES = 128
F32 = jnp.float32
BF16 = jnp.bfloat16
VMEM_LIMIT = 60 * 1024 * 1024


def dot(a, b, dims):
    return lax.dot_general(a, b, (dims, ((), ())), preferred_element_type=F32)


def cost(flops, moved, chunk=1):
    scale = (10, 18)[min(chunk, 1)]
    return pl.CostEstimate(flops=scale * flops, transcendentals=0, bytes_accessed=scale * moved)


NN = ((1,), (0,))
NT = ((1,), (1,))
TN = ((0,), (0,))


def slot_values(ids_t, n_experts, capacity):
    topk, tok = ids_t.shape
    rows = lax.broadcasted_iota(jnp.int32, (n_experts, tok), 0)
    hit = ids_t[0:1, :] == rows
    for k in range(1, topk):
        hit = jnp.logical_or(hit, ids_t[k : k + 1, :] == rows)
    hit_f = jnp.where(hit, 1.0, 0.0)
    earlier = lax.broadcasted_iota(jnp.int32, (tok, tok), 0) < lax.broadcasted_iota(
        jnp.int32, (tok, tok), 1
    )
    count = dot(hit_f.astype(BF16), jnp.where(earlier, 1.0, 0.0).astype(BF16), NN)
    return jnp.where(jnp.logical_and(hit, count < capacity), count, -1.0)


def slot_rows(values, chunk, local_exp, capacity):
    n_experts, tok = values.shape
    n_rows = n_experts // local_exp * capacity
    expert_of = lax.broadcasted_iota(jnp.int32, (n_rows, n_experts), 0) // capacity * local_exp + chunk
    spread = jnp.where(expert_of == lax.broadcasted_iota(jnp.int32, (n_rows, n_experts), 1), 1.0, 0.0)
    spread = spread.astype(BF16)
    at = dot(spread, values.astype(BF16), NN)
    place = (lax.broadcasted_iota(jnp.int32, (n_rows, tok), 0) % capacity).astype(F32)
    return at == place, spread


def dispatch_kernel(chunk, local_exp, capacity, ids_ref, probs_ref, tok_ref, grad_ref, out_ref):
    ids_t = ids_ref[...]
    topk, tok = ids_t.shape
    n_experts = out_ref.shape[0] // capacity * local_exp
    width = tok_ref.shape[1]
    values = slot_values(ids_t, n_experts, capacity)
    rows = lax.broadcasted_iota(jnp.int32, (n_experts, tok), 0)
    prob = jnp.zeros((n_experts, tok), F32)
    for k in range(topk):
        prob = prob + jnp.where(ids_t[k : k + 1, :] == rows, probs_ref[k : k + 1, :].astype(F32), 0.0)
    onehot, spread = slot_rows(values, chunk, local_exp, capacity)
    prob_rows = dot(spread, prob.astype(BF16), NN)
    pick = jnp.where(onehot, 1.0, 0.0).astype(BF16)
    weighted = jnp.where(onehot, prob_rows, 0.0).astype(BF16)
    out_ref[:, :width] = dot(pick, tok_ref[...], NN).astype(BF16)
    out_ref[:, width:] = dot(weighted, grad_ref[...], NN).astype(BF16)


def dispatch(chunk, local_exp, capacity, n_experts, ids_t, probs_t, tokens, out_grad):
    tok, width = tokens.shape
    n_rows = n_experts // local_exp * capacity
    return pl.pallas_call(
        functools.partial(dispatch_kernel, chunk, local_exp, capacity),
        out_shape=jax.ShapeDtypeStruct((n_rows, 2 * width), BF16),
        compiler_params=pltpu.CompilerParams(vmem_limit_bytes=VMEM_LIMIT),
        cost_estimate=cost(4 * n_rows * tok * width, 4 * width * (tok + n_rows), 0),
        name=f"dispatch{chunk}",
    )(ids_t, probs_t, tokens, out_grad)


def hidden_kernel(
    where_ref, x_ref, do_ref, xa_ref, xb_ref, da_col_ref, db_col_ref, wg_ref, wu_ref, wd_ref,
    hid_ref, da_ref, db_ref, s_ref, a_ref, b_ref, sum_ref,
):
    step = pl.program_id(0)
    gate = dot(x_ref[...], wg_ref[0], NN)
    upper = dot(x_ref[...], wu_ref[0], NN)
    sig = jax.nn.sigmoid(gate)
    act = gate * sig
    hid = (act * upper).astype(BF16)
    hid_ref[...] = hid
    dhid = dot(do_ref[...], wd_ref[0], NN)
    part = jnp.sum(hid.astype(F32) * dhid, axis=1, keepdims=True)
    dgate = (dhid * upper * sig * (1.0 + gate * (1.0 - sig))).astype(BF16)
    dup = (dhid * act).astype(BF16)
    da_ref[...] = dgate
    db_ref[...] = dup
    for out_ref, x_col, do_col in ((a_ref, xa_ref, da_col_ref), (b_ref, xb_ref, db_col_ref)):
        out_ref[0] = dot(x_col[...], dgate, TN).astype(BF16)
        out_ref[1] = dot(x_col[...], dup, TN).astype(BF16)
        out_ref[2] = dot(do_col[...], hid, TN).astype(BF16)

    @pl.when(step == 0)
    def _():
        sum_ref[...] = jnp.broadcast_to(part, sum_ref.shape)

    @pl.when(step > 0)
    def _():
        sum_ref[...] = sum_ref[...] + part

    @pl.when(step == pl.num_programs(0) - 1)
    def _():
        total = sum_ref[...]
        high = total.astype(BF16).astype(F32)
        lane = lax.broadcasted_iota(jnp.int32, s_ref.shape, 1)
        s_ref[...] = jnp.where(lane == 0, high, jnp.where(lane == 1, total - high, 0.0)).astype(BF16)


def whole(shape):
    return pl.BlockSpec(shape, lambda *_: (0,) * len(shape), pipeline_mode=pl.Buffered(1))


def hidden_grads(chunk, where, half, rows, wg, wu, wd):
    n_rows, width = rows.shape[0], rows.shape[1] // 2
    hidden = wg.shape[2]
    block = 2 * LANES
    lefts = width // half
    once = pl.Buffered(1)
    weight = pl.BlockSpec((1, width, block), lambda i, at: (chunk, 0, i))
    result = pl.BlockSpec((n_rows, block), lambda i, at: (0, i))
    shard = pl.BlockSpec((3, half, block), lambda i, at: (0, 0, i))
    return pl.pallas_call(
        hidden_kernel,
        grid_spec=pltpu.PrefetchScalarGridSpec(
            num_scalar_prefetch=1,
            grid=(hidden // block,),
            in_specs=[
                pl.BlockSpec((n_rows, width), lambda i, at: (0, 0), pipeline_mode=once),
                pl.BlockSpec((n_rows, width), lambda i, at: (0, 1), pipeline_mode=once),
                pl.BlockSpec((n_rows, half), lambda i, at: (0, at[0]), pipeline_mode=once),
                pl.BlockSpec((n_rows, half), lambda i, at: (0, at[1]), pipeline_mode=once),
                pl.BlockSpec((n_rows, half), lambda i, at: (0, at[0] + lefts), pipeline_mode=once),
                pl.BlockSpec((n_rows, half), lambda i, at: (0, at[1] + lefts), pipeline_mode=once),
                weight,
                weight,
                weight,
            ],
            out_specs=[result] * 3 + [whole((n_rows, LANES)), shard, shard],
            scratch_shapes=[pltpu.VMEM((n_rows, LANES), F32)],
        ),
        out_shape=[jax.ShapeDtypeStruct((n_rows, hidden), BF16)] * 3
        + [jax.ShapeDtypeStruct((n_rows, LANES), BF16)]
        + [jax.ShapeDtypeStruct((3, half, hidden), BF16)] * 2,
        compiler_params=pltpu.CompilerParams(vmem_limit_bytes=VMEM_LIMIT),
        cost_estimate=cost(8 * n_rows * width * hidden, 6 * width * hidden + n_rows * (4 * width + 6 * hidden), chunk),
        name=f"hidden{chunk}",
    )(where, *[rows] * 6, wg, wu, wd)


def weight_kernel(n_add, where_ref, x_ref, do_ref, hid_ref, da_ref, db_ref, *refs):
    adds, outs = refs[:n_add], refs[n_add:]
    for m, (left, right) in enumerate(((x_ref, da_ref), (x_ref, db_ref), (do_ref, hid_ref))):
        part = dot(left[...], right[...], TN)
        for addend in adds:
            part = part + addend[m].astype(F32)
        for i, out_ref in enumerate(outs):

            @pl.when(pl.program_id(0) == i)
            def _():
                out_ref[m] = part.astype(BF16)


def weight_grads(name, chunk, where, count, half, rows, hid, da, db, *adds):
    n_rows, width = rows.shape[0], rows.shape[1] // 2
    hidden = hid.shape[1]
    lefts = width // half
    shape = (3, half, hidden)
    return pl.pallas_call(
        functools.partial(weight_kernel, len(adds)),
        grid_spec=pltpu.PrefetchScalarGridSpec(
            num_scalar_prefetch=1,
            grid=(count,),
            in_specs=[
                pl.BlockSpec((n_rows, half), lambda i, at: (0, at[i])),
                pl.BlockSpec((n_rows, half), lambda i, at: (0, at[i] + lefts)),
            ]
            + [whole(a.shape) for a in (hid, da, db, *adds)],
            out_specs=[whole(shape)] * count,
        ),
        out_shape=[jax.ShapeDtypeStruct(shape, BF16)] * count,
        compiler_params=pltpu.CompilerParams(vmem_limit_bytes=VMEM_LIMIT),
        cost_estimate=cost(6 * count * n_rows * half * hidden, 6 * n_rows * hidden + 6 * count * half * hidden, chunk),
        name=name,
    )(where, rows, rows, hid, da, db, *adds)


def update_kernel(chunk, where_ref, mask_ref, *refs):
    grads, weights = refs[:6], refs[6:9]
    outs = refs[-3:]
    for second in range(2):

        @pl.when(pl.program_id(0) == second)
        def _():
            for m in range(3):
                grad = sum(g[m].astype(F32) for g in grads[3 * second : 3 * second + 3])
                weight = weights[m][0].astype(F32)
                rate = mask_ref[chunk, m].astype(F32)
                outs[m][0] = (weight - step_size * grad - shrink_rate * rate * weight).astype(BF16)


def update(chunk, where, mask, grads, weights, into):
    _, half, hidden = grads[0].shape
    local = weights[0].shape[0]
    steps = 4
    block = half // steps
    early = pl.BlockSpec((3, block, hidden), lambda h, r, w: (0, r * (1 - h) + (steps - 1) * h, 0))
    late = pl.BlockSpec((3, block, hidden), lambda h, r, w: (0, r * h, 0))
    weight = pl.BlockSpec((1, block, hidden), lambda h, r, w: (chunk, (2 * w[0] + h) * steps + r, 0))
    result = pl.BlockSpec((1, block, hidden), lambda h, r, w: (chunk, h * steps + r, 0))
    extra = list(into or [])
    return pl.pallas_call(
        functools.partial(update_kernel, chunk),
        grid_spec=pltpu.PrefetchScalarGridSpec(
            num_scalar_prefetch=1,
            grid=(2, steps),
            in_specs=[pl.BlockSpec(memory_space=pltpu.SMEM)]
            + [early] * 3
            + [late] * 3
            + [weight] * 3
            + [pl.BlockSpec(memory_space=pl.ANY)] * len(extra),
            out_specs=[result] * 3,
        ),
        out_shape=[jax.ShapeDtypeStruct((local, 2 * half, hidden), BF16)] * 3,
        input_output_aliases={11 + i: i for i in range(len(extra))},
        compiler_params=pltpu.CompilerParams(vmem_limit_bytes=VMEM_LIMIT),
        cost_estimate=cost(10 * half * hidden, 60 * half * hidden),
        name=f"update{chunk}",
    )(where, mask, *grads, *weights, *extra)


def dx_kernel(da_ref, db_ref, s_ref, wg_ref, wu_ref, *refs):
    out_ref = refs[-1]
    n_owner, capacity, lanes = out_ref.shape
    width = wg_ref.shape[1]
    dx = (dot(da_ref[...], wg_ref[0], NT) + dot(db_ref[...], wu_ref[0], NT)).astype(BF16)
    out_ref[:, :, :width] = dx.reshape(n_owner, capacity, width)
    out_ref[:, :, width:] = s_ref[...].reshape(n_owner, capacity, lanes - width)


def input_grads(chunk, local_exp, capacity, da, db, s, wg, wu, into):
    n_rows, hidden = da.shape
    width = wg.shape[1]
    n_owner = n_rows // capacity
    weight = pl.BlockSpec((1, width, hidden), lambda i: (chunk, 0, 0), pipeline_mode=pl.Buffered(1))
    extra = [] if into is None else [into]
    return pl.pallas_call(
        dx_kernel,
        grid=(1,),
        in_specs=[whole((n_rows, hidden)), whole((n_rows, hidden)), whole((n_rows, LANES)), weight, weight]
        + [pl.BlockSpec(memory_space=pl.ANY)] * len(extra),
        out_specs=pl.BlockSpec(
            (n_owner, capacity, width + LANES), lambda i: (0, chunk, 0), pipeline_mode=pl.Buffered(1)
        ),
        out_shape=jax.ShapeDtypeStruct((n_owner, local_exp * capacity, width + LANES), BF16),
        input_output_aliases={5: 0} if extra else {},
        compiler_params=pltpu.CompilerParams(vmem_limit_bytes=VMEM_LIMIT),
        cost_estimate=cost(4 * n_rows * width * hidden, 4 * width * hidden + 2 * n_rows * (width + 2 * hidden), chunk),
        name=f"dx{chunk}",
    )(da, db, s, wg, wu, *extra)


def combine_kernel(local_exp, capacity, ids_ref, back_ref, tok_ref, prob_ref):
    ids_t = ids_ref[...]
    topk, tok = ids_t.shape
    n_rows = back_ref.shape[0] * capacity
    n_experts = back_ref.shape[0] * local_exp
    width = tok_ref.shape[1]
    values = slot_values(ids_t, n_experts, capacity)
    total = jnp.zeros((tok, width), F32)
    by_expert = jnp.zeros((n_experts, tok), F32)
    for chunk in range(local_exp):
        onehot, spread = slot_rows(values, chunk, local_exp, capacity)
        pick = jnp.where(onehot, 1.0, 0.0)
        slots = slice(chunk * capacity, (chunk + 1) * capacity)
        dx = back_ref[:, slots, :width].reshape(n_rows, width)
        total = total + dot(pick.astype(BF16), dx, TN)
        s = back_ref[:, slots, width:].reshape(n_rows, LANES).astype(F32)
        placed = pick * (s[:, 0:1] + s[:, 1:2])
        high = placed.astype(BF16)
        low = (placed - high.astype(F32)).astype(BF16)
        by_expert = by_expert + dot(spread, high, TN) + dot(spread, low, TN)
    tok_ref[...] = total.astype(BF16)
    rows = lax.broadcasted_iota(jnp.int32, (n_experts, tok), 0)
    for k in range(topk):
        mine = jnp.where(ids_t[k : k + 1, :] == rows, by_expert, 0.0)
        prob_ref[k : k + 1, :] = jnp.sum(mine, axis=0, keepdims=True)


def combine(local_exp, capacity, ids_t, back, width):
    topk, tok = ids_t.shape
    return pl.pallas_call(
        functools.partial(combine_kernel, local_exp, capacity),
        out_shape=[
            jax.ShapeDtypeStruct((tok, width), BF16),
            jax.ShapeDtypeStruct((topk, tok), F32),
        ],
        compiler_params=pltpu.CompilerParams(vmem_limit_bytes=VMEM_LIMIT),
        cost_estimate=cost(2 * back.shape[0] * back.shape[1] * tok * width, 2 * back.size),
        name="combine",
    )(ids_t, back)


def body(tokens, out_grad, expert_ids, route_probs, w_gate, w_up, w_down, decay_mask):
    n_owner = lax.axis_size("expert")
    n_group = lax.axis_size("dp")
    local_exp = w_gate.shape[0]
    width = tokens.shape[1]
    tok_rows, topk = expert_ids.shape
    n_experts = n_owner * local_exp
    capacity = tok_rows * topk // n_experts
    ids_t = expert_ids.T
    probs_t = route_probs.T
    half = width // n_group // 2
    plane = lax.axis_index("dp").astype(jnp.int32)
    where = plane.reshape(1)

    def half_shard(ahead, second):
        return 2 * ((plane + ahead) % n_group) + second

    def blocks(*pairs):
        return jnp.stack([half_shard(*pair) for pair in pairs]).astype(jnp.int32)

    def up(a):
        return lax.ppermute(a, "dp", [(i, (i + 1) % n_group) for i in range(n_group)])

    def down(a):
        return lax.ppermute(a, "dp", [(i, (i - 1) % n_group) for i in range(n_group)])

    def send(chunk):
        return dispatch(chunk, local_exp, capacity, n_experts, ids_t, probs_t, tokens, out_grad)

    def swap(a):
        return lax.all_to_all(a, "expert", split_axis=0, concat_axis=0, tiled=True)

    def swap_rows(a):
        a = a.reshape(n_owner, capacity, a.shape[1])
        return swap(a).reshape(n_owner * capacity, a.shape[2])

    def order(value, *after):
        return lax.optimization_barrier((value, *after))[0]

    weights = (w_gate, w_up, w_down)
    far_pairs = ((2, 0), (2, 1))
    near_pairs = ((1, 1), (n_group - 1, 0))
    own_pairs = ((0, 0), (0, 1))
    new, dx, before = None, None, None
    sends = [send(chunk) for chunk in range(local_exp)]
    rows = order(swap_rows(sends[0]), *sends[1:])
    for chunk in range(local_exp):
        hid, da, db, s, *far = hidden_grads(chunk, blocks(*far_pairs), half, rows, *weights)
        far_up, far_down = up(far[0]), down(far[1])
        grads = (rows, hid, da, db)
        if before:
            rows, _, *last = lax.optimization_barrier((rows, far[0], *before[1]))
            own, (near_up, near_down) = before[0], before[2]
            new = update(chunk - 1, where, decay_mask, (own[0], last[0], near_down, own[1], near_up, last[1]), weights, new)
            grads = (rows, hid, da, db)
        near = weight_grads(f"near{chunk}", chunk, blocks(*near_pairs), 2, half, *grads)
        near_up, near_down = up(near[0]), down(near[1])
        if chunk + 1 < local_exp:
            following = swap_rows(order(sends[chunk + 1], near[0]))
        if before:
            dx = input_grads(chunk, local_exp, capacity, da, db, s, w_gate, w_up, order(dx, near[0]))
            far_up, far_down = order(far_up, dx), order(far_down, dx)
            back = swap(dx)
        far_up, far_down, _ = lax.optimization_barrier((far_up, far_down, near[0]))
        sum_up = weight_grads(f"up{chunk}", chunk, blocks((1, 0)), 1, half, *grads, far_up)[0]
        sum_down = weight_grads(f"down{chunk}", chunk, blocks((n_group - 1, 1)), 1, half, *grads, far_down)[0]
        own = list(weight_grads(f"own{chunk}", chunk, blocks(*own_pairs), 2, half, *grads))
        sent = [up(sum_up), down(sum_down)]
        if chunk + 1 < local_exp:
            dx = input_grads(chunk, local_exp, capacity, order(da, sum_up, sum_down), db, s, w_gate, w_up, dx)
            rows, dx, own[0], near_up, near_down, *_ = lax.optimization_barrier(
                (following, dx, own[0], near_up, near_down, sum_up, sum_down)
            )
        before = (own, sent, (near_up, near_down))
    back, near_up, near_down = lax.optimization_barrier((back, near_up, near_down))
    new = update(
        local_exp - 1, where, decay_mask, (own[0], sent[0], near_down, own[1], near_up, sent[1]), weights, new
    )
    grad_tokens, scores = combine(local_exp, capacity, ids_t, back, width)
    grad_probs = (scores / probs_t.astype(F32)).astype(BF16).T

    return (grad_tokens, grad_probs, *new)


def solution(mesh):
    placed = (
        P(("dp", "expert"), None),
        P(("dp", "expert"), None),
        P(("dp", "expert"), None),
        P(("dp", "expert"), None),
        P("expert", None, None),
        P("expert", None, None),
        P("expert", None, None),
        P("expert", None),
    )
    return jax.shard_map(
        body,
        mesh=mesh,
        in_specs=placed,
        out_specs=(
            P(("dp", "expert"), None),
            P(("dp", "expert"), None),
            P("expert", "dp", None),
            P("expert", "dp", None),
            P("expert", "dp", None),
        ),
        check_vma=False,
    )
```

```python
import functools

import jax
import jax.numpy as jnp
from jax import lax
from jax.experimental import pallas as pl
from jax.experimental.pallas import tpu as pltpu
from jax.sharding import PartitionSpec as P

step_size = 0.004
shrink_rate = 0.1
LANES = 128
F32 = jnp.float32
BF16 = jnp.bfloat16
VMEM_LIMIT = 60 * 1024 * 1024


def dot(a, b, dims):
    return lax.dot_general(a, b, (dims, ((), ())), preferred_element_type=F32)


def cost(flops, moved, chunk=1):
    scale = (10, 18)[min(chunk, 1)]
    return pl.CostEstimate(flops=scale * flops, transcendentals=0, bytes_accessed=scale * moved)


NN = ((1,), (0,))
NT = ((1,), (1,))
TN = ((0,), (0,))


def slot_values(ids_t, n_experts, capacity):
    topk, tok = ids_t.shape
    rows = lax.broadcasted_iota(jnp.int32, (n_experts, tok), 0)
    hit = ids_t[0:1, :] == rows
    for k in range(1, topk):
        hit = jnp.logical_or(hit, ids_t[k : k + 1, :] == rows)
    hit_f = jnp.where(hit, 1.0, 0.0)
    earlier = lax.broadcasted_iota(jnp.int32, (tok, tok), 0) < lax.broadcasted_iota(
        jnp.int32, (tok, tok), 1
    )
    count = dot(hit_f.astype(BF16), jnp.where(earlier, 1.0, 0.0).astype(BF16), NN)
    return jnp.where(jnp.logical_and(hit, count < capacity), count, -1.0)


def slot_rows(values, chunk, local_exp, capacity):
    n_experts, tok = values.shape
    n_rows = n_experts // local_exp * capacity
    expert_of = lax.broadcasted_iota(jnp.int32, (n_rows, n_experts), 0) // capacity * local_exp + chunk
    spread = jnp.where(expert_of == lax.broadcasted_iota(jnp.int32, (n_rows, n_experts), 1), 1.0, 0.0)
    spread = spread.astype(BF16)
    at = dot(spread, values.astype(BF16), NN)
    place = (lax.broadcasted_iota(jnp.int32, (n_rows, tok), 0) % capacity).astype(F32)
    return at == place, spread


def dispatch_kernel(chunk, local_exp, capacity, ids_ref, probs_ref, tok_ref, grad_ref, out_ref):
    ids_t = ids_ref[...]
    topk, tok = ids_t.shape
    n_experts = out_ref.shape[0] // capacity * local_exp
    width = tok_ref.shape[1]
    values = slot_values(ids_t, n_experts, capacity)
    rows = lax.broadcasted_iota(jnp.int32, (n_experts, tok), 0)
    prob = jnp.zeros((n_experts, tok), F32)
    for k in range(topk):
        prob = prob + jnp.where(ids_t[k : k + 1, :] == rows, probs_ref[k : k + 1, :].astype(F32), 0.0)
    onehot, spread = slot_rows(values, chunk, local_exp, capacity)
    prob_rows = dot(spread, prob.astype(BF16), NN)
    pick = jnp.where(onehot, 1.0, 0.0).astype(BF16)
    weighted = jnp.where(onehot, prob_rows, 0.0).astype(BF16)
    out_ref[:, :width] = dot(pick, tok_ref[...], NN).astype(BF16)
    out_ref[:, width:] = dot(weighted, grad_ref[...], NN).astype(BF16)


def dispatch(chunk, local_exp, capacity, n_experts, ids_t, probs_t, tokens, out_grad):
    tok, width = tokens.shape
    n_rows = n_experts // local_exp * capacity
    return pl.pallas_call(
        functools.partial(dispatch_kernel, chunk, local_exp, capacity),
        out_shape=jax.ShapeDtypeStruct((n_rows, 2 * width), BF16),
        compiler_params=pltpu.CompilerParams(vmem_limit_bytes=VMEM_LIMIT),
        cost_estimate=cost(4 * n_rows * tok * width, 4 * width * (tok + n_rows), 0),
        name=f"dispatch{chunk}",
    )(ids_t, probs_t, tokens, out_grad)


def hidden_kernel(
    where_ref, x_ref, do_ref, xa_ref, xb_ref, da_col_ref, db_col_ref, wg_ref, wu_ref, wd_ref,
    hid_ref, da_ref, db_ref, s_ref, a_ref, b_ref, sum_ref,
):
    step = pl.program_id(0)
    gate = dot(x_ref[...], wg_ref[0], NN)
    upper = dot(x_ref[...], wu_ref[0], NN)
    sig = jax.nn.sigmoid(gate)
    act = gate * sig
    hid = (act * upper).astype(BF16)
    hid_ref[...] = hid
    dhid = dot(do_ref[...], wd_ref[0], NN)
    part = jnp.sum(hid.astype(F32) * dhid, axis=1, keepdims=True)
    dgate = (dhid * upper * sig * (1.0 + gate * (1.0 - sig))).astype(BF16)
    dup = (dhid * act).astype(BF16)
    da_ref[...] = dgate
    db_ref[...] = dup
    for out_ref, x_col, do_col in ((a_ref, xa_ref, da_col_ref), (b_ref, xb_ref, db_col_ref)):
        out_ref[0] = dot(x_col[...], dgate, TN).astype(BF16)
        out_ref[1] = dot(x_col[...], dup, TN).astype(BF16)
        out_ref[2] = dot(do_col[...], hid, TN).astype(BF16)

    @pl.when(step == 0)
    def _():
        sum_ref[...] = jnp.broadcast_to(part, sum_ref.shape)

    @pl.when(step > 0)
    def _():
        sum_ref[...] = sum_ref[...] + part

    @pl.when(step == pl.num_programs(0) - 1)
    def _():
        total = sum_ref[...]
        high = total.astype(BF16).astype(F32)
        lane = lax.broadcasted_iota(jnp.int32, s_ref.shape, 1)
        s_ref[...] = jnp.where(lane == 0, high, jnp.where(lane == 1, total - high, 0.0)).astype(BF16)


def whole(shape):
    return pl.BlockSpec(shape, lambda *_: (0,) * len(shape), pipeline_mode=pl.Buffered(1))


def hidden_grads(chunk, where, half, rows, wg, wu, wd):
    n_rows, width = rows.shape[0], rows.shape[1] // 2
    hidden = wg.shape[2]
    block = 2 * LANES
    lefts = width // half
    once = pl.Buffered(1)
    weight = pl.BlockSpec((1, width, block), lambda i, at: (chunk, 0, i))
    result = pl.BlockSpec((n_rows, block), lambda i, at: (0, i))
    shard = pl.BlockSpec((3, half, block), lambda i, at: (0, 0, i))
    return pl.pallas_call(
        hidden_kernel,
        grid_spec=pltpu.PrefetchScalarGridSpec(
            num_scalar_prefetch=1,
            grid=(hidden // block,),
            in_specs=[
                pl.BlockSpec((n_rows, width), lambda i, at: (0, 0), pipeline_mode=once),
                pl.BlockSpec((n_rows, width), lambda i, at: (0, 1), pipeline_mode=once),
                pl.BlockSpec((n_rows, half), lambda i, at: (0, at[0]), pipeline_mode=once),
                pl.BlockSpec((n_rows, half), lambda i, at: (0, at[1]), pipeline_mode=once),
                pl.BlockSpec((n_rows, half), lambda i, at: (0, at[0] + lefts), pipeline_mode=once),
                pl.BlockSpec((n_rows, half), lambda i, at: (0, at[1] + lefts), pipeline_mode=once),
                weight,
                weight,
                weight,
            ],
            out_specs=[result] * 3 + [whole((n_rows, LANES)), shard, shard],
            scratch_shapes=[pltpu.VMEM((n_rows, LANES), F32)],
        ),
        out_shape=[jax.ShapeDtypeStruct((n_rows, hidden), BF16)] * 3
        + [jax.ShapeDtypeStruct((n_rows, LANES), BF16)]
        + [jax.ShapeDtypeStruct((3, half, hidden), BF16)] * 2,
        compiler_params=pltpu.CompilerParams(vmem_limit_bytes=VMEM_LIMIT),
        cost_estimate=cost(8 * n_rows * width * hidden, 6 * width * hidden + n_rows * (4 * width + 6 * hidden), chunk),
        name=f"hidden{chunk}",
    )(where, *[rows] * 6, wg, wu, wd)


def weight_kernel(n_add, n_after, where_ref, x_ref, do_ref, hid_ref, da_ref, db_ref, *refs):
    adds, outs = refs[:n_add], refs[n_add + n_after :]
    for m, (left, right) in enumerate(((x_ref, da_ref), (x_ref, db_ref), (do_ref, hid_ref))):
        part = dot(left[...], right[...], TN)
        for addend in adds:
            part = part + addend[m].astype(F32)
        for i, out_ref in enumerate(outs):

            @pl.when(pl.program_id(0) == i)
            def _():
                out_ref[m] = part.astype(BF16)


def weight_grads(name, chunk, where, count, half, rows, hid, da, db, *adds, after=()):
    n_rows, width = rows.shape[0], rows.shape[1] // 2
    hidden = hid.shape[1]
    lefts = width // half
    shape = (3, half, hidden)
    return pl.pallas_call(
        functools.partial(weight_kernel, len(adds), len(after)),
        grid_spec=pltpu.PrefetchScalarGridSpec(
            num_scalar_prefetch=1,
            grid=(count,),
            in_specs=[
                pl.BlockSpec((n_rows, half), lambda i, at: (0, at[i])),
                pl.BlockSpec((n_rows, half), lambda i, at: (0, at[i] + lefts)),
            ]
            + [whole(a.shape) for a in (hid, da, db, *adds)]
            + [pl.BlockSpec(memory_space=pl.ANY)] * len(after),
            out_specs=[whole(shape)] * count,
        ),
        out_shape=[jax.ShapeDtypeStruct(shape, BF16)] * count,
        compiler_params=pltpu.CompilerParams(vmem_limit_bytes=VMEM_LIMIT),
        cost_estimate=cost(6 * count * n_rows * half * hidden, 6 * n_rows * hidden + 6 * count * half * hidden, chunk),
        name=name,
    )(where, rows, rows, hid, da, db, *adds, *after)


def mark_kernel(a_ref, b_ref, out_ref):
    out_ref[...] = a_ref[0] + b_ref[0]


def mark(chunk, first, second):
    corner = pl.BlockSpec((1, 16, LANES), lambda i: (0, 0, 0))
    return pl.pallas_call(
        mark_kernel,
        grid=(1,),
        in_specs=[corner, corner],
        out_specs=pl.BlockSpec((16, LANES), lambda i: (0, 0)),
        out_shape=jax.ShapeDtypeStruct((16, LANES), BF16),
        cost_estimate=cost(5 * 3 * first.size, 5 * 3 * first.size, chunk),
        name=f"mark{chunk}",
    )(first, second)


def update_kernel(chunk, where_ref, mask_ref, *refs):
    grads, weights = refs[:6], refs[6:9]
    outs = refs[-3:]
    for second in range(2):

        @pl.when(pl.program_id(0) == second)
        def _():
            for m in range(3):
                grad = sum(g[m].astype(F32) for g in grads[3 * second : 3 * second + 3])
                weight = weights[m][0].astype(F32)
                rate = mask_ref[chunk, m].astype(F32)
                outs[m][0] = (weight - step_size * grad - shrink_rate * rate * weight).astype(BF16)


def update(chunk, where, mask, grads, weights, into):
    _, half, hidden = grads[0].shape
    local = weights[0].shape[0]
    steps = 2
    block = half // steps
    early = pl.BlockSpec((3, block, hidden), lambda h, r, w: (0, r * (1 - h) + (steps - 1) * h, 0))
    late = pl.BlockSpec((3, block, hidden), lambda h, r, w: (0, r * h, 0))
    weight = pl.BlockSpec((1, block, hidden), lambda h, r, w: (chunk, (2 * w[0] + h) * steps + r, 0))
    result = pl.BlockSpec((1, block, hidden), lambda h, r, w: (chunk, h * steps + r, 0))
    extra = list(into or [])
    return pl.pallas_call(
        functools.partial(update_kernel, chunk),
        grid_spec=pltpu.PrefetchScalarGridSpec(
            num_scalar_prefetch=1,
            grid=(2, steps),
            in_specs=[pl.BlockSpec(memory_space=pltpu.SMEM)]
            + [early] * 3
            + [late] * 3
            + [weight] * 3
            + [pl.BlockSpec(memory_space=pl.ANY)] * len(extra),
            out_specs=[result] * 3,
        ),
        out_shape=[jax.ShapeDtypeStruct((local, 2 * half, hidden), BF16)] * 3,
        input_output_aliases={11 + i: i for i in range(len(extra))},
        compiler_params=pltpu.CompilerParams(vmem_limit_bytes=VMEM_LIMIT),
        cost_estimate=cost(10 * half * hidden, 60 * half * hidden),
        name=f"update{chunk}",
    )(where, mask, *grads, *weights, *extra)


def dx_kernel(da_ref, db_ref, s_ref, wg_ref, wu_ref, *refs):
    out_ref = refs[-1]
    n_owner, capacity, lanes = out_ref.shape
    width = wg_ref.shape[1]
    dx = (dot(da_ref[...], wg_ref[0], NT) + dot(db_ref[...], wu_ref[0], NT)).astype(BF16)
    out_ref[:, :, :width] = dx.reshape(n_owner, capacity, width)
    out_ref[:, :, width:] = s_ref[...].reshape(n_owner, capacity, lanes - width)


def input_grads(chunk, local_exp, capacity, da, db, s, wg, wu, into):
    n_rows, hidden = da.shape
    width = wg.shape[1]
    n_owner = n_rows // capacity
    weight = pl.BlockSpec((1, width, hidden), lambda i: (chunk, 0, 0), pipeline_mode=pl.Buffered(1))
    extra = [] if into is None else [into]
    return pl.pallas_call(
        dx_kernel,
        grid=(1,),
        in_specs=[whole((n_rows, hidden)), whole((n_rows, hidden)), whole((n_rows, LANES)), weight, weight]
        + [pl.BlockSpec(memory_space=pl.ANY)] * len(extra),
        out_specs=pl.BlockSpec(
            (n_owner, capacity, width + LANES), lambda i: (0, chunk, 0), pipeline_mode=pl.Buffered(1)
        ),
        out_shape=jax.ShapeDtypeStruct((n_owner, local_exp * capacity, width + LANES), BF16),
        input_output_aliases={5: 0} if extra else {},
        compiler_params=pltpu.CompilerParams(vmem_limit_bytes=VMEM_LIMIT),
        cost_estimate=cost(4 * n_rows * width * hidden, 4 * width * hidden + 2 * n_rows * (width + 2 * hidden), chunk),
        name=f"dx{chunk}",
    )(da, db, s, wg, wu, *extra)


def combine_kernel(local_exp, capacity, ids_ref, back_ref, tok_ref, prob_ref):
    ids_t = ids_ref[...]
    topk, tok = ids_t.shape
    n_rows = back_ref.shape[0] * capacity
    n_experts = back_ref.shape[0] * local_exp
    width = tok_ref.shape[1]
    values = slot_values(ids_t, n_experts, capacity)
    total = jnp.zeros((tok, width), F32)
    by_expert = jnp.zeros((n_experts, tok), F32)
    for chunk in range(local_exp):
        onehot, spread = slot_rows(values, chunk, local_exp, capacity)
        pick = jnp.where(onehot, 1.0, 0.0)
        slots = slice(chunk * capacity, (chunk + 1) * capacity)
        dx = back_ref[:, slots, :width].reshape(n_rows, width)
        total = total + dot(pick.astype(BF16), dx, TN)
        s = back_ref[:, slots, width:].reshape(n_rows, LANES).astype(F32)
        placed = pick * (s[:, 0:1] + s[:, 1:2])
        high = placed.astype(BF16)
        low = (placed - high.astype(F32)).astype(BF16)
        by_expert = by_expert + dot(spread, high, TN) + dot(spread, low, TN)
    tok_ref[...] = total.astype(BF16)
    rows = lax.broadcasted_iota(jnp.int32, (n_experts, tok), 0)
    for k in range(topk):
        mine = jnp.where(ids_t[k : k + 1, :] == rows, by_expert, 0.0)
        prob_ref[k : k + 1, :] = jnp.sum(mine, axis=0, keepdims=True)


def combine(local_exp, capacity, ids_t, back, width):
    topk, tok = ids_t.shape
    return pl.pallas_call(
        functools.partial(combine_kernel, local_exp, capacity),
        out_shape=[
            jax.ShapeDtypeStruct((tok, width), BF16),
            jax.ShapeDtypeStruct((topk, tok), F32),
        ],
        compiler_params=pltpu.CompilerParams(vmem_limit_bytes=VMEM_LIMIT),
        cost_estimate=cost(2 * back.shape[0] * back.shape[1] * tok * width, 2 * back.size),
        name="combine",
    )(ids_t, back)


def body(tokens, out_grad, expert_ids, route_probs, w_gate, w_up, w_down, decay_mask):
    n_owner = lax.axis_size("expert")
    n_group = lax.axis_size("dp")
    local_exp = w_gate.shape[0]
    width = tokens.shape[1]
    tok_rows, topk = expert_ids.shape
    n_experts = n_owner * local_exp
    capacity = tok_rows * topk // n_experts
    ids_t = expert_ids.T
    probs_t = route_probs.T
    half = width // n_group // 2
    plane = lax.axis_index("dp").astype(jnp.int32)
    where = plane.reshape(1)

    def half_shard(ahead, second):
        return 2 * ((plane + ahead) % n_group) + second

    def blocks(*pairs):
        return jnp.stack([half_shard(*pair) for pair in pairs]).astype(jnp.int32)

    def up(a):
        return lax.ppermute(a, "dp", [(i, (i + 1) % n_group) for i in range(n_group)])

    def down(a):
        return lax.ppermute(a, "dp", [(i, (i - 1) % n_group) for i in range(n_group)])

    def send(chunk):
        return dispatch(chunk, local_exp, capacity, n_experts, ids_t, probs_t, tokens, out_grad)

    def swap(a):
        return lax.all_to_all(a, "expert", split_axis=0, concat_axis=0, tiled=True)

    def swap_rows(a):
        a = a.reshape(n_owner, capacity, a.shape[1])
        return swap(a).reshape(n_owner * capacity, a.shape[2])

    def order(value, *after):
        return lax.optimization_barrier((value, *after))[0]

    weights = (w_gate, w_up, w_down)
    far_pairs = ((2, 0), (2, 1))
    near_pairs = ((1, 1), (n_group - 1, 0))
    own_pairs = ((0, 0), (0, 1))
    new, dx, before = None, None, None
    sends = [send(chunk) for chunk in range(local_exp)]
    rows = order(swap_rows(sends[0]), *sends[1:])
    for chunk in range(local_exp):
        hid, da, db, s, *far = hidden_grads(chunk, blocks(*far_pairs), half, rows, *weights)
        far_up, far_down = up(far[0]), down(far[1])
        grads, after = (rows, hid, da, db), ()
        if before:
            dx, left = lax.optimization_barrier((dx, mark(chunk, *far)))
            after = [left]
            dx = input_grads(chunk, local_exp, capacity, da, db, s, w_gate, w_up, dx)
            back = swap(dx)
            rows, _, *last = lax.optimization_barrier((rows, dx, *before[1]))
            own, (near_up, near_down) = before[0], before[2]
            new = update(chunk - 1, where, decay_mask, (own[0], last[0], near_down, own[1], near_up, last[1]), weights, new)
            grads = (rows, hid, da, db)
        if chunk + 1 < local_exp:
            following, *after = lax.optimization_barrier((sends[chunk + 1], mark(chunk, *far)))
            following = swap_rows(following)
        near = weight_grads(f"near{chunk}", chunk, blocks(*near_pairs), 2, half, *grads, after=after)
        near_up, near_down = up(near[0]), down(near[1])
        far_up, far_down, _ = lax.optimization_barrier((far_up, far_down, near[0]))
        sum_up = weight_grads(f"up{chunk}", chunk, blocks((1, 0)), 1, half, *grads, far_up)[0]
        sum_down = weight_grads(f"down{chunk}", chunk, blocks((n_group - 1, 1)), 1, half, *grads, far_down)[0]
        own = list(weight_grads(f"own{chunk}", chunk, blocks(*own_pairs), 2, half, *grads))
        sent = [up(sum_up), down(sum_down)]
        if chunk + 1 < local_exp:
            dx = input_grads(chunk, local_exp, capacity, order(da, sum_up, sum_down), db, s, w_gate, w_up, dx)
            rows, dx, own[0], near_up, near_down, *_ = lax.optimization_barrier(
                (following, dx, own[0], near_up, near_down, sum_up, sum_down)
            )
        before = (own, sent, (near_up, near_down))
    back, near_up, near_down = lax.optimization_barrier((back, near_up, near_down))
    new = update(
        local_exp - 1, where, decay_mask, (own[0], sent[0], near_down, own[1], near_up, sent[1]), weights, new
    )
    grad_tokens, scores = combine(local_exp, capacity, ids_t, back, width)
    grad_probs = (scores / probs_t.astype(F32)).astype(BF16).T

    return (grad_tokens, grad_probs, *new)


def solution(mesh):
    placed = (
        P(("dp", "expert"), None),
        P(("dp", "expert"), None),
        P(("dp", "expert"), None),
        P(("dp", "expert"), None),
        P("expert", None, None),
        P("expert", None, None),
        P("expert", None, None),
        P("expert", None),
    )
    return jax.shard_map(
        body,
        mesh=mesh,
        in_specs=placed,
        out_specs=(
            P(("dp", "expert"), None),
            P(("dp", "expert"), None),
            P("expert", "dp", None),
            P("expert", "dp", None),
            P("expert", "dp", None),
        ),
        check_vma=False,
    )
```

```python
import functools

import jax
import jax.numpy as jnp
from jax import lax
from jax.experimental import pallas as pl
from jax.experimental.pallas import tpu as pltpu
from jax.sharding import PartitionSpec as P

step_size = 0.004
shrink_rate = 0.1
LANES = 128
F32 = jnp.float32
BF16 = jnp.bfloat16
VMEM_LIMIT = 60 * 1024 * 1024


def dot(a, b, dims):
    return lax.dot_general(a, b, (dims, ((), ())), preferred_element_type=F32)


def cost(flops, moved, chunk=1):
    scale = (7, 24)[min(chunk, 1)]
    return pl.CostEstimate(flops=scale * flops, transcendentals=0, bytes_accessed=scale * moved)


NN = ((1,), (0,))
NT = ((1,), (1,))
TN = ((0,), (0,))


def slot_values(ids_t, n_experts, capacity):
    topk, tok = ids_t.shape
    rows = lax.broadcasted_iota(jnp.int32, (n_experts, tok), 0)
    hit = ids_t[0:1, :] == rows
    for k in range(1, topk):
        hit = jnp.logical_or(hit, ids_t[k : k + 1, :] == rows)
    hit_f = jnp.where(hit, 1.0, 0.0)
    earlier = lax.broadcasted_iota(jnp.int32, (tok, tok), 0) < lax.broadcasted_iota(
        jnp.int32, (tok, tok), 1
    )
    count = dot(hit_f.astype(BF16), jnp.where(earlier, 1.0, 0.0).astype(BF16), NN)
    return jnp.where(jnp.logical_and(hit, count < capacity), count, -1.0)


def slot_rows(values, chunk, local_exp, capacity, first=0, n_rows=None):
    n_experts, tok = values.shape
    n_rows = n_rows or n_experts // local_exp * capacity
    row = lax.broadcasted_iota(jnp.int32, (n_rows, n_experts), 0) + first
    expert_of = row // capacity * local_exp + chunk
    spread = jnp.where(expert_of == lax.broadcasted_iota(jnp.int32, (n_rows, n_experts), 1), 1.0, 0.0)
    spread = spread.astype(BF16)
    at = dot(spread, values.astype(BF16), NN)
    place = (lax.broadcasted_iota(jnp.int32, (n_rows, tok), 0) % capacity).astype(F32)
    return at == place, spread


def dispatch_kernel(
    chunk, local_exp, capacity, ids_ref, probs_ref, tok_ref, grad_ref, out_ref, values_ref, prob_ref
):
    n_experts, tok = values_ref.shape
    n_rows = out_ref.shape[0]
    width = tok_ref.shape[1]
    step = pl.program_id(0)

    @pl.when(step == 0)
    def _():
        ids_t = ids_ref[...]
        rows = lax.broadcasted_iota(jnp.int32, (n_experts, tok), 0)
        prob = jnp.zeros((n_experts, tok), F32)
        for k in range(ids_t.shape[0]):
            prob = prob + jnp.where(ids_t[k : k + 1, :] == rows, probs_ref[k : k + 1, :].astype(F32), 0.0)
        values_ref[...] = slot_values(ids_t, n_experts, capacity)
        prob_ref[...] = prob

    onehot, spread = slot_rows(values_ref[...], chunk, local_exp, capacity, step * n_rows, n_rows)
    prob_rows = dot(spread, prob_ref[...].astype(BF16), NN)
    pick = jnp.where(onehot, 1.0, 0.0).astype(BF16)
    weighted = jnp.where(onehot, prob_rows, 0.0).astype(BF16)
    out_ref[:, :width] = dot(pick, tok_ref[...], NN).astype(BF16)
    out_ref[:, width:] = dot(weighted, grad_ref[...], NN).astype(BF16)


def dispatch(chunk, local_exp, capacity, n_experts, ids_t, probs_t, tokens, out_grad):
    tok, width = tokens.shape
    n_rows = n_experts // local_exp * capacity
    steps = 4
    return pl.pallas_call(
        functools.partial(dispatch_kernel, chunk, local_exp, capacity),
        grid=(steps,),
        in_specs=[whole(a.shape) for a in (ids_t, probs_t, tokens, out_grad)],
        out_specs=pl.BlockSpec((n_rows // steps, 2 * width), lambda i: (i, 0)),
        out_shape=jax.ShapeDtypeStruct((n_rows, 2 * width), BF16),
        scratch_shapes=[pltpu.VMEM((n_experts, tok), F32), pltpu.VMEM((n_experts, tok), F32)],
        compiler_params=pltpu.CompilerParams(vmem_limit_bytes=VMEM_LIMIT),
        cost_estimate=cost(4 * n_rows * tok * width, 4 * width * (tok + n_rows), 0),
        name=f"dispatch{chunk}",
    )(ids_t, probs_t, tokens, out_grad)


def hidden_kernel(
    where_ref, x_ref, rows_ref, wg_ref, wu_ref, wd_ref,
    hid_ref, da_ref, db_ref, s_ref, a_ref, b_ref, sum_ref, do_ref, sem,
):
    step = pl.program_id(0)
    width = x_ref.shape[1]
    fetch = pltpu.make_async_copy(rows_ref.at[:, pl.ds(width, width)], do_ref, sem)

    @pl.when(step == 0)
    def _():
        fetch.start()

    gate = dot(x_ref[...], wg_ref[0], NN)
    upper = dot(x_ref[...], wu_ref[0], NN)
    sig = jax.nn.sigmoid(gate)
    act = gate * sig
    hid = (act * upper).astype(BF16)
    hid_ref[...] = hid

    @pl.when(step == 0)
    def _():
        fetch.wait()

    dhid = dot(do_ref[...], wd_ref[0], NN)
    part = jnp.sum(hid.astype(F32) * dhid, axis=1, keepdims=True)
    dgate = (dhid * upper * sig * (1.0 + gate * (1.0 - sig))).astype(BF16)
    dup = (dhid * act).astype(BF16)
    da_ref[...] = dgate
    db_ref[...] = dup
    half = a_ref.shape[1]
    for i, out_ref in enumerate((a_ref, b_ref)):
        columns = pl.ds(pl.multiple_of(where_ref[i] * half, half), half)
        out_ref[0] = dot(x_ref[:, columns], dgate, TN).astype(BF16)
        out_ref[1] = dot(x_ref[:, columns], dup, TN).astype(BF16)
        out_ref[2] = dot(do_ref[:, columns], hid, TN).astype(BF16)

    @pl.when(step == 0)
    def _():
        sum_ref[...] = jnp.broadcast_to(part, sum_ref.shape)

    @pl.when(step > 0)
    def _():
        sum_ref[...] = sum_ref[...] + part

    @pl.when(step == pl.num_programs(0) - 1)
    def _():
        total = sum_ref[...]
        high = total.astype(BF16).astype(F32)
        lane = lax.broadcasted_iota(jnp.int32, s_ref.shape, 1)
        s_ref[...] = jnp.where(lane == 0, high, jnp.where(lane == 1, total - high, 0.0)).astype(BF16)


def whole(shape):
    return pl.BlockSpec(shape, lambda *_: (0,) * len(shape), pipeline_mode=pl.Buffered(1))


def hidden_grads(chunk, where, half, rows, wg, wu, wd):
    n_rows, width = rows.shape[0], rows.shape[1] // 2
    hidden = wg.shape[2]
    block = 2 * LANES
    once = pl.Buffered(1)
    weight = pl.BlockSpec((1, width, block), lambda i, at: (chunk, 0, i))
    result = pl.BlockSpec((n_rows, block), lambda i, at: (0, i))
    shard = pl.BlockSpec((3, half, block), lambda i, at: (0, 0, i))
    return pl.pallas_call(
        hidden_kernel,
        grid_spec=pltpu.PrefetchScalarGridSpec(
            num_scalar_prefetch=1,
            grid=(hidden // block,),
            in_specs=[
                pl.BlockSpec((n_rows, width), lambda i, at: (0, 0), pipeline_mode=once),
                pl.BlockSpec(memory_space=pl.ANY),
                weight,
                weight,
                weight,
            ],
            out_specs=[result] * 3 + [whole((n_rows, LANES)), shard, shard],
            scratch_shapes=[
                pltpu.VMEM((n_rows, LANES), F32),
                pltpu.VMEM((n_rows, width), BF16),
                pltpu.SemaphoreType.DMA,
            ],
        ),
        out_shape=[jax.ShapeDtypeStruct((n_rows, hidden), BF16)] * 3
        + [jax.ShapeDtypeStruct((n_rows, LANES), BF16)]
        + [jax.ShapeDtypeStruct((3, half, hidden), BF16)] * 2,
        compiler_params=pltpu.CompilerParams(vmem_limit_bytes=VMEM_LIMIT),
        cost_estimate=cost(8 * n_rows * width * hidden, 6 * width * hidden + n_rows * (4 * width + 6 * hidden), chunk),
        name=f"hidden{chunk}",
    )(where, rows, rows, wg, wu, wd)


def weight_kernel(n_add, n_after, where_ref, x_ref, do_ref, hid_ref, da_ref, db_ref, *refs):
    adds, outs = refs[:n_add], refs[n_add + n_after :]
    for m, (left, right) in enumerate(((x_ref, da_ref), (x_ref, db_ref), (do_ref, hid_ref))):
        part = dot(left[...], right[...], TN)
        for addend in adds:
            part = part + addend[m].astype(F32)
        for i, out_ref in enumerate(outs):

            @pl.when(pl.program_id(0) == i)
            def _():
                out_ref[m] = part.astype(BF16)


def weight_grads(name, chunk, where, count, half, rows, hid, da, db, *adds, after=()):
    n_rows, width = rows.shape[0], rows.shape[1] // 2
    hidden = hid.shape[1]
    lefts = width // half
    shape = (3, half, hidden)
    return pl.pallas_call(
        functools.partial(weight_kernel, len(adds), len(after)),
        grid_spec=pltpu.PrefetchScalarGridSpec(
            num_scalar_prefetch=1,
            grid=(count,),
            in_specs=[
                pl.BlockSpec((n_rows, half), lambda i, at: (0, at[i])),
                pl.BlockSpec((n_rows, half), lambda i, at: (0, at[i] + lefts)),
            ]
            + [whole(a.shape) for a in (hid, da, db, *adds)]
            + [pl.BlockSpec(memory_space=pl.ANY)] * len(after),
            out_specs=[whole(shape)] * count,
        ),
        out_shape=[jax.ShapeDtypeStruct(shape, BF16)] * count,
        compiler_params=pltpu.CompilerParams(vmem_limit_bytes=VMEM_LIMIT),
        cost_estimate=cost(6 * count * n_rows * half * hidden, 6 * n_rows * hidden + 6 * count * half * hidden, chunk),
        name=name,
    )(where, rows, rows, hid, da, db, *adds, *after)


def mark_kernel(a_ref, b_ref, out_ref):
    out_ref[...] = a_ref[0] + b_ref[0]


def mark(chunk, first, second):
    corner = pl.BlockSpec((1, 16, LANES), lambda i: (0, 0, 0))
    return pl.pallas_call(
        mark_kernel,
        grid=(1,),
        in_specs=[corner, corner],
        out_specs=pl.BlockSpec((16, LANES), lambda i: (0, 0)),
        out_shape=jax.ShapeDtypeStruct((16, LANES), BF16),
        cost_estimate=cost(5 * 3 * first.size, 5 * 3 * first.size, chunk),
        name=f"mark{chunk}",
    )(first, second)


def update_kernel(chunk, where_ref, mask_ref, *refs):
    grads, weights = refs[:4], refs[4:7]
    outs = refs[-3:]
    for second in range(2):

        @pl.when(pl.program_id(0) == second)
        def _():
            for m in range(3):
                grad = sum(g[m].astype(F32) for g in grads[2 * second : 2 * second + 2])
                weight = weights[m][0].astype(F32)
                rate = mask_ref[chunk, m].astype(F32)
                outs[m][0] = (weight - step_size * grad - shrink_rate * rate * weight).astype(BF16)


def update(chunk, where, mask, grads, weights, into):
    _, half, hidden = grads[0].shape
    local = weights[0].shape[0]
    steps = 2
    block = half // steps
    early = pl.BlockSpec((3, block, hidden), lambda h, r, w: (0, r * (1 - h) + (steps - 1) * h, 0))
    late = pl.BlockSpec((3, block, hidden), lambda h, r, w: (0, r * h, 0))
    weight = pl.BlockSpec((1, block, hidden), lambda h, r, w: (chunk, (2 * w[0] + h) * steps + r, 0))
    result = pl.BlockSpec((1, block, hidden), lambda h, r, w: (chunk, h * steps + r, 0))
    extra = list(into or [])
    return pl.pallas_call(
        functools.partial(update_kernel, chunk),
        grid_spec=pltpu.PrefetchScalarGridSpec(
            num_scalar_prefetch=1,
            grid=(2, steps),
            in_specs=[pl.BlockSpec(memory_space=pltpu.SMEM)]
            + [early] * 2
            + [late] * 2
            + [weight] * 3
            + [pl.BlockSpec(memory_space=pl.ANY)] * len(extra),
            out_specs=[result] * 3,
        ),
        out_shape=[jax.ShapeDtypeStruct((local, 2 * half, hidden), BF16)] * 3,
        input_output_aliases={9 + i: i for i in range(len(extra))},
        compiler_params=pltpu.CompilerParams(vmem_limit_bytes=VMEM_LIMIT),
        cost_estimate=cost(10 * half * hidden, 60 * half * hidden),
        name=f"update{chunk}",
    )(where, mask, *grads, *weights, *extra)


def dx_kernel(da_ref, db_ref, s_ref, wg_ref, wu_ref, *refs):
    out_ref = refs[-1]
    n_owner, capacity, block = out_ref.shape
    last = pl.num_programs(0) - 1

    @pl.when(pl.program_id(0) < last)
    def _():
        dx = dot(da_ref[...], wg_ref[0], NT) + dot(db_ref[...], wu_ref[0], NT)
        out_ref[...] = dx.astype(BF16).reshape(n_owner, capacity, block)

    @pl.when(pl.program_id(0) == last)
    def _():
        out_ref[:, :, :LANES] = s_ref[...].reshape(n_owner, capacity, LANES)


def input_grads(chunk, local_exp, capacity, da, db, s, wg, wu, into):
    n_rows, hidden = da.shape
    width = wg.shape[1]
    n_owner = n_rows // capacity
    block = width // 4
    weight = pl.BlockSpec((1, block, hidden), lambda i: (chunk, jnp.minimum(i, 3), 0))
    extra = [] if into is None else [into]
    return pl.pallas_call(
        dx_kernel,
        grid=(5,),
        in_specs=[whole((n_rows, hidden)), whole((n_rows, hidden)), whole((n_rows, LANES)), weight, weight]
        + [pl.BlockSpec(memory_space=pl.ANY)] * len(extra),
        out_specs=pl.BlockSpec((n_owner, capacity, block), lambda i: (0, chunk, i)),
        out_shape=jax.ShapeDtypeStruct((n_owner, local_exp * capacity, width + LANES), BF16),
        input_output_aliases={5: 0} if extra else {},
        compiler_params=pltpu.CompilerParams(vmem_limit_bytes=VMEM_LIMIT),
        cost_estimate=cost(4 * n_rows * width * hidden, 4 * width * hidden + 2 * n_rows * (width + 2 * hidden), chunk),
        name=f"dx{chunk}",
    )(da, db, s, wg, wu, *extra)


def combine_kernel(local_exp, capacity, ids_ref, probs_ref, back_ref, tok_ref, prob_ref):
    ids_t = ids_ref[...]
    topk, tok = ids_t.shape
    n_rows = back_ref.shape[0] * capacity
    n_experts = back_ref.shape[0] * local_exp
    width = tok_ref.shape[1]
    values = slot_values(ids_t, n_experts, capacity)
    total = jnp.zeros((tok, width), F32)
    by_expert = jnp.zeros((n_experts, tok), F32)
    for chunk in range(local_exp):
        onehot, spread = slot_rows(values, chunk, local_exp, capacity)
        pick = jnp.where(onehot, 1.0, 0.0)
        slots = slice(chunk * capacity, (chunk + 1) * capacity)
        dx = back_ref[:, slots, :width].reshape(n_rows, width)
        total = total + dot(pick.astype(BF16), dx, TN)
        s = back_ref[:, slots, width:].reshape(n_rows, LANES).astype(F32)
        placed = pick * (s[:, 0:1] + s[:, 1:2])
        high = placed.astype(BF16)
        low = (placed - high.astype(F32)).astype(BF16)
        by_expert = by_expert + dot(spread, high, TN) + dot(spread, low, TN)
    tok_ref[...] = total.astype(BF16)
    rows = lax.broadcasted_iota(jnp.int32, (n_experts, tok), 0)
    for k in range(topk):
        mine = jnp.where(ids_t[k : k + 1, :] == rows, by_expert, 0.0)
        score = jnp.sum(mine, axis=0, keepdims=True)
        prob_ref[k : k + 1, :] = (score / probs_ref[k : k + 1, :].astype(F32)).astype(BF16)


def combine(local_exp, capacity, ids_t, probs_t, back, width):
    topk, tok = ids_t.shape
    return pl.pallas_call(
        functools.partial(combine_kernel, local_exp, capacity),
        out_shape=[
            jax.ShapeDtypeStruct((tok, width), BF16),
            jax.ShapeDtypeStruct((topk, tok), BF16),
        ],
        compiler_params=pltpu.CompilerParams(vmem_limit_bytes=VMEM_LIMIT),
        cost_estimate=cost(2 * back.shape[0] * back.shape[1] * tok * width, 2 * back.size),
        name="combine",
    )(ids_t, probs_t, back)


def body(tokens, out_grad, expert_ids, route_probs, w_gate, w_up, w_down, decay_mask):
    n_owner = lax.axis_size("expert")
    n_group = lax.axis_size("dp")
    local_exp = w_gate.shape[0]
    width = tokens.shape[1]
    tok_rows, topk = expert_ids.shape
    n_experts = n_owner * local_exp
    capacity = tok_rows * topk // n_experts
    ids_t = expert_ids.T
    probs_t = route_probs.T
    half = width // n_group // 2
    plane = lax.axis_index("dp").astype(jnp.int32)
    where = plane.reshape(1)

    def half_shard(ahead, second):
        return 2 * ((plane + ahead) % n_group) + second

    def blocks(*pairs):
        return jnp.stack([half_shard(*pair) for pair in pairs]).astype(jnp.int32)

    def up(a):
        return lax.ppermute(a, "dp", [(i, (i + 1) % n_group) for i in range(n_group)])

    def down(a):
        return lax.ppermute(a, "dp", [(i, (i - 1) % n_group) for i in range(n_group)])

    def send(chunk):
        return dispatch(chunk, local_exp, capacity, n_experts, ids_t, probs_t, tokens, out_grad)

    def swap(a):
        return lax.all_to_all(a, "expert", split_axis=0, concat_axis=0, tiled=True)

    def swap_rows(a):
        a = a.reshape(n_owner, capacity, a.shape[1])
        return swap(a).reshape(n_owner * capacity, a.shape[2])

    def order(value, *after):
        return lax.optimization_barrier((value, *after))[0]

    def own_sum(chunk, grads, near_up, near_down):
        return [
            weight_grads(f"own{chunk}{second}", chunk, blocks((0, second)), 1, half, *grads, landed)[0]
            for second, landed in enumerate((near_down, near_up))
        ]

    weights = (w_gate, w_up, w_down)
    far_pairs = ((2, 0), (2, 1))
    near_pairs = ((1, 1), (n_group - 1, 0))
    new, dx, before = None, None, None
    sends = [send(chunk) for chunk in range(local_exp)]
    rows = order(swap_rows(sends[0]), *sends[1:])
    for chunk in range(local_exp):
        hid, da, db, s, *far = hidden_grads(chunk, blocks(*far_pairs), half, rows, *weights)
        far_up, far_down = up(far[0]), down(far[1])
        grads, after = (rows, hid, da, db), ()
        if before:
            dx, left = lax.optimization_barrier((dx, mark(chunk, *far)))
            after = [left]
            dx = input_grads(chunk, local_exp, capacity, da, db, s, w_gate, w_up, dx)
            back = swap(dx)
            rows, _, *last = lax.optimization_barrier((rows, dx, *before[-1]))
            grads = (rows, hid, da, db)
        if chunk + 1 < local_exp:
            following, *after = lax.optimization_barrier((sends[chunk + 1], mark(chunk, *far)))
            following = swap_rows(following)
        near = weight_grads(f"near{chunk}", chunk, blocks(*near_pairs), 2, half, *grads, after=after)
        near_up, near_down = up(near[0]), down(near[1])
        far_up, far_down, _ = lax.optimization_barrier((far_up, far_down, near[0]))
        sum_up = weight_grads(f"up{chunk}", chunk, blocks((1, 0)), 1, half, *grads, far_up)[0]
        sum_down = weight_grads(f"down{chunk}", chunk, blocks((n_group - 1, 1)), 1, half, *grads, far_down)[0]
        if before:
            landed = before[1]
            *landed, sum_up, sum_down = lax.optimization_barrier((*landed, sum_up, sum_down))
            own = own_sum(chunk - 1, before[0], *landed)
            new = update(chunk - 1, where, decay_mask, (own[0], last[0], own[1], last[1]), weights, new)
        sent = [up(sum_up), down(sum_down)]
        if chunk + 1 < local_exp:
            dx = input_grads(chunk, local_exp, capacity, order(da, sum_up, sum_down), db, s, w_gate, w_up, dx)
            rows, dx, near_up, near_down = lax.optimization_barrier((following, dx, near_up, near_down))
            before = (grads, (near_up, near_down), sent)
    own = own_sum(local_exp - 1, grads, near_up, near_down)
    back, *own = lax.optimization_barrier((back, *own))
    new = update(
        local_exp - 1, where, decay_mask, (own[0], sent[0], own[1], sent[1]), weights, new
    )
    grad_tokens, grad_probs = combine(local_exp, capacity, ids_t, probs_t, back, width)
    grad_probs = grad_probs.T
    return (grad_tokens, grad_probs, *new)


def solution(mesh):
    placed = (
        P(("dp", "expert"), None),
        P(("dp", "expert"), None),
        P(("dp", "expert"), None),
        P(("dp", "expert"), None),
        P("expert", None, None),
        P("expert", None, None),
        P("expert", None, None),
        P("expert", None),
    )
    return jax.shard_map(
        body,
        mesh=mesh,
        in_specs=placed,
        out_specs=(
            P(("dp", "expert"), None),
            P(("dp", "expert"), None),
            P("expert", "dp", None),
            P("expert", "dp", None),
            P("expert", "dp", None),
        ),
        check_vma=False,
    )
```

```python
import functools

import jax
import jax.numpy as jnp
from jax import lax
from jax.experimental import pallas as pl
from jax.experimental.pallas import tpu as pltpu
from jax.sharding import PartitionSpec as P

step_size = 0.004
shrink_rate = 0.1
LANES = 128
F32 = jnp.float32
BF16 = jnp.bfloat16
VMEM_LIMIT = 60 * 1024 * 1024


def dot(a, b, dims):
    return lax.dot_general(a, b, (dims, ((), ())), preferred_element_type=F32)


def cost(flops, moved, chunk=1):
    scale = (7, 24)[min(chunk, 1)]
    return pl.CostEstimate(flops=scale * flops, transcendentals=0, bytes_accessed=scale * moved)


NN = ((1,), (0,))
NT = ((1,), (1,))
TN = ((0,), (0,))


def slot_values(ids_t, n_experts, capacity):
    topk, tok = ids_t.shape
    rows = lax.broadcasted_iota(jnp.int32, (n_experts, tok), 0)
    hit = ids_t[0:1, :] == rows
    for k in range(1, topk):
        hit = jnp.logical_or(hit, ids_t[k : k + 1, :] == rows)
    hit_f = jnp.where(hit, 1.0, 0.0)
    earlier = lax.broadcasted_iota(jnp.int32, (tok, tok), 0) < lax.broadcasted_iota(
        jnp.int32, (tok, tok), 1
    )
    count = dot(hit_f.astype(BF16), jnp.where(earlier, 1.0, 0.0).astype(BF16), NN)
    return jnp.where(jnp.logical_and(hit, count < capacity), count, -1.0)


def slot_rows(values, chunk, local_exp, capacity):
    n_experts, tok = values.shape
    n_rows = n_experts // local_exp * capacity
    expert_of = lax.broadcasted_iota(jnp.int32, (n_rows, n_experts), 0) // capacity * local_exp + chunk
    spread = jnp.where(expert_of == lax.broadcasted_iota(jnp.int32, (n_rows, n_experts), 1), 1.0, 0.0)
    spread = spread.astype(BF16)
    at = dot(spread, values.astype(BF16), NN)
    place = (lax.broadcasted_iota(jnp.int32, (n_rows, tok), 0) % capacity).astype(F32)
    return at == place, spread


def dispatch_kernel(chunk, local_exp, capacity, ids_ref, probs_ref, tok_ref, grad_ref, out_ref):
    ids_t = ids_ref[...]
    topk, tok = ids_t.shape
    n_experts = out_ref.shape[0] // capacity * local_exp
    width = tok_ref.shape[1]
    values = slot_values(ids_t, n_experts, capacity)
    rows = lax.broadcasted_iota(jnp.int32, (n_experts, tok), 0)
    prob = jnp.zeros((n_experts, tok), F32)
    for k in range(topk):
        prob = prob + jnp.where(ids_t[k : k + 1, :] == rows, probs_ref[k : k + 1, :].astype(F32), 0.0)
    onehot, spread = slot_rows(values, chunk, local_exp, capacity)
    prob_rows = dot(spread, prob.astype(BF16), NN)
    pick = jnp.where(onehot, 1.0, 0.0).astype(BF16)
    weighted = jnp.where(onehot, prob_rows, 0.0).astype(BF16)
    out_ref[:, :width] = dot(pick, tok_ref[...], NN).astype(BF16)
    out_ref[:, width:] = dot(weighted, grad_ref[...], NN).astype(BF16)


def dispatch(chunk, local_exp, capacity, n_experts, ids_t, probs_t, tokens, out_grad):
    tok, width = tokens.shape
    n_rows = n_experts // local_exp * capacity
    return pl.pallas_call(
        functools.partial(dispatch_kernel, chunk, local_exp, capacity),
        out_shape=jax.ShapeDtypeStruct((n_rows, 2 * width), BF16),
        compiler_params=pltpu.CompilerParams(vmem_limit_bytes=VMEM_LIMIT),
        cost_estimate=cost(4 * n_rows * tok * width, 4 * width * (tok + n_rows), 0),
        name=f"dispatch{chunk}",
    )(ids_t, probs_t, tokens, out_grad)


def hidden_kernel(
    where_ref, x_ref, do_ref, xa_ref, xb_ref, da_col_ref, db_col_ref, wg_ref, wu_ref, wd_ref,
    hid_ref, da_ref, db_ref, s_ref, a_ref, b_ref, sum_ref,
):
    step = pl.program_id(0)
    gate = dot(x_ref[...], wg_ref[0], NN)
    upper = dot(x_ref[...], wu_ref[0], NN)
    sig = jax.nn.sigmoid(gate)
    act = gate * sig
    hid = (act * upper).astype(BF16)
    hid_ref[...] = hid
    dhid = dot(do_ref[...], wd_ref[0], NN)
    part = jnp.sum(hid.astype(F32) * dhid, axis=1, keepdims=True)
    dgate = (dhid * upper * sig * (1.0 + gate * (1.0 - sig))).astype(BF16)
    dup = (dhid * act).astype(BF16)
    da_ref[...] = dgate
    db_ref[...] = dup
    for out_ref, x_col, do_col in ((a_ref, xa_ref, da_col_ref), (b_ref, xb_ref, db_col_ref)):
        out_ref[0] = dot(x_col[...], dgate, TN).astype(BF16)
        out_ref[1] = dot(x_col[...], dup, TN).astype(BF16)
        out_ref[2] = dot(do_col[...], hid, TN).astype(BF16)

    @pl.when(step == 0)
    def _():
        sum_ref[...] = jnp.broadcast_to(part, sum_ref.shape)

    @pl.when(step > 0)
    def _():
        sum_ref[...] = sum_ref[...] + part

    @pl.when(step == pl.num_programs(0) - 1)
    def _():
        total = sum_ref[...]
        high = total.astype(BF16).astype(F32)
        lane = lax.broadcasted_iota(jnp.int32, s_ref.shape, 1)
        s_ref[...] = jnp.where(lane == 0, high, jnp.where(lane == 1, total - high, 0.0)).astype(BF16)


def whole(shape):
    return pl.BlockSpec(shape, lambda *_: (0,) * len(shape), pipeline_mode=pl.Buffered(1))


def hidden_grads(chunk, where, half, rows, wg, wu, wd):
    n_rows, width = rows.shape[0], rows.shape[1] // 2
    hidden = wg.shape[2]
    block = 2 * LANES
    lefts = width // half
    once = pl.Buffered(1)
    weight = pl.BlockSpec((1, width, block), lambda i, at: (chunk, 0, i))
    result = pl.BlockSpec((n_rows, block), lambda i, at: (0, i))
    shard = pl.BlockSpec((3, half, block), lambda i, at: (0, 0, i))
    return pl.pallas_call(
        hidden_kernel,
        grid_spec=pltpu.PrefetchScalarGridSpec(
            num_scalar_prefetch=1,
            grid=(hidden // block,),
            in_specs=[
                pl.BlockSpec((n_rows, width), lambda i, at: (0, 0), pipeline_mode=once),
                pl.BlockSpec((n_rows, width), lambda i, at: (0, 1), pipeline_mode=once),
                pl.BlockSpec((n_rows, half), lambda i, at: (0, at[0]), pipeline_mode=once),
                pl.BlockSpec((n_rows, half), lambda i, at: (0, at[1]), pipeline_mode=once),
                pl.BlockSpec((n_rows, half), lambda i, at: (0, at[0] + lefts), pipeline_mode=once),
                pl.BlockSpec((n_rows, half), lambda i, at: (0, at[1] + lefts), pipeline_mode=once),
                weight,
                weight,
                weight,
            ],
            out_specs=[result] * 3 + [whole((n_rows, LANES)), shard, shard],
            scratch_shapes=[pltpu.VMEM((n_rows, LANES), F32)],
        ),
        out_shape=[jax.ShapeDtypeStruct((n_rows, hidden), BF16)] * 3
        + [jax.ShapeDtypeStruct((n_rows, LANES), BF16)]
        + [jax.ShapeDtypeStruct((3, half, hidden), BF16)] * 2,
        compiler_params=pltpu.CompilerParams(vmem_limit_bytes=VMEM_LIMIT),
        cost_estimate=cost(8 * n_rows * width * hidden, 6 * width * hidden + n_rows * (4 * width + 6 * hidden), chunk),
        name=f"hidden{chunk}",
    )(where, *[rows] * 6, wg, wu, wd)


def weight_kernel(n_add, n_after, where_ref, x_ref, do_ref, hid_ref, da_ref, db_ref, *refs):
    adds, outs = refs[:n_add], refs[n_add + n_after :]
    for m, (left, right) in enumerate(((x_ref, da_ref), (x_ref, db_ref), (do_ref, hid_ref))):
        part = dot(left[...], right[...], TN)
        for addend in adds:
            part = part + addend[m].astype(F32)
        for i, out_ref in enumerate(outs):

            @pl.when(pl.program_id(0) == i)
            def _():
                out_ref[m] = part.astype(BF16)


def weight_grads(name, chunk, where, count, half, rows, hid, da, db, *adds, after=()):
    n_rows, width = rows.shape[0], rows.shape[1] // 2
    hidden = hid.shape[1]
    lefts = width // half
    shape = (3, half, hidden)
    return pl.pallas_call(
        functools.partial(weight_kernel, len(adds), len(after)),
        grid_spec=pltpu.PrefetchScalarGridSpec(
            num_scalar_prefetch=1,
            grid=(count,),
            in_specs=[
                pl.BlockSpec((n_rows, half), lambda i, at: (0, at[i])),
                pl.BlockSpec((n_rows, half), lambda i, at: (0, at[i] + lefts)),
            ]
            + [whole(a.shape) for a in (hid, da, db, *adds)]
            + [pl.BlockSpec(memory_space=pl.ANY)] * len(after),
            out_specs=[whole(shape)] * count,
        ),
        out_shape=[jax.ShapeDtypeStruct(shape, BF16)] * count,
        compiler_params=pltpu.CompilerParams(vmem_limit_bytes=VMEM_LIMIT),
        cost_estimate=cost(6 * count * n_rows * half * hidden, 6 * n_rows * hidden + 6 * count * half * hidden, chunk),
        name=name,
    )(where, rows, rows, hid, da, db, *adds, *after)


def mark_kernel(a_ref, b_ref, out_ref):
    out_ref[...] = a_ref[0] + b_ref[0]


def mark(chunk, first, second):
    corner = pl.BlockSpec((1, 16, LANES), lambda i: (0, 0, 0))
    return pl.pallas_call(
        mark_kernel,
        grid=(1,),
        in_specs=[corner, corner],
        out_specs=pl.BlockSpec((16, LANES), lambda i: (0, 0)),
        out_shape=jax.ShapeDtypeStruct((16, LANES), BF16),
        cost_estimate=cost(5 * 3 * first.size, 5 * 3 * first.size, chunk),
        name=f"mark{chunk}",
    )(first, second)


def update_kernel(chunk, where_ref, mask_ref, *refs):
    grads, weights = refs[:4], refs[4:7]
    outs = refs[-3:]
    for second in range(2):

        @pl.when(pl.program_id(0) == second)
        def _():
            for m in range(3):
                grad = sum(g[m].astype(F32) for g in grads[2 * second : 2 * second + 2])
                weight = weights[m][0].astype(F32)
                rate = mask_ref[chunk, m].astype(F32)
                outs[m][0] = (weight - step_size * grad - shrink_rate * rate * weight).astype(BF16)


def update(chunk, where, mask, grads, weights, into):
    _, half, hidden = grads[0].shape
    local = weights[0].shape[0]
    steps = 2
    block = half // steps
    early = pl.BlockSpec((3, block, hidden), lambda h, r, w: (0, r * (1 - h) + (steps - 1) * h, 0))
    late = pl.BlockSpec((3, block, hidden), lambda h, r, w: (0, r * h, 0))
    weight = pl.BlockSpec((1, block, hidden), lambda h, r, w: (chunk, (2 * w[0] + h) * steps + r, 0))
    result = pl.BlockSpec((1, block, hidden), lambda h, r, w: (chunk, h * steps + r, 0))
    extra = list(into or [])
    return pl.pallas_call(
        functools.partial(update_kernel, chunk),
        grid_spec=pltpu.PrefetchScalarGridSpec(
            num_scalar_prefetch=1,
            grid=(2, steps),
            in_specs=[pl.BlockSpec(memory_space=pltpu.SMEM)]
            + [early] * 2
            + [late] * 2
            + [weight] * 3
            + [pl.BlockSpec(memory_space=pl.ANY)] * len(extra),
            out_specs=[result] * 3,
        ),
        out_shape=[jax.ShapeDtypeStruct((local, 2 * half, hidden), BF16)] * 3,
        input_output_aliases={9 + i: i for i in range(len(extra))},
        compiler_params=pltpu.CompilerParams(vmem_limit_bytes=VMEM_LIMIT),
        cost_estimate=cost(10 * half * hidden, 60 * half * hidden),
        name=f"update{chunk}",
    )(where, mask, *grads, *weights, *extra)


def dx_kernel(da_ref, db_ref, s_ref, wg_ref, wu_ref, *refs):
    out_ref = refs[-1]
    n_owner, capacity, block = out_ref.shape
    last = pl.num_programs(0) - 1

    @pl.when(pl.program_id(0) < last)
    def _():
        dx = dot(da_ref[...], wg_ref[0], NT) + dot(db_ref[...], wu_ref[0], NT)
        out_ref[...] = dx.astype(BF16).reshape(n_owner, capacity, block)

    @pl.when(pl.program_id(0) == last)
    def _():
        out_ref[:, :, :LANES] = s_ref[...].reshape(n_owner, capacity, LANES)


def input_grads(chunk, local_exp, capacity, da, db, s, wg, wu, into):
    n_rows, hidden = da.shape
    width = wg.shape[1]
    n_owner = n_rows // capacity
    block = width // 4
    weight = pl.BlockSpec((1, block, hidden), lambda i: (chunk, jnp.minimum(i, 3), 0))
    extra = [] if into is None else [into]
    return pl.pallas_call(
        dx_kernel,
        grid=(5,),
        in_specs=[whole((n_rows, hidden)), whole((n_rows, hidden)), whole((n_rows, LANES)), weight, weight]
        + [pl.BlockSpec(memory_space=pl.ANY)] * len(extra),
        out_specs=pl.BlockSpec((n_owner, capacity, block), lambda i: (0, chunk, i)),
        out_shape=jax.ShapeDtypeStruct((n_owner, local_exp * capacity, width + LANES), BF16),
        input_output_aliases={5: 0} if extra else {},
        compiler_params=pltpu.CompilerParams(vmem_limit_bytes=VMEM_LIMIT),
        cost_estimate=cost(4 * n_rows * width * hidden, 4 * width * hidden + 2 * n_rows * (width + 2 * hidden), chunk),
        name=f"dx{chunk}",
    )(da, db, s, wg, wu, *extra)


def combine_kernel(local_exp, capacity, ids_ref, probs_ref, back_ref, tok_ref, prob_ref):
    ids_t = ids_ref[...]
    topk, tok = ids_t.shape
    n_rows = back_ref.shape[0] * capacity
    n_experts = back_ref.shape[0] * local_exp
    width = tok_ref.shape[1]
    values = slot_values(ids_t, n_experts, capacity)
    total = jnp.zeros((tok, width), F32)
    by_expert = jnp.zeros((n_experts, tok), F32)
    for chunk in range(local_exp):
        onehot, spread = slot_rows(values, chunk, local_exp, capacity)
        pick = jnp.where(onehot, 1.0, 0.0)
        slots = slice(chunk * capacity, (chunk + 1) * capacity)
        dx = back_ref[:, slots, :width].reshape(n_rows, width)
        total = total + dot(pick.astype(BF16), dx, TN)
        s = back_ref[:, slots, width:].reshape(n_rows, LANES).astype(F32)
        placed = pick * (s[:, 0:1] + s[:, 1:2])
        high = placed.astype(BF16)
        low = (placed - high.astype(F32)).astype(BF16)
        by_expert = by_expert + dot(spread, high, TN) + dot(spread, low, TN)
    tok_ref[...] = total.astype(BF16)
    rows = lax.broadcasted_iota(jnp.int32, (n_experts, tok), 0)
    for k in range(topk):
        mine = jnp.where(ids_t[k : k + 1, :] == rows, by_expert, 0.0)
        score = jnp.sum(mine, axis=0, keepdims=True)
        prob_ref[k : k + 1, :] = (score / probs_ref[k : k + 1, :].astype(F32)).astype(BF16)


def combine(local_exp, capacity, ids_t, probs_t, back, width):
    topk, tok = ids_t.shape
    return pl.pallas_call(
        functools.partial(combine_kernel, local_exp, capacity),
        out_shape=[
            jax.ShapeDtypeStruct((tok, width), BF16),
            jax.ShapeDtypeStruct((topk, tok), BF16),
        ],
        compiler_params=pltpu.CompilerParams(vmem_limit_bytes=VMEM_LIMIT),
        cost_estimate=cost(2 * back.shape[0] * back.shape[1] * tok * width, 2 * back.size),
        name="combine",
    )(ids_t, probs_t, back)


def body(tokens, out_grad, expert_ids, route_probs, w_gate, w_up, w_down, decay_mask):
    n_owner = lax.axis_size("expert")
    n_group = lax.axis_size("dp")
    local_exp = w_gate.shape[0]
    width = tokens.shape[1]
    tok_rows, topk = expert_ids.shape
    n_experts = n_owner * local_exp
    capacity = tok_rows * topk // n_experts
    ids_t = expert_ids.T
    probs_t = route_probs.T
    half = width // n_group // 2
    plane = lax.axis_index("dp").astype(jnp.int32)
    where = plane.reshape(1)

    def half_shard(ahead, second):
        return 2 * ((plane + ahead) % n_group) + second

    def blocks(*pairs):
        return jnp.stack([half_shard(*pair) for pair in pairs]).astype(jnp.int32)

    def up(a):
        return lax.ppermute(a, "dp", [(i, (i + 1) % n_group) for i in range(n_group)])

    def down(a):
        return lax.ppermute(a, "dp", [(i, (i - 1) % n_group) for i in range(n_group)])

    def send(chunk):
        return dispatch(chunk, local_exp, capacity, n_experts, ids_t, probs_t, tokens, out_grad)

    def swap(a):
        return lax.all_to_all(a, "expert", split_axis=0, concat_axis=0, tiled=True)

    def swap_rows(a):
        a = a.reshape(n_owner, capacity, a.shape[1])
        return swap(a).reshape(n_owner * capacity, a.shape[2])

    def order(value, *after):
        return lax.optimization_barrier((value, *after))[0]

    def own_sum(chunk, grads, near_up, near_down):
        return [
            weight_grads(f"own{chunk}{second}", chunk, blocks((0, second)), 1, half, *grads, landed)[0]
            for second, landed in enumerate((near_down, near_up))
        ]

    weights = (w_gate, w_up, w_down)
    far_pairs = ((2, 0), (2, 1))
    near_pairs = ((1, 1), (n_group - 1, 0))
    new, dx, before = None, None, None
    sends = [send(chunk) for chunk in range(local_exp)]
    rows = order(swap_rows(sends[0]), *sends[1:])
    for chunk in range(local_exp):
        hid, da, db, s, *far = hidden_grads(chunk, blocks(*far_pairs), half, rows, *weights)
        far_up, far_down = up(far[0]), down(far[1])
        grads, after = (rows, hid, da, db), ()
        if before:
            dx, left = lax.optimization_barrier((dx, mark(chunk, *far)))
            after = [left]
            dx = input_grads(chunk, local_exp, capacity, da, db, s, w_gate, w_up, dx)
            back = swap(dx)
            rows, _, *last = lax.optimization_barrier((rows, dx, *before[-1]))
            grads = (rows, hid, da, db)
        if chunk + 1 < local_exp:
            following, *after = lax.optimization_barrier((sends[chunk + 1], mark(chunk, *far)))
            following = swap_rows(following)
        near = weight_grads(f"near{chunk}", chunk, blocks(*near_pairs), 2, half, *grads, after=after)
        near_up, near_down = up(near[0]), down(near[1])
        far_up, far_down, _ = lax.optimization_barrier((far_up, far_down, near[0]))
        sum_up = weight_grads(f"up{chunk}", chunk, blocks((1, 0)), 1, half, *grads, far_up)[0]
        sum_down = weight_grads(f"down{chunk}", chunk, blocks((n_group - 1, 1)), 1, half, *grads, far_down)[0]
        if before:
            landed = before[1]
            *landed, sum_up, sum_down = lax.optimization_barrier((*landed, sum_up, sum_down))
            own = own_sum(chunk - 1, before[0], *landed)
            new = update(chunk - 1, where, decay_mask, (own[0], last[0], own[1], last[1]), weights, new)
        sent = [up(sum_up), down(sum_down)]
        if chunk + 1 < local_exp:
            dx = input_grads(chunk, local_exp, capacity, order(da, sum_up, sum_down), db, s, w_gate, w_up, dx)
            rows, dx, near_up, near_down = lax.optimization_barrier((following, dx, near_up, near_down))
            before = (grads, (near_up, near_down), sent)
    own = own_sum(local_exp - 1, grads, near_up, near_down)
    back, *own = lax.optimization_barrier((back, *own))
    new = update(
        local_exp - 1, where, decay_mask, (own[0], sent[0], own[1], sent[1]), weights, new
    )
    grad_tokens, grad_probs = combine(local_exp, capacity, ids_t, probs_t, back, width)
    grad_probs = grad_probs.T
    return (grad_tokens, grad_probs, *new)


def solution(mesh):
    placed = (
        P(("dp", "expert"), None),
        P(("dp", "expert"), None),
        P(("dp", "expert"), None),
        P(("dp", "expert"), None),
        P("expert", None, None),
        P("expert", None, None),
        P("expert", None, None),
        P("expert", None),
    )
    return jax.shard_map(
        body,
        mesh=mesh,
        in_specs=placed,
        out_specs=(
            P(("dp", "expert"), None),
            P(("dp", "expert"), None),
            P("expert", "dp", None),
            P("expert", "dp", None),
            P("expert", "dp", None),
        ),
        check_vma=False,
    )
```

```python
import functools

import jax
import jax.numpy as jnp
from jax import lax
from jax.experimental import pallas as pl
from jax.experimental.pallas import tpu as pltpu
from jax.sharding import PartitionSpec as P

step_size = 0.004
shrink_rate = 0.1
LANES = 128
F32 = jnp.float32
BF16 = jnp.bfloat16
VMEM_LIMIT = 60 * 1024 * 1024


def dot(a, b, dims):
    return lax.dot_general(a, b, (dims, ((), ())), preferred_element_type=F32)


def cost(flops, moved, chunk=1):
    scale = (7, 24)[min(chunk, 1)]
    return pl.CostEstimate(flops=scale * flops, transcendentals=0, bytes_accessed=scale * moved)


NN = ((1,), (0,))
NT = ((1,), (1,))
TN = ((0,), (0,))


def slot_values(ids_t, n_experts, capacity):
    topk, tok = ids_t.shape
    rows = lax.broadcasted_iota(jnp.int32, (n_experts, tok), 0)
    hit = ids_t[0:1, :] == rows
    for k in range(1, topk):
        hit = jnp.logical_or(hit, ids_t[k : k + 1, :] == rows)
    hit_f = jnp.where(hit, 1.0, 0.0)
    earlier = lax.broadcasted_iota(jnp.int32, (tok, tok), 0) < lax.broadcasted_iota(
        jnp.int32, (tok, tok), 1
    )
    count = dot(hit_f.astype(BF16), jnp.where(earlier, 1.0, 0.0).astype(BF16), NN)
    return jnp.where(jnp.logical_and(hit, count < capacity), count, -1.0)


def slot_rows(values, chunk, local_exp, capacity):
    n_experts, tok = values.shape
    n_rows = n_experts // local_exp * capacity
    expert_of = lax.broadcasted_iota(jnp.int32, (n_rows, n_experts), 0) // capacity * local_exp + chunk
    spread = jnp.where(expert_of == lax.broadcasted_iota(jnp.int32, (n_rows, n_experts), 1), 1.0, 0.0)
    spread = spread.astype(BF16)
    at = dot(spread, values.astype(BF16), NN)
    place = (lax.broadcasted_iota(jnp.int32, (n_rows, tok), 0) % capacity).astype(F32)
    return at == place, spread


def dispatch_kernel(chunk, local_exp, capacity, ids_ref, probs_ref, tok_ref, grad_ref, out_ref):
    ids_t = ids_ref[...]
    topk, tok = ids_t.shape
    n_experts = out_ref.shape[0] // capacity * local_exp
    width = tok_ref.shape[1]
    values = slot_values(ids_t, n_experts, capacity)
    rows = lax.broadcasted_iota(jnp.int32, (n_experts, tok), 0)
    prob = jnp.zeros((n_experts, tok), F32)
    for k in range(topk):
        prob = prob + jnp.where(ids_t[k : k + 1, :] == rows, probs_ref[k : k + 1, :].astype(F32), 0.0)
    onehot, spread = slot_rows(values, chunk, local_exp, capacity)
    prob_rows = dot(spread, prob.astype(BF16), NN)
    pick = jnp.where(onehot, 1.0, 0.0).astype(BF16)
    weighted = jnp.where(onehot, prob_rows, 0.0).astype(BF16)
    out_ref[:, :width] = dot(pick, tok_ref[...], NN).astype(BF16)
    out_ref[:, width:] = dot(weighted, grad_ref[...], NN).astype(BF16)


def dispatch(chunk, local_exp, capacity, n_experts, ids_t, probs_t, tokens, out_grad):
    tok, width = tokens.shape
    n_rows = n_experts // local_exp * capacity
    return pl.pallas_call(
        functools.partial(dispatch_kernel, chunk, local_exp, capacity),
        out_shape=jax.ShapeDtypeStruct((n_rows, 2 * width), BF16),
        compiler_params=pltpu.CompilerParams(vmem_limit_bytes=VMEM_LIMIT),
        cost_estimate=cost(4 * n_rows * tok * width, 4 * width * (tok + n_rows), 0),
        name=f"dispatch{chunk}",
    )(ids_t, probs_t, tokens, out_grad)


def hidden_kernel(
    where_ref, x_ref, do_ref, xa_ref, xb_ref, da_col_ref, db_col_ref, wg_ref, wu_ref, wd_ref,
    hid_ref, da_ref, db_ref, s_ref, a_ref, b_ref, sum_ref,
):
    step = pl.program_id(0)
    gate = dot(x_ref[...], wg_ref[0], NN)
    upper = dot(x_ref[...], wu_ref[0], NN)
    sig = jax.nn.sigmoid(gate)
    act = gate * sig
    hid = (act * upper).astype(BF16)
    hid_ref[...] = hid
    dhid = dot(do_ref[...], wd_ref[0], NN)
    part = jnp.sum(hid.astype(F32) * dhid, axis=1, keepdims=True)
    dgate = (dhid * upper * sig * (1.0 + gate * (1.0 - sig))).astype(BF16)
    dup = (dhid * act).astype(BF16)
    da_ref[...] = dgate
    db_ref[...] = dup
    for out_ref, x_col, do_col in ((a_ref, xa_ref, da_col_ref), (b_ref, xb_ref, db_col_ref)):
        out_ref[0] = dot(x_col[...], dgate, TN).astype(BF16)
        out_ref[1] = dot(x_col[...], dup, TN).astype(BF16)
        out_ref[2] = dot(do_col[...], hid, TN).astype(BF16)

    @pl.when(step == 0)
    def _():
        sum_ref[...] = jnp.broadcast_to(part, sum_ref.shape)

    @pl.when(step > 0)
    def _():
        sum_ref[...] = sum_ref[...] + part

    @pl.when(step == pl.num_programs(0) - 1)
    def _():
        total = sum_ref[...]
        high = total.astype(BF16).astype(F32)
        lane = lax.broadcasted_iota(jnp.int32, s_ref.shape, 1)
        s_ref[...] = jnp.where(lane == 0, high, jnp.where(lane == 1, total - high, 0.0)).astype(BF16)


def whole(shape):
    return pl.BlockSpec(shape, lambda *_: (0,) * len(shape), pipeline_mode=pl.Buffered(1))


def hidden_grads(chunk, where, half, rows, wg, wu, wd):
    n_rows, width = rows.shape[0], rows.shape[1] // 2
    hidden = wg.shape[2]
    block = 2 * LANES
    lefts = width // half
    once = pl.Buffered(1)
    weight = pl.BlockSpec((1, width, block), lambda i, at: (chunk, 0, i))
    result = pl.BlockSpec((n_rows, block), lambda i, at: (0, i))
    shard = pl.BlockSpec((3, half, block), lambda i, at: (0, 0, i))
    return pl.pallas_call(
        hidden_kernel,
        grid_spec=pltpu.PrefetchScalarGridSpec(
            num_scalar_prefetch=1,
            grid=(hidden // block,),
            in_specs=[
                pl.BlockSpec((n_rows, width), lambda i, at: (0, 0), pipeline_mode=once),
                pl.BlockSpec((n_rows, width), lambda i, at: (0, 1), pipeline_mode=once),
                pl.BlockSpec((n_rows, half), lambda i, at: (0, at[0]), pipeline_mode=once),
                pl.BlockSpec((n_rows, half), lambda i, at: (0, at[1]), pipeline_mode=once),
                pl.BlockSpec((n_rows, half), lambda i, at: (0, at[0] + lefts), pipeline_mode=once),
                pl.BlockSpec((n_rows, half), lambda i, at: (0, at[1] + lefts), pipeline_mode=once),
                weight,
                weight,
                weight,
            ],
            out_specs=[result] * 3 + [whole((n_rows, LANES)), shard, shard],
            scratch_shapes=[pltpu.VMEM((n_rows, LANES), F32)],
        ),
        out_shape=[jax.ShapeDtypeStruct((n_rows, hidden), BF16)] * 3
        + [jax.ShapeDtypeStruct((n_rows, LANES), BF16)]
        + [jax.ShapeDtypeStruct((3, half, hidden), BF16)] * 2,
        compiler_params=pltpu.CompilerParams(vmem_limit_bytes=VMEM_LIMIT),
        cost_estimate=cost(8 * n_rows * width * hidden, 6 * width * hidden + n_rows * (4 * width + 6 * hidden), chunk),
        name=f"hidden{chunk}",
    )(where, *[rows] * 6, wg, wu, wd)


def hidden_part_kernel(
    first, last, where_ref, x_ref, do_ref, xa_ref, xb_ref, da_col_ref, db_col_ref, wg_ref, wu_ref, wd_ref, *refs
):
    hid_ref, da_ref, db_ref, s_ref, a_ref, b_ref = refs[-6:]
    gate = dot(x_ref[...], wg_ref[0], NN)
    upper = dot(x_ref[...], wu_ref[0], NN)
    sig = jax.nn.sigmoid(gate)
    act = gate * sig
    hid = (act * upper).astype(BF16)
    hid_ref[...] = hid
    dhid = dot(do_ref[...], wd_ref[0], NN)
    total = jnp.broadcast_to(jnp.sum(hid.astype(F32) * dhid, axis=1, keepdims=True), s_ref.shape)
    dgate = (dhid * upper * sig * (1.0 + gate * (1.0 - sig))).astype(BF16)
    dup = (dhid * act).astype(BF16)
    da_ref[...] = dgate
    db_ref[...] = dup
    for out_ref, x_col, do_col in ((a_ref, xa_ref, da_col_ref), (b_ref, xb_ref, db_col_ref)):
        out_ref[0] = dot(x_col[...], dgate, TN).astype(BF16)
        out_ref[1] = dot(x_col[...], dup, TN).astype(BF16)
        out_ref[2] = dot(do_col[...], hid, TN).astype(BF16)
    if not first:
        total = total + refs[0][...]
    if last:
        high = total.astype(BF16).astype(F32)
        lane = lax.broadcasted_iota(jnp.int32, s_ref.shape, 1)
        total = jnp.where(lane == 0, high, jnp.where(lane == 1, total - high, 0.0))
    s_ref[...] = total.astype(s_ref.dtype)


def hidden_parts(chunk, where, half, rows, wg, wu, wd, sent):
    n_rows, width = rows.shape[0], rows.shape[1] // 2
    hidden = wg.shape[2]
    block = 2 * LANES
    lefts = width // half
    parts = hidden // block
    once = pl.Buffered(1)
    shard = jax.ShapeDtypeStruct((3, half, block), BF16)
    kept, total, pairs = [], None, []
    for part in range(parts):
        first, last = part == 0, part + 1 == parts
        if last and len(pairs) > 1:
            total, *pairs[0] = lax.optimization_barrier((total, *pairs[0]))
        extra = [] if first else [total]
        result = pl.BlockSpec((n_rows, block), lambda i, at, part=part: (0, part), pipeline_mode=once)
        weight = pl.BlockSpec((1, width, block), lambda i, at, part=part: (chunk, 0, part), pipeline_mode=once)
        *kept, total, a, b = pl.pallas_call(
            functools.partial(hidden_part_kernel, first, last),
            grid_spec=pltpu.PrefetchScalarGridSpec(
                num_scalar_prefetch=1,
                grid=(1,),
                in_specs=[
                    pl.BlockSpec((n_rows, width), lambda i, at: (0, 0), pipeline_mode=once),
                    pl.BlockSpec((n_rows, width), lambda i, at: (0, 1), pipeline_mode=once),
                    pl.BlockSpec((n_rows, half), lambda i, at: (0, at[0]), pipeline_mode=once),
                    pl.BlockSpec((n_rows, half), lambda i, at: (0, at[1]), pipeline_mode=once),
                    pl.BlockSpec((n_rows, half), lambda i, at: (0, at[0] + lefts), pipeline_mode=once),
                    pl.BlockSpec((n_rows, half), lambda i, at: (0, at[1] + lefts), pipeline_mode=once),
                    weight,
                    weight,
                    weight,
                ]
                + [whole((n_rows, LANES))] * len(extra)
                + [pl.BlockSpec(memory_space=pl.ANY)] * len(kept),
                out_specs=[result] * 3 + [whole((n_rows, LANES)), whole(shard.shape), whole(shard.shape)],
            ),
            out_shape=[jax.ShapeDtypeStruct((n_rows, hidden), BF16)] * 3
            + [jax.ShapeDtypeStruct((n_rows, LANES), BF16 if last else F32), shard, shard],
            input_output_aliases={11 + i: i for i in range(len(kept))},
            compiler_params=pltpu.CompilerParams(vmem_limit_bytes=VMEM_LIMIT),
            cost_estimate=cost(6 * n_rows * width * block, 6 * width * block, chunk),
            name=f"hidden{chunk}{part}",
        )(where, *[rows] * 6, wg, wu, wd, *extra, *kept)
        pairs.append(sent(a, b))
        if not last:
            early = (a, b)
    return (*kept, total, early, pairs)


def weight_kernel(n_add, n_after, where_ref, x_ref, do_ref, hid_ref, da_ref, db_ref, *refs):
    adds, outs = refs[:n_add], refs[n_add + n_after :]
    for m, (left, right) in enumerate(((x_ref, da_ref), (x_ref, db_ref), (do_ref, hid_ref))):
        part = dot(left[...], right[...], TN)
        pieces = [a[m] for a in adds if a.shape[2] < hid_ref.shape[1]]
        if pieces:
            part = part + jnp.concatenate(pieces, axis=1).astype(F32)
        for addend in adds[len(pieces) :]:
            part = part + addend[m].astype(F32)
        for i, out_ref in enumerate(outs):

            @pl.when(pl.program_id(0) == i)
            def _():
                out_ref[m] = part.astype(BF16)


def weight_grads(name, chunk, where, count, half, rows, hid, da, db, *adds, after=()):
    n_rows, width = rows.shape[0], rows.shape[1] // 2
    hidden = hid.shape[1]
    lefts = width // half
    shape = (3, half, hidden)
    return pl.pallas_call(
        functools.partial(weight_kernel, len(adds), len(after)),
        grid_spec=pltpu.PrefetchScalarGridSpec(
            num_scalar_prefetch=1,
            grid=(count,),
            in_specs=[
                pl.BlockSpec((n_rows, half), lambda i, at: (0, at[i])),
                pl.BlockSpec((n_rows, half), lambda i, at: (0, at[i] + lefts)),
            ]
            + [whole(a.shape) for a in (hid, da, db, *adds)]
            + [pl.BlockSpec(memory_space=pl.ANY)] * len(after),
            out_specs=[whole(shape)] * count,
        ),
        out_shape=[jax.ShapeDtypeStruct(shape, BF16)] * count,
        compiler_params=pltpu.CompilerParams(vmem_limit_bytes=VMEM_LIMIT),
        cost_estimate=cost(6 * count * n_rows * half * hidden, 6 * n_rows * hidden + 6 * count * half * hidden, chunk),
        name=name,
    )(where, rows, rows, hid, da, db, *adds, *after)


def mark_kernel(a_ref, b_ref, out_ref):
    out_ref[...] = a_ref[0] + b_ref[0]


def mark(chunk, first, second):
    corner = pl.BlockSpec((1, 16, LANES), lambda i: (0, 0, 0))
    return pl.pallas_call(
        mark_kernel,
        grid=(1,),
        in_specs=[corner, corner],
        out_specs=pl.BlockSpec((16, LANES), lambda i: (0, 0)),
        out_shape=jax.ShapeDtypeStruct((16, LANES), BF16),
        cost_estimate=cost(5 * 3 * first.size, 5 * 3 * first.size, chunk),
        name=f"mark{chunk}",
    )(first, second)


def update_kernel(chunk, where_ref, mask_ref, *refs):
    grads, weights = refs[:4], refs[4:7]
    outs = refs[-3:]
    for second in range(2):

        @pl.when(pl.program_id(0) == second)
        def _():
            for m in range(3):
                grad = sum(g[m].astype(F32) for g in grads[2 * second : 2 * second + 2])
                weight = weights[m][0].astype(F32)
                rate = mask_ref[chunk, m].astype(F32)
                outs[m][0] = (weight - step_size * grad - shrink_rate * rate * weight).astype(BF16)


def update(chunk, where, mask, grads, weights, into):
    _, half, hidden = grads[0].shape
    local = weights[0].shape[0]
    steps = 2
    block = half // steps
    early = pl.BlockSpec((3, block, hidden), lambda h, r, w: (0, r * (1 - h) + (steps - 1) * h, 0))
    late = pl.BlockSpec((3, block, hidden), lambda h, r, w: (0, r * h, 0))
    weight = pl.BlockSpec((1, block, hidden), lambda h, r, w: (chunk, (2 * w[0] + h) * steps + r, 0))
    result = pl.BlockSpec((1, block, hidden), lambda h, r, w: (chunk, h * steps + r, 0))
    extra = list(into or [])
    return pl.pallas_call(
        functools.partial(update_kernel, chunk),
        grid_spec=pltpu.PrefetchScalarGridSpec(
            num_scalar_prefetch=1,
            grid=(2, steps),
            in_specs=[pl.BlockSpec(memory_space=pltpu.SMEM)]
            + [early] * 2
            + [late] * 2
            + [weight] * 3
            + [pl.BlockSpec(memory_space=pl.ANY)] * len(extra),
            out_specs=[result] * 3,
        ),
        out_shape=[jax.ShapeDtypeStruct((local, 2 * half, hidden), BF16)] * 3,
        input_output_aliases={9 + i: i for i in range(len(extra))},
        compiler_params=pltpu.CompilerParams(vmem_limit_bytes=VMEM_LIMIT),
        cost_estimate=cost(10 * half * hidden, 60 * half * hidden),
        name=f"update{chunk}",
    )(where, mask, *grads, *weights, *extra)


def dx_kernel(da_ref, db_ref, s_ref, wg_ref, wu_ref, *refs):
    out_ref = refs[-1]
    n_owner, capacity, block = out_ref.shape
    last = pl.num_programs(0) - 1

    @pl.when(pl.program_id(0) < last)
    def _():
        dx = dot(da_ref[...], wg_ref[0], NT) + dot(db_ref[...], wu_ref[0], NT)
        out_ref[...] = dx.astype(BF16).reshape(n_owner, capacity, block)

    @pl.when(pl.program_id(0) == last)
    def _():
        out_ref[:, :, :LANES] = s_ref[...].reshape(n_owner, capacity, LANES)


def input_grads(chunk, local_exp, capacity, da, db, s, wg, wu, into):
    n_rows, hidden = da.shape
    width = wg.shape[1]
    n_owner = n_rows // capacity
    block = width // 4
    weight = pl.BlockSpec((1, block, hidden), lambda i: (chunk, jnp.minimum(i, 3), 0))
    extra = [] if into is None else [into]
    return pl.pallas_call(
        dx_kernel,
        grid=(5,),
        in_specs=[whole((n_rows, hidden)), whole((n_rows, hidden)), whole((n_rows, LANES)), weight, weight]
        + [pl.BlockSpec(memory_space=pl.ANY)] * len(extra),
        out_specs=pl.BlockSpec((n_owner, capacity, block), lambda i: (0, chunk, i)),
        out_shape=jax.ShapeDtypeStruct((n_owner, local_exp * capacity, width + LANES), BF16),
        input_output_aliases={5: 0} if extra else {},
        compiler_params=pltpu.CompilerParams(vmem_limit_bytes=VMEM_LIMIT),
        cost_estimate=cost(4 * n_rows * width * hidden, 4 * width * hidden + 2 * n_rows * (width + 2 * hidden), chunk),
        name=f"dx{chunk}",
    )(da, db, s, wg, wu, *extra)


def combine_kernel(local_exp, capacity, ids_ref, probs_ref, back_ref, tok_ref, prob_ref):
    ids_t = ids_ref[...]
    topk, tok = ids_t.shape
    n_rows = back_ref.shape[0] * capacity
    n_experts = back_ref.shape[0] * local_exp
    width = tok_ref.shape[1]
    values = slot_values(ids_t, n_experts, capacity)
    total = jnp.zeros((tok, width), F32)
    by_expert = jnp.zeros((n_experts, tok), F32)
    for chunk in range(local_exp):
        onehot, spread = slot_rows(values, chunk, local_exp, capacity)
        pick = jnp.where(onehot, 1.0, 0.0)
        slots = slice(chunk * capacity, (chunk + 1) * capacity)
        dx = back_ref[:, slots, :width].reshape(n_rows, width)
        total = total + dot(pick.astype(BF16), dx, TN)
        s = back_ref[:, slots, width:].reshape(n_rows, LANES).astype(F32)
        placed = pick * (s[:, 0:1] + s[:, 1:2])
        high = placed.astype(BF16)
        low = (placed - high.astype(F32)).astype(BF16)
        by_expert = by_expert + dot(spread, high, TN) + dot(spread, low, TN)
    tok_ref[...] = total.astype(BF16)
    rows = lax.broadcasted_iota(jnp.int32, (n_experts, tok), 0)
    for k in range(topk):
        mine = jnp.where(ids_t[k : k + 1, :] == rows, by_expert, 0.0)
        score = jnp.sum(mine, axis=0, keepdims=True)
        prob_ref[k : k + 1, :] = (score / probs_ref[k : k + 1, :].astype(F32)).astype(BF16)


def combine(local_exp, capacity, ids_t, probs_t, back, width):
    topk, tok = ids_t.shape
    return pl.pallas_call(
        functools.partial(combine_kernel, local_exp, capacity),
        out_shape=[
            jax.ShapeDtypeStruct((tok, width), BF16),
            jax.ShapeDtypeStruct((topk, tok), BF16),
        ],
        compiler_params=pltpu.CompilerParams(vmem_limit_bytes=VMEM_LIMIT),
        cost_estimate=cost(2 * back.shape[0] * back.shape[1] * tok * width, 2 * back.size),
        name="combine",
    )(ids_t, probs_t, back)


def body(tokens, out_grad, expert_ids, route_probs, w_gate, w_up, w_down, decay_mask):
    n_owner = lax.axis_size("expert")
    n_group = lax.axis_size("dp")
    local_exp = w_gate.shape[0]
    width = tokens.shape[1]
    tok_rows, topk = expert_ids.shape
    n_experts = n_owner * local_exp
    capacity = tok_rows * topk // n_experts
    ids_t = expert_ids.T
    probs_t = route_probs.T
    half = width // n_group // 2
    plane = lax.axis_index("dp").astype(jnp.int32)
    where = plane.reshape(1)

    def half_shard(ahead, second):
        return 2 * ((plane + ahead) % n_group) + second

    def blocks(*pairs):
        return jnp.stack([half_shard(*pair) for pair in pairs]).astype(jnp.int32)

    def up(a):
        return lax.ppermute(a, "dp", [(i, (i + 1) % n_group) for i in range(n_group)])

    def down(a):
        return lax.ppermute(a, "dp", [(i, (i - 1) % n_group) for i in range(n_group)])

    def send(chunk):
        return dispatch(chunk, local_exp, capacity, n_experts, ids_t, probs_t, tokens, out_grad)

    def swap(a):
        return lax.all_to_all(a, "expert", split_axis=0, concat_axis=0, tiled=True)

    def swap_rows(a):
        a = a.reshape(n_owner, capacity, a.shape[1])
        return swap(a).reshape(n_owner * capacity, a.shape[2])

    def order(value, *after):
        return lax.optimization_barrier((value, *after))[0]

    def own_sum(chunk, grads, near_up, near_down):
        return [
            weight_grads(f"own{chunk}{second}", chunk, blocks((0, second)), 1, half, *grads, landed)[0]
            for second, landed in enumerate((near_down, near_up))
        ]

    weights = (w_gate, w_up, w_down)
    far_pairs = ((2, 0), (2, 1))
    near_pairs = ((1, 1), (n_group - 1, 0))
    new, dx, before = None, None, None
    sends = [send(chunk) for chunk in range(local_exp)]
    rows = order(swap_rows(sends[0]), *sends[1:])
    for chunk in range(local_exp):
        if chunk:
            hid, da, db, s, *far = hidden_grads(chunk, blocks(*far_pairs), half, rows, *weights)
            far_up, far_down = [up(far[0])], [down(far[1])]
        else:
            hid, da, db, s, far, pairs = hidden_parts(
                chunk, blocks(*far_pairs), half, rows, *weights, lambda a, b: (up(a), down(b))
            )
            far_up, far_down = [pair[0] for pair in pairs], [pair[1] for pair in pairs]
        grads, after = (rows, hid, da, db), ()
        if before:
            dx, left = lax.optimization_barrier((dx, mark(chunk, *far)))
            after = [left]
            dx = input_grads(chunk, local_exp, capacity, da, db, s, w_gate, w_up, dx)
            back = swap(dx)
            rows, _, *last = lax.optimization_barrier((rows, dx, *before[-1]))
            grads = (rows, hid, da, db)
        if chunk + 1 < local_exp:
            following, *after = lax.optimization_barrier((sends[chunk + 1], mark(chunk, *far)))
            following = swap_rows(following)
        near = weight_grads(f"near{chunk}", chunk, blocks(*near_pairs), 2, half, *grads, after=after)
        near_up, near_down = up(near[0]), down(near[1])
        far_up, far_down, _ = lax.optimization_barrier((far_up, far_down, near[0]))
        sum_up = weight_grads(f"up{chunk}", chunk, blocks((1, 0)), 1, half, *grads, *far_up)[0]
        sum_down = weight_grads(f"down{chunk}", chunk, blocks((n_group - 1, 1)), 1, half, *grads, *far_down)[0]
        if before:
            landed = before[1]
            *landed, sum_up, sum_down = lax.optimization_barrier((*landed, sum_up, sum_down))
            own = own_sum(chunk - 1, before[0], *landed)
            new = update(chunk - 1, where, decay_mask, (own[0], last[0], own[1], last[1]), weights, new)
        sent = [up(sum_up), down(sum_down)]
        if chunk + 1 < local_exp:
            dx = input_grads(chunk, local_exp, capacity, order(da, sum_up, sum_down), db, s, w_gate, w_up, dx)
            rows, dx, near_up, near_down = lax.optimization_barrier((following, dx, near_up, near_down))
            before = (grads, (near_up, near_down), sent)
    own = own_sum(local_exp - 1, grads, near_up, near_down)
    back, *own = lax.optimization_barrier((back, *own))
    new = update(
        local_exp - 1, where, decay_mask, (own[0], sent[0], own[1], sent[1]), weights, new
    )
    grad_tokens, grad_probs = combine(local_exp, capacity, ids_t, probs_t, back, width)
    grad_probs = grad_probs.T
    return (grad_tokens, grad_probs, *new)


def solution(mesh):
    placed = (
        P(("dp", "expert"), None),
        P(("dp", "expert"), None),
        P(("dp", "expert"), None),
        P(("dp", "expert"), None),
        P("expert", None, None),
        P("expert", None, None),
        P("expert", None, None),
        P("expert", None),
    )
    return jax.shard_map(
        body,
        mesh=mesh,
        in_specs=placed,
        out_specs=(
            P(("dp", "expert"), None),
            P(("dp", "expert"), None),
            P("expert", "dp", None),
            P("expert", "dp", None),
            P("expert", "dp", None),
        ),
        check_vma=False,
    )
```

```python
import functools

import jax
import jax.numpy as jnp
from jax import lax
from jax.experimental import pallas as pl
from jax.experimental.pallas import tpu as pltpu
from jax.sharding import PartitionSpec as P

step_size = 0.004
shrink_rate = 0.1
LANES = 128
F32 = jnp.float32
BF16 = jnp.bfloat16
VMEM_LIMIT = 63 * 1024 * 1024


def dot(a, b, dims):
    return lax.dot_general(a, b, (dims, ((), ())), preferred_element_type=F32)


def cost(flops, moved, chunk=1):
    scale = (7, 24)[min(chunk, 1)]
    return pl.CostEstimate(flops=scale * flops, transcendentals=0, bytes_accessed=scale * moved)


NN = ((1,), (0,))
NT = ((1,), (1,))
TN = ((0,), (0,))


def slot_values(ids_t, n_experts, capacity):
    topk, tok = ids_t.shape
    rows = lax.broadcasted_iota(jnp.int32, (n_experts, tok), 0)
    hit = ids_t[0:1, :] == rows
    for k in range(1, topk):
        hit = jnp.logical_or(hit, ids_t[k : k + 1, :] == rows)
    hit_f = jnp.where(hit, 1.0, 0.0)
    earlier = lax.broadcasted_iota(jnp.int32, (tok, tok), 0) < lax.broadcasted_iota(
        jnp.int32, (tok, tok), 1
    )
    count = dot(hit_f.astype(BF16), jnp.where(earlier, 1.0, 0.0).astype(BF16), NN)
    return jnp.where(jnp.logical_and(hit, count < capacity), count, -1.0)


def slot_rows(values, chunk, local_exp, capacity):
    n_experts, tok = values.shape
    n_rows = n_experts // local_exp * capacity
    expert_of = lax.broadcasted_iota(jnp.int32, (n_rows, n_experts), 0) // capacity * local_exp + chunk
    spread = jnp.where(expert_of == lax.broadcasted_iota(jnp.int32, (n_rows, n_experts), 1), 1.0, 0.0)
    spread = spread.astype(BF16)
    at = dot(spread, values.astype(BF16), NN)
    place = (lax.broadcasted_iota(jnp.int32, (n_rows, tok), 0) % capacity).astype(F32)
    return at == place, spread


def dispatch_kernel(chunk, local_exp, capacity, ids_ref, probs_ref, tok_ref, grad_ref, out_ref):
    ids_t = ids_ref[...]
    topk, tok = ids_t.shape
    n_experts = out_ref.shape[0] // capacity * local_exp
    width = tok_ref.shape[1]
    values = slot_values(ids_t, n_experts, capacity)
    rows = lax.broadcasted_iota(jnp.int32, (n_experts, tok), 0)
    prob = jnp.zeros((n_experts, tok), F32)
    for k in range(topk):
        prob = prob + jnp.where(ids_t[k : k + 1, :] == rows, probs_ref[k : k + 1, :].astype(F32), 0.0)
    onehot, spread = slot_rows(values, chunk, local_exp, capacity)
    prob_rows = dot(spread, prob.astype(BF16), NN)
    pick = jnp.where(onehot, 1.0, 0.0).astype(BF16)
    weighted = jnp.where(onehot, prob_rows, 0.0).astype(BF16)
    out_ref[:, :width] = dot(pick, tok_ref[...], NN).astype(BF16)
    out_ref[:, width:] = dot(weighted, grad_ref[...], NN).astype(BF16)


def dispatch(chunk, local_exp, capacity, n_experts, ids_t, probs_t, tokens, out_grad):
    tok, width = tokens.shape
    n_rows = n_experts // local_exp * capacity
    return pl.pallas_call(
        functools.partial(dispatch_kernel, chunk, local_exp, capacity),
        out_shape=jax.ShapeDtypeStruct((n_rows, 2 * width), BF16),
        compiler_params=pltpu.CompilerParams(vmem_limit_bytes=VMEM_LIMIT),
        cost_estimate=cost(4 * n_rows * tok * width, 4 * width * (tok + n_rows), 0),
        name=f"dispatch{chunk}",
    )(ids_t, probs_t, tokens, out_grad)


def hidden_kernel(
    where_ref, x_ref, do_ref, xa_ref, xb_ref, da_col_ref, db_col_ref, wg_ref, wu_ref, wd_ref,
    hid_ref, da_ref, db_ref, s_ref, a_ref, b_ref, sum_ref,
):
    step = pl.program_id(0)
    gate = dot(x_ref[...], wg_ref[0], NN)
    upper = dot(x_ref[...], wu_ref[0], NN)
    sig = jax.nn.sigmoid(gate)
    act = gate * sig
    hid = (act * upper).astype(BF16)
    hid_ref[...] = hid
    dhid = dot(do_ref[...], wd_ref[0], NN)
    part = jnp.sum(hid.astype(F32) * dhid, axis=1, keepdims=True)
    dgate = (dhid * upper * sig * (1.0 + gate * (1.0 - sig))).astype(BF16)
    dup = (dhid * act).astype(BF16)
    da_ref[...] = dgate
    db_ref[...] = dup
    for out_ref, x_col, do_col in ((a_ref, xa_ref, da_col_ref), (b_ref, xb_ref, db_col_ref)):
        out_ref[0] = dot(x_col[...], dgate, TN).astype(BF16)
        out_ref[1] = dot(x_col[...], dup, TN).astype(BF16)
        out_ref[2] = dot(do_col[...], hid, TN).astype(BF16)

    @pl.when(step == 0)
    def _():
        sum_ref[...] = jnp.broadcast_to(part, sum_ref.shape)

    @pl.when(step > 0)
    def _():
        sum_ref[...] = sum_ref[...] + part

    @pl.when(step == pl.num_programs(0) - 1)
    def _():
        total = sum_ref[...]
        high = total.astype(BF16).astype(F32)
        lane = lax.broadcasted_iota(jnp.int32, s_ref.shape, 1)
        s_ref[...] = jnp.where(lane == 0, high, jnp.where(lane == 1, total - high, 0.0)).astype(BF16)


def whole(shape):
    return pl.BlockSpec(shape, lambda *_: (0,) * len(shape), pipeline_mode=pl.Buffered(1))


def hidden_grads(chunk, where, half, rows, wg, wu, wd):
    n_rows, width = rows.shape[0], rows.shape[1] // 2
    hidden = wg.shape[2]
    block = 2 * LANES
    lefts = width // half
    once = pl.Buffered(1)
    weight = pl.BlockSpec((1, width, block), lambda i, at: (chunk, 0, i))
    result = pl.BlockSpec((n_rows, block), lambda i, at: (0, i))
    shard = pl.BlockSpec((3, half, block), lambda i, at: (0, 0, i))
    return pl.pallas_call(
        hidden_kernel,
        grid_spec=pltpu.PrefetchScalarGridSpec(
            num_scalar_prefetch=1,
            grid=(hidden // block,),
            in_specs=[
                pl.BlockSpec((n_rows, width), lambda i, at: (0, 0), pipeline_mode=once),
                pl.BlockSpec((n_rows, width), lambda i, at: (0, 1), pipeline_mode=once),
                pl.BlockSpec((n_rows, half), lambda i, at: (0, at[0]), pipeline_mode=once),
                pl.BlockSpec((n_rows, half), lambda i, at: (0, at[1]), pipeline_mode=once),
                pl.BlockSpec((n_rows, half), lambda i, at: (0, at[0] + lefts), pipeline_mode=once),
                pl.BlockSpec((n_rows, half), lambda i, at: (0, at[1] + lefts), pipeline_mode=once),
                weight,
                weight,
                weight,
            ],
            out_specs=[result] * 3 + [whole((n_rows, LANES)), shard, shard],
            scratch_shapes=[pltpu.VMEM((n_rows, LANES), F32)],
        ),
        out_shape=[jax.ShapeDtypeStruct((n_rows, hidden), BF16)] * 3
        + [jax.ShapeDtypeStruct((n_rows, LANES), BF16)]
        + [jax.ShapeDtypeStruct((3, half, hidden), BF16)] * 2,
        compiler_params=pltpu.CompilerParams(vmem_limit_bytes=VMEM_LIMIT),
        cost_estimate=cost(8 * n_rows * width * hidden, 6 * width * hidden + n_rows * (4 * width + 6 * hidden), chunk),
        name=f"hidden{chunk}",
    )(where, *[rows] * 6, wg, wu, wd)


def weight_kernel(n_add, n_after, where_ref, x_ref, do_ref, hid_ref, da_ref, db_ref, *refs):
    adds, outs = refs[:n_add], refs[n_add + n_after :]
    for m, (left, right) in enumerate(((x_ref, da_ref), (x_ref, db_ref), (do_ref, hid_ref))):
        part = dot(left[...], right[...], TN)
        for addend in adds:
            part = part + addend[m].astype(F32)
        for i, out_ref in enumerate(outs):

            @pl.when(pl.program_id(0) == i)
            def _():
                out_ref[m] = part.astype(BF16)


def weight_grads(name, chunk, where, count, half, rows, hid, da, db, *adds, after=()):
    n_rows, width = rows.shape[0], rows.shape[1] // 2
    hidden = hid.shape[1]
    lefts = width // half
    shape = (3, half, hidden)
    return pl.pallas_call(
        functools.partial(weight_kernel, len(adds), len(after)),
        grid_spec=pltpu.PrefetchScalarGridSpec(
            num_scalar_prefetch=1,
            grid=(count,),
            in_specs=[
                pl.BlockSpec((n_rows, half), lambda i, at: (0, at[i])),
                pl.BlockSpec((n_rows, half), lambda i, at: (0, at[i] + lefts)),
            ]
            + [whole(a.shape) for a in (hid, da, db, *adds)]
            + [pl.BlockSpec(memory_space=pl.ANY)] * len(after),
            out_specs=[whole(shape)] * count,
        ),
        out_shape=[jax.ShapeDtypeStruct(shape, BF16)] * count,
        compiler_params=pltpu.CompilerParams(vmem_limit_bytes=VMEM_LIMIT),
        cost_estimate=cost(6 * count * n_rows * half * hidden, 6 * n_rows * hidden + 6 * count * half * hidden, chunk),
        name=name,
    )(where, rows, rows, hid, da, db, *adds, *after)


def mark_kernel(a_ref, b_ref, out_ref):
    out_ref[...] = a_ref[0] + b_ref[0]


def mark(chunk, first, second):
    corner = pl.BlockSpec((1, 16, LANES), lambda i: (0, 0, 0))
    return pl.pallas_call(
        mark_kernel,
        grid=(1,),
        in_specs=[corner, corner],
        out_specs=pl.BlockSpec((16, LANES), lambda i: (0, 0)),
        out_shape=jax.ShapeDtypeStruct((16, LANES), BF16),
        cost_estimate=cost(5 * 3 * first.size, 5 * 3 * first.size, chunk),
        name=f"mark{chunk}",
    )(first, second)


def update_kernel(chunk, where_ref, mask_ref, *refs):
    grads, weights = refs[:4], refs[4:7]
    outs = refs[-3:]
    for second in range(2):

        @pl.when(pl.program_id(0) == second)
        def _():
            for m in range(3):
                grad = sum(g[m].astype(F32) for g in grads[2 * second : 2 * second + 2])
                weight = weights[m][0].astype(F32)
                rate = mask_ref[chunk, m].astype(F32)
                outs[m][0] = (weight - step_size * grad - shrink_rate * rate * weight).astype(BF16)


def update(chunk, where, mask, grads, weights, into):
    _, half, hidden = grads[0].shape
    local = weights[0].shape[0]
    steps = 2
    block = half // steps
    early = pl.BlockSpec((3, block, hidden), lambda h, r, w: (0, r * (1 - h) + (steps - 1) * h, 0))
    late = pl.BlockSpec((3, block, hidden), lambda h, r, w: (0, r * h, 0))
    weight = pl.BlockSpec((1, block, hidden), lambda h, r, w: (chunk, (2 * w[0] + h) * steps + r, 0))
    result = pl.BlockSpec((1, block, hidden), lambda h, r, w: (chunk, h * steps + r, 0))
    extra = list(into or [])
    return pl.pallas_call(
        functools.partial(update_kernel, chunk),
        grid_spec=pltpu.PrefetchScalarGridSpec(
            num_scalar_prefetch=1,
            grid=(2, steps),
            in_specs=[pl.BlockSpec(memory_space=pltpu.SMEM)]
            + [early] * 2
            + [late] * 2
            + [weight] * 3
            + [pl.BlockSpec(memory_space=pl.ANY)] * len(extra),
            out_specs=[result] * 3,
        ),
        out_shape=[jax.ShapeDtypeStruct((local, 2 * half, hidden), BF16)] * 3,
        input_output_aliases={9 + i: i for i in range(len(extra))},
        compiler_params=pltpu.CompilerParams(vmem_limit_bytes=VMEM_LIMIT),
        cost_estimate=cost(10 * half * hidden, 60 * half * hidden),
        name=f"update{chunk}",
    )(where, mask, *grads, *weights, *extra)


def dx_kernel(da_ref, db_ref, s_ref, wg_ref, wu_ref, *refs):
    out_ref = refs[-1]
    n_owner, capacity, block = out_ref.shape
    last = pl.num_programs(0) - 1

    @pl.when(pl.program_id(0) < last)
    def _():
        dx = dot(da_ref[...], wg_ref[0], NT) + dot(db_ref[...], wu_ref[0], NT)
        out_ref[...] = dx.astype(BF16).reshape(n_owner, capacity, block)

    @pl.when(pl.program_id(0) == last)
    def _():
        out_ref[:, :, :LANES] = s_ref[...].reshape(n_owner, capacity, LANES)


def input_grads(chunk, local_exp, capacity, da, db, s, wg, wu, into):
    n_rows, hidden = da.shape
    width = wg.shape[1]
    n_owner = n_rows // capacity
    block = width // 4
    weight = pl.BlockSpec((1, block, hidden), lambda i: (chunk, jnp.minimum(i, 3), 0))
    extra = [] if into is None else [into]
    return pl.pallas_call(
        dx_kernel,
        grid=(5,),
        in_specs=[whole((n_rows, hidden)), whole((n_rows, hidden)), whole((n_rows, LANES)), weight, weight]
        + [pl.BlockSpec(memory_space=pl.ANY)] * len(extra),
        out_specs=pl.BlockSpec((n_owner, capacity, block), lambda i: (0, chunk, i)),
        out_shape=jax.ShapeDtypeStruct((n_owner, local_exp * capacity, width + LANES), BF16),
        input_output_aliases={5: 0} if extra else {},
        compiler_params=pltpu.CompilerParams(vmem_limit_bytes=VMEM_LIMIT),
        cost_estimate=cost(4 * n_rows * width * hidden, 4 * width * hidden + 2 * n_rows * (width + 2 * hidden), chunk),
        name=f"dx{chunk}",
    )(da, db, s, wg, wu, *extra)


def combine_kernel(local_exp, capacity, ids_ref, probs_ref, back_ref, tok_ref, prob_ref):
    ids_t = ids_ref[...]
    topk, tok = ids_t.shape
    n_rows = back_ref.shape[0] * capacity
    n_experts = back_ref.shape[0] * local_exp
    width = tok_ref.shape[1]
    values = slot_values(ids_t, n_experts, capacity)
    total = jnp.zeros((tok, width), F32)
    by_expert = jnp.zeros((n_experts, tok), F32)
    for chunk in range(local_exp):
        onehot, spread = slot_rows(values, chunk, local_exp, capacity)
        pick = jnp.where(onehot, 1.0, 0.0)
        slots = slice(chunk * capacity, (chunk + 1) * capacity)
        dx = back_ref[:, slots, :width].reshape(n_rows, width)
        total = total + dot(pick.astype(BF16), dx, TN)
        s = back_ref[:, slots, width:].reshape(n_rows, LANES).astype(F32)
        placed = pick * (s[:, 0:1] + s[:, 1:2])
        high = placed.astype(BF16)
        low = (placed - high.astype(F32)).astype(BF16)
        by_expert = by_expert + dot(spread, high, TN) + dot(spread, low, TN)
    tok_ref[...] = total.astype(BF16)
    rows = lax.broadcasted_iota(jnp.int32, (n_experts, tok), 0)
    for k in range(topk):
        mine = jnp.where(ids_t[k : k + 1, :] == rows, by_expert, 0.0)
        score = jnp.sum(mine, axis=0, keepdims=True)
        prob_ref[k : k + 1, :] = (score / probs_ref[k : k + 1, :].astype(F32)).astype(BF16)


def combine(local_exp, capacity, ids_t, probs_t, back, width):
    topk, tok = ids_t.shape
    return pl.pallas_call(
        functools.partial(combine_kernel, local_exp, capacity),
        out_shape=[
            jax.ShapeDtypeStruct((tok, width), BF16),
            jax.ShapeDtypeStruct((topk, tok), BF16),
        ],
        compiler_params=pltpu.CompilerParams(vmem_limit_bytes=VMEM_LIMIT),
        cost_estimate=cost(2 * back.shape[0] * back.shape[1] * tok * width, 2 * back.size),
        name="combine",
    )(ids_t, probs_t, back)


def body(tokens, out_grad, expert_ids, route_probs, w_gate, w_up, w_down, decay_mask):
    n_owner = lax.axis_size("expert")
    n_group = lax.axis_size("dp")
    local_exp = w_gate.shape[0]
    width = tokens.shape[1]
    tok_rows, topk = expert_ids.shape
    n_experts = n_owner * local_exp
    capacity = tok_rows * topk // n_experts
    ids_t = expert_ids.T
    probs_t = route_probs.T
    half = width // n_group // 2
    plane = lax.axis_index("dp").astype(jnp.int32)
    where = plane.reshape(1)

    def half_shard(ahead, second):
        return 2 * ((plane + ahead) % n_group) + second

    def blocks(*pairs):
        return jnp.stack([half_shard(*pair) for pair in pairs]).astype(jnp.int32)

    def up(a):
        return lax.ppermute(a, "dp", [(i, (i + 1) % n_group) for i in range(n_group)])

    def down(a):
        return lax.ppermute(a, "dp", [(i, (i - 1) % n_group) for i in range(n_group)])

    def send(chunk):
        return dispatch(chunk, local_exp, capacity, n_experts, ids_t, probs_t, tokens, out_grad)

    def swap(a):
        return lax.all_to_all(a, "expert", split_axis=0, concat_axis=0, tiled=True)

    def swap_rows(a):
        a = a.reshape(n_owner, capacity, a.shape[1])
        return swap(a).reshape(n_owner * capacity, a.shape[2])

    def order(value, *after):
        return lax.optimization_barrier((value, *after))[0]

    def own_sum(chunk, grads, near_up, near_down):
        return [
            weight_grads(f"own{chunk}{second}", chunk, blocks((0, second)), 1, half, *grads, landed)[0]
            for second, landed in enumerate((near_down, near_up))
        ]

    weights = (w_gate, w_up, w_down)
    far_pairs = ((2, 0), (2, 1))
    near_pairs = ((1, 1), (n_group - 1, 0))
    new, dx, before = None, None, None
    sends = [send(chunk) for chunk in range(local_exp)]
    rows = order(swap_rows(sends[0]), *sends[1:])
    for chunk in range(local_exp):
        hid, da, db, s, *far = hidden_grads(chunk, blocks(*far_pairs), half, rows, *weights)
        far_up, far_down = up(far[0]), down(far[1])
        grads, after = (rows, hid, da, db), ()
        if before:
            dx, left = lax.optimization_barrier((dx, mark(chunk, *far)))
            after = [left]
            dx = input_grads(chunk, local_exp, capacity, da, db, s, w_gate, w_up, dx)
            back = swap(dx)
            rows, _, *last = lax.optimization_barrier((rows, dx, *before[-1]))
            grads = (rows, hid, da, db)
        if chunk + 1 < local_exp:
            following, *after = lax.optimization_barrier((sends[chunk + 1], mark(chunk, *far)))
            following = swap_rows(following)
        near = weight_grads(f"near{chunk}", chunk, blocks(*near_pairs), 2, half, *grads, after=after)
        near_up, near_down = up(near[0]), down(near[1])
        far_up, far_down, _ = lax.optimization_barrier((far_up, far_down, near[0]))
        sum_up = weight_grads(f"up{chunk}", chunk, blocks((1, 0)), 1, half, *grads, far_up)[0]
        sum_down = weight_grads(f"down{chunk}", chunk, blocks((n_group - 1, 1)), 1, half, *grads, far_down)[0]
        if before:
            landed = before[1]
            *landed, sum_up, sum_down = lax.optimization_barrier((*landed, sum_up, sum_down))
            own = own_sum(chunk - 1, before[0], *landed)
            new = update(chunk - 1, where, decay_mask, (own[0], last[0], own[1], last[1]), weights, new)
        sent = [up(sum_up), down(sum_down)]
        if chunk + 1 < local_exp:
            dx = input_grads(chunk, local_exp, capacity, order(da, sum_up, sum_down), db, s, w_gate, w_up, dx)
            rows, dx, near_up, near_down = lax.optimization_barrier((following, dx, near_up, near_down))
            before = (grads, (near_up, near_down), sent)
    own = own_sum(local_exp - 1, grads, near_up, near_down)
    back, *own = lax.optimization_barrier((back, *own))
    new = update(
        local_exp - 1, where, decay_mask, (own[0], sent[0], own[1], sent[1]), weights, new
    )
    grad_tokens, grad_probs = combine(local_exp, capacity, ids_t, probs_t, back, width)
    grad_probs = grad_probs.T
    return (grad_tokens, grad_probs, *new)


def solution(mesh):
    placed = (
        P(("dp", "expert"), None),
        P(("dp", "expert"), None),
        P(("dp", "expert"), None),
        P(("dp", "expert"), None),
        P("expert", None, None),
        P("expert", None, None),
        P("expert", None, None),
        P("expert", None),
    )
    return jax.shard_map(
        body,
        mesh=mesh,
        in_specs=placed,
        out_specs=(
            P(("dp", "expert"), None),
            P(("dp", "expert"), None),
            P("expert", "dp", None),
            P("expert", "dp", None),
            P("expert", "dp", None),
        ),
        check_vma=False,
    )
```

```python
import functools

import jax
import jax.numpy as jnp
from jax import lax
from jax.experimental import pallas as pl
from jax.experimental.pallas import tpu as pltpu
from jax.sharding import PartitionSpec as P

step_size = 0.004
shrink_rate = 0.1
LANES = 128
F32 = jnp.float32
BF16 = jnp.bfloat16
VMEM_LIMIT = 63 * 1024 * 1024


def dot(a, b, dims):
    return lax.dot_general(a, b, (dims, ((), ())), preferred_element_type=F32)


def cost(flops, moved, chunk=1):
    scale = (7, 24)[min(chunk, 1)]
    return pl.CostEstimate(flops=scale * flops, transcendentals=0, bytes_accessed=scale * moved)


NN = ((1,), (0,))
NT = ((1,), (1,))
TN = ((0,), (0,))


def slot_values(ids_t, n_experts, capacity):
    topk, tok = ids_t.shape
    rows = lax.broadcasted_iota(jnp.int32, (n_experts, tok), 0)
    hit = ids_t[0:1, :] == rows
    for k in range(1, topk):
        hit = jnp.logical_or(hit, ids_t[k : k + 1, :] == rows)
    hit_f = jnp.where(hit, 1.0, 0.0)
    earlier = lax.broadcasted_iota(jnp.int32, (tok, tok), 0) < lax.broadcasted_iota(
        jnp.int32, (tok, tok), 1
    )
    count = dot(hit_f.astype(BF16), jnp.where(earlier, 1.0, 0.0).astype(BF16), NN)
    return jnp.where(jnp.logical_and(hit, count < capacity), count, -1.0)


def slot_rows(values, chunk, local_exp, capacity):
    n_experts, tok = values.shape
    n_rows = n_experts // local_exp * capacity
    expert_of = lax.broadcasted_iota(jnp.int32, (n_rows, n_experts), 0) // capacity * local_exp + chunk
    spread = jnp.where(expert_of == lax.broadcasted_iota(jnp.int32, (n_rows, n_experts), 1), 1.0, 0.0)
    spread = spread.astype(BF16)
    at = dot(spread, values.astype(BF16), NN)
    place = (lax.broadcasted_iota(jnp.int32, (n_rows, tok), 0) % capacity).astype(F32)
    return at == place, spread


def dispatch_kernel(chunk, local_exp, capacity, ids_ref, probs_ref, tok_ref, grad_ref, out_ref):
    ids_t = ids_ref[...]
    topk, tok = ids_t.shape
    n_experts = out_ref.shape[0] // capacity * local_exp
    width = tok_ref.shape[1]
    values = slot_values(ids_t, n_experts, capacity)
    rows = lax.broadcasted_iota(jnp.int32, (n_experts, tok), 0)
    prob = jnp.zeros((n_experts, tok), F32)
    for k in range(topk):
        prob = prob + jnp.where(ids_t[k : k + 1, :] == rows, probs_ref[k : k + 1, :].astype(F32), 0.0)
    onehot, spread = slot_rows(values, chunk, local_exp, capacity)
    prob_rows = dot(spread, prob.astype(BF16), NN)
    pick = jnp.where(onehot, 1.0, 0.0).astype(BF16)
    weighted = jnp.where(onehot, prob_rows, 0.0).astype(BF16)
    out_ref[:, :width] = dot(pick, tok_ref[...], NN).astype(BF16)
    out_ref[:, width:] = dot(weighted, grad_ref[...], NN).astype(BF16)


def dispatch(chunk, local_exp, capacity, n_experts, ids_t, probs_t, tokens, out_grad):
    tok, width = tokens.shape
    n_rows = n_experts // local_exp * capacity
    return pl.pallas_call(
        functools.partial(dispatch_kernel, chunk, local_exp, capacity),
        out_shape=jax.ShapeDtypeStruct((n_rows, 2 * width), BF16),
        compiler_params=pltpu.CompilerParams(vmem_limit_bytes=VMEM_LIMIT),
        cost_estimate=cost(4 * n_rows * tok * width, 4 * width * (tok + n_rows), 0),
        name=f"dispatch{chunk}",
    )(ids_t, probs_t, tokens, out_grad)


def hidden_kernel(
    where_ref, x_ref, do_ref, xa_ref, xb_ref, da_col_ref, db_col_ref, wg_ref, wu_ref, wd_ref,
    hid_ref, da_ref, db_ref, s_ref, a_ref, b_ref, sum_ref,
):
    step = pl.program_id(0)
    gate = dot(x_ref[...], wg_ref[0], NN)
    upper = dot(x_ref[...], wu_ref[0], NN)
    sig = jax.nn.sigmoid(gate)
    act = gate * sig
    hid = (act * upper).astype(BF16)
    hid_ref[...] = hid
    dhid = dot(do_ref[...], wd_ref[0], NN)
    part = jnp.sum(hid.astype(F32) * dhid, axis=1, keepdims=True)
    dgate = (dhid * upper * sig * (1.0 + gate * (1.0 - sig))).astype(BF16)
    dup = (dhid * act).astype(BF16)
    da_ref[...] = dgate
    db_ref[...] = dup
    for out_ref, x_col, do_col in ((a_ref, xa_ref, da_col_ref), (b_ref, xb_ref, db_col_ref)):
        out_ref[0] = dot(x_col[...], dgate, TN).astype(BF16)
        out_ref[1] = dot(x_col[...], dup, TN).astype(BF16)
        out_ref[2] = dot(do_col[...], hid, TN).astype(BF16)

    @pl.when(step == 0)
    def _():
        sum_ref[...] = jnp.broadcast_to(part, sum_ref.shape)

    @pl.when(step > 0)
    def _():
        sum_ref[...] = sum_ref[...] + part

    @pl.when(step == pl.num_programs(0) - 1)
    def _():
        total = sum_ref[...]
        high = total.astype(BF16).astype(F32)
        lane = lax.broadcasted_iota(jnp.int32, s_ref.shape, 1)
        s_ref[...] = jnp.where(lane == 0, high, jnp.where(lane == 1, total - high, 0.0)).astype(BF16)


def whole(shape):
    return pl.BlockSpec(shape, lambda *_: (0,) * len(shape), pipeline_mode=pl.Buffered(1))


def hidden_grads(chunk, where, half, rows, wg, wu, wd):
    n_rows, width = rows.shape[0], rows.shape[1] // 2
    hidden = wg.shape[2]
    block = 2 * LANES
    lefts = width // half
    once = pl.Buffered(1)
    weight = pl.BlockSpec((1, width, block), lambda i, at: (chunk, 0, i))
    result = pl.BlockSpec((n_rows, block), lambda i, at: (0, i))
    shard = pl.BlockSpec((3, half, block), lambda i, at: (0, 0, i))
    return pl.pallas_call(
        hidden_kernel,
        grid_spec=pltpu.PrefetchScalarGridSpec(
            num_scalar_prefetch=1,
            grid=(hidden // block,),
            in_specs=[
                pl.BlockSpec((n_rows, width), lambda i, at: (0, 0), pipeline_mode=once),
                pl.BlockSpec((n_rows, width), lambda i, at: (0, 1), pipeline_mode=once),
                pl.BlockSpec((n_rows, half), lambda i, at: (0, at[0]), pipeline_mode=once),
                pl.BlockSpec((n_rows, half), lambda i, at: (0, at[1]), pipeline_mode=once),
                pl.BlockSpec((n_rows, half), lambda i, at: (0, at[0] + lefts), pipeline_mode=once),
                pl.BlockSpec((n_rows, half), lambda i, at: (0, at[1] + lefts), pipeline_mode=once),
                weight,
                weight,
                weight,
            ],
            out_specs=[result] * 3 + [whole((n_rows, LANES)), shard, shard],
            scratch_shapes=[pltpu.VMEM((n_rows, LANES), F32)],
        ),
        out_shape=[jax.ShapeDtypeStruct((n_rows, hidden), BF16)] * 3
        + [jax.ShapeDtypeStruct((n_rows, LANES), BF16)]
        + [jax.ShapeDtypeStruct((3, half, hidden), BF16)] * 2,
        compiler_params=pltpu.CompilerParams(vmem_limit_bytes=VMEM_LIMIT),
        cost_estimate=cost(8 * n_rows * width * hidden, 6 * width * hidden + n_rows * (4 * width + 6 * hidden), chunk),
        name=f"hidden{chunk}",
    )(where, *[rows] * 6, wg, wu, wd)


def weight_kernel(n_add, n_after, where_ref, x_ref, do_ref, hid_ref, da_ref, db_ref, *refs):
    adds, outs = refs[:n_add], refs[n_add + n_after :]
    for m, (left, right) in enumerate(((x_ref, da_ref), (x_ref, db_ref), (do_ref, hid_ref))):
        part = dot(left[...], right[...], TN)
        for addend in adds:
            part = part + addend[m].astype(F32)
        for i, out_ref in enumerate(outs):

            @pl.when(pl.program_id(0) == i)
            def _():
                out_ref[m] = part.astype(BF16)


def weight_grads(name, chunk, where, count, half, rows, hid, da, db, *adds, after=()):
    n_rows, width = rows.shape[0], rows.shape[1] // 2
    hidden = hid.shape[1]
    lefts = width // half
    shape = (3, half, hidden)
    return pl.pallas_call(
        functools.partial(weight_kernel, len(adds), len(after)),
        grid_spec=pltpu.PrefetchScalarGridSpec(
            num_scalar_prefetch=1,
            grid=(count,),
            in_specs=[
                pl.BlockSpec((n_rows, half), lambda i, at: (0, at[i])),
                pl.BlockSpec((n_rows, half), lambda i, at: (0, at[i] + lefts)),
            ]
            + [whole(a.shape) for a in (hid, da, db, *adds)]
            + [pl.BlockSpec(memory_space=pl.ANY)] * len(after),
            out_specs=[whole(shape)] * count,
        ),
        out_shape=[jax.ShapeDtypeStruct(shape, BF16)] * count,
        compiler_params=pltpu.CompilerParams(vmem_limit_bytes=VMEM_LIMIT),
        cost_estimate=cost(6 * count * n_rows * half * hidden, 6 * n_rows * hidden + 6 * count * half * hidden, chunk),
        name=name,
    )(where, rows, rows, hid, da, db, *adds, *after)


def mark_kernel(a_ref, b_ref, out_ref):
    out_ref[...] = a_ref[0] + b_ref[0]


def mark(chunk, first, second):
    corner = pl.BlockSpec((1, 16, LANES), lambda i: (0, 0, 0))
    return pl.pallas_call(
        mark_kernel,
        grid=(1,),
        in_specs=[corner, corner],
        out_specs=pl.BlockSpec((16, LANES), lambda i: (0, 0)),
        out_shape=jax.ShapeDtypeStruct((16, LANES), BF16),
        cost_estimate=cost(5 * 3 * first.size, 5 * 3 * first.size, chunk),
        name=f"mark{chunk}",
    )(first, second)


def update_kernel(chunk, where_ref, mask_ref, *refs):
    grads, weights = refs[:4], refs[4:7]
    outs = refs[-3:]
    for second in range(2):

        @pl.when(pl.program_id(0) == second)
        def _():
            for m in range(3):
                grad = sum(g[m].astype(F32) for g in grads[2 * second : 2 * second + 2])
                weight = weights[m][0].astype(F32)
                rate = mask_ref[chunk, m].astype(F32)
                outs[m][0] = (weight * (1.0 - shrink_rate * rate) - step_size * grad).astype(BF16)


def update(chunk, where, mask, grads, weights, into):
    _, half, hidden = grads[0].shape
    local = weights[0].shape[0]
    steps = 1
    block = half // steps
    early = pl.BlockSpec((3, block, hidden), lambda h, r, w: (0, r * (1 - h) + (steps - 1) * h, 0))
    late = pl.BlockSpec((3, block, hidden), lambda h, r, w: (0, r * h, 0))
    weight = pl.BlockSpec((1, block, hidden), lambda h, r, w: (chunk, (2 * w[0] + h) * steps + r, 0))
    result = pl.BlockSpec((1, block, hidden), lambda h, r, w: (chunk, h * steps + r, 0))
    extra = list(into or [])
    return pl.pallas_call(
        functools.partial(update_kernel, chunk),
        grid_spec=pltpu.PrefetchScalarGridSpec(
            num_scalar_prefetch=1,
            grid=(2, steps),
            in_specs=[pl.BlockSpec(memory_space=pltpu.SMEM)]
            + [early] * 2
            + [late] * 2
            + [weight] * 3
            + [pl.BlockSpec(memory_space=pl.ANY)] * len(extra),
            out_specs=[result] * 3,
        ),
        out_shape=[jax.ShapeDtypeStruct((local, 2 * half, hidden), BF16)] * 3,
        input_output_aliases={9 + i: i for i in range(len(extra))},
        compiler_params=pltpu.CompilerParams(vmem_limit_bytes=VMEM_LIMIT),
        cost_estimate=cost(10 * half * hidden, 60 * half * hidden),
        name=f"update{chunk}",
    )(where, mask, *grads, *weights, *extra)


def dx_kernel(da_ref, db_ref, s_ref, wg_ref, wu_ref, *refs):
    out_ref = refs[-1]
    n_owner, capacity, block = out_ref.shape
    last = pl.num_programs(0) - 1

    @pl.when(pl.program_id(0) < last)
    def _():
        dx = dot(da_ref[...], wg_ref[0], NT) + dot(db_ref[...], wu_ref[0], NT)
        out_ref[...] = dx.astype(BF16).reshape(n_owner, capacity, block)

    @pl.when(pl.program_id(0) == last)
    def _():
        out_ref[:, :, :LANES] = s_ref[...].reshape(n_owner, capacity, LANES)


def input_grads(chunk, local_exp, capacity, da, db, s, wg, wu, into):
    n_rows, hidden = da.shape
    width = wg.shape[1]
    n_owner = n_rows // capacity
    block = width // 4
    weight = pl.BlockSpec((1, block, hidden), lambda i: (chunk, jnp.minimum(i, 3), 0))
    extra = [] if into is None else [into]
    return pl.pallas_call(
        dx_kernel,
        grid=(5,),
        in_specs=[whole((n_rows, hidden)), whole((n_rows, hidden)), whole((n_rows, LANES)), weight, weight]
        + [pl.BlockSpec(memory_space=pl.ANY)] * len(extra),
        out_specs=pl.BlockSpec((n_owner, capacity, block), lambda i: (0, chunk, i)),
        out_shape=jax.ShapeDtypeStruct((n_owner, local_exp * capacity, width + LANES), BF16),
        input_output_aliases={5: 0} if extra else {},
        compiler_params=pltpu.CompilerParams(vmem_limit_bytes=VMEM_LIMIT),
        cost_estimate=cost(4 * n_rows * width * hidden, 4 * width * hidden + 2 * n_rows * (width + 2 * hidden), chunk),
        name=f"dx{chunk}",
    )(da, db, s, wg, wu, *extra)


def combine_kernel(local_exp, capacity, ids_ref, probs_ref, back_ref, tok_ref, prob_ref):
    ids_t = ids_ref[...]
    topk, tok = ids_t.shape
    n_rows = back_ref.shape[0] * capacity
    n_experts = back_ref.shape[0] * local_exp
    width = tok_ref.shape[1]
    values = slot_values(ids_t, n_experts, capacity)
    total = jnp.zeros((tok, width), F32)
    by_expert = jnp.zeros((n_experts, tok), F32)
    for chunk in range(local_exp):
        onehot, spread = slot_rows(values, chunk, local_exp, capacity)
        pick = jnp.where(onehot, 1.0, 0.0)
        slots = slice(chunk * capacity, (chunk + 1) * capacity)
        dx = back_ref[:, slots, :width].reshape(n_rows, width)
        total = total + dot(pick.astype(BF16), dx, TN)
        s = back_ref[:, slots, width:].reshape(n_rows, LANES).astype(F32)
        placed = pick * (s[:, 0:1] + s[:, 1:2])
        high = placed.astype(BF16)
        low = (placed - high.astype(F32)).astype(BF16)
        by_expert = by_expert + dot(spread, high, TN) + dot(spread, low, TN)
    tok_ref[...] = total.astype(BF16)
    rows = lax.broadcasted_iota(jnp.int32, (n_experts, tok), 0)
    for k in range(topk):
        mine = jnp.where(ids_t[k : k + 1, :] == rows, by_expert, 0.0)
        score = jnp.sum(mine, axis=0, keepdims=True)
        prob_ref[k : k + 1, :] = (score / probs_ref[k : k + 1, :].astype(F32)).astype(BF16)


def combine(local_exp, capacity, ids_t, probs_t, back, width):
    topk, tok = ids_t.shape
    return pl.pallas_call(
        functools.partial(combine_kernel, local_exp, capacity),
        out_shape=[
            jax.ShapeDtypeStruct((tok, width), BF16),
            jax.ShapeDtypeStruct((topk, tok), BF16),
        ],
        compiler_params=pltpu.CompilerParams(vmem_limit_bytes=VMEM_LIMIT),
        cost_estimate=cost(2 * back.shape[0] * back.shape[1] * tok * width, 2 * back.size),
        name="combine",
    )(ids_t, probs_t, back)


def body(tokens, out_grad, expert_ids, route_probs, w_gate, w_up, w_down, decay_mask):
    n_owner = lax.axis_size("expert")
    n_group = lax.axis_size("dp")
    local_exp = w_gate.shape[0]
    width = tokens.shape[1]
    tok_rows, topk = expert_ids.shape
    n_experts = n_owner * local_exp
    capacity = tok_rows * topk // n_experts
    ids_t = expert_ids.T
    probs_t = route_probs.T
    half = width // n_group // 2
    plane = lax.axis_index("dp").astype(jnp.int32)
    where = plane.reshape(1)

    def half_shard(ahead, second):
        return 2 * ((plane + ahead) % n_group) + second

    def blocks(*pairs):
        return jnp.stack([half_shard(*pair) for pair in pairs]).astype(jnp.int32)

    def up(a):
        return lax.ppermute(a, "dp", [(i, (i + 1) % n_group) for i in range(n_group)])

    def down(a):
        return lax.ppermute(a, "dp", [(i, (i - 1) % n_group) for i in range(n_group)])

    def send(chunk):
        return dispatch(chunk, local_exp, capacity, n_experts, ids_t, probs_t, tokens, out_grad)

    def swap(a):
        return lax.all_to_all(a, "expert", split_axis=0, concat_axis=0, tiled=True)

    def swap_rows(a):
        a = a.reshape(n_owner, capacity, a.shape[1])
        return swap(a).reshape(n_owner * capacity, a.shape[2])

    def order(value, *after):
        return lax.optimization_barrier((value, *after))[0]

    def own_sum(chunk, grads, near_up, near_down):
        return [
            weight_grads(f"own{chunk}{second}", chunk, blocks((0, second)), 1, half, *grads, landed)[0]
            for second, landed in enumerate((near_down, near_up))
        ]

    weights = (w_gate, w_up, w_down)
    far_pairs = ((2, 0), (2, 1))
    near_pairs = ((1, 1), (n_group - 1, 0))
    new, dx, before = None, None, None
    sends = [send(chunk) for chunk in range(local_exp)]
    rows = order(swap_rows(sends[0]), *sends[1:])
    for chunk in range(local_exp):
        hid, da, db, s, *far = hidden_grads(chunk, blocks(*far_pairs), half, rows, *weights)
        far_up, far_down = up(far[0]), down(far[1])
        grads, after = (rows, hid, da, db), ()
        if before:
            dx, left = lax.optimization_barrier((dx, mark(chunk, *far)))
            after = [left]
            dx = input_grads(chunk, local_exp, capacity, da, db, s, w_gate, w_up, dx)
            back = swap(dx)
            rows, _, *last = lax.optimization_barrier((rows, dx, *before[-1]))
            grads = (rows, hid, da, db)
        if chunk + 1 < local_exp:
            following, *after = lax.optimization_barrier((sends[chunk + 1], mark(chunk, *far)))
            following = swap_rows(following)
        near = weight_grads(f"near{chunk}", chunk, blocks(*near_pairs), 2, half, *grads, after=after)
        near_up, near_down = up(near[0]), down(near[1])
        far_up, far_down, _ = lax.optimization_barrier((far_up, far_down, near[0]))
        sum_up = weight_grads(f"up{chunk}", chunk, blocks((1, 0)), 1, half, *grads, far_up)[0]
        sum_down = weight_grads(f"down{chunk}", chunk, blocks((n_group - 1, 1)), 1, half, *grads, far_down)[0]
        if before:
            landed = before[1]
            *landed, sum_up, sum_down = lax.optimization_barrier((*landed, sum_up, sum_down))
            own = own_sum(chunk - 1, before[0], *landed)
            new = update(chunk - 1, where, decay_mask, (own[0], last[0], own[1], last[1]), weights, new)
        sent = [up(sum_up), down(sum_down)]
        if chunk + 1 < local_exp:
            dx = input_grads(chunk, local_exp, capacity, order(da, sum_up, sum_down), db, s, w_gate, w_up, dx)
            rows, dx, near_up, near_down = lax.optimization_barrier((following, dx, near_up, near_down))
            before = (grads, (near_up, near_down), sent)
    own = own_sum(local_exp - 1, grads, near_up, near_down)
    back, *own = lax.optimization_barrier((back, *own))
    new = update(
        local_exp - 1, where, decay_mask, (own[0], sent[0], own[1], sent[1]), weights, new
    )
    grad_tokens, grad_probs = combine(local_exp, capacity, ids_t, probs_t, back, width)
    grad_probs = grad_probs.T
    return (grad_tokens, grad_probs, *new)


def solution(mesh):
    placed = (
        P(("dp", "expert"), None),
        P(("dp", "expert"), None),
        P(("dp", "expert"), None),
        P(("dp", "expert"), None),
        P("expert", None, None),
        P("expert", None, None),
        P("expert", None, None),
        P("expert", None),
    )
    return jax.shard_map(
        body,
        mesh=mesh,
        in_specs=placed,
        out_specs=(
            P(("dp", "expert"), None),
            P(("dp", "expert"), None),
            P("expert", "dp", None),
            P("expert", "dp", None),
            P("expert", "dp", None),
        ),
        check_vma=False,
    )
```
